32 devices in a mesh: grp: 8 (over z, y), fsdp: 4 (over x, core).
Axes of the slice: x: 2, y: 2, z: 4, core: 2. Of those that a mesh axis runs over, the one named last changes fastest.
Arguments:
- layer_input: bfloat16 [2, 32768, 768], P(None, ('grp', 'fsdp')), may hold values from -6 to 6
- segment_ids: int32 [2, 32768], P(None, ('grp', 'fsdp')), may hold values from 0 to 255, never falling along the last dimension, each value on 1 to 1024 neighbouring positions
- bucket_table: int32 [2048], replicated, may hold values from 0 to 31, as said below
- gain_attn: bfloat16 [768], P('fsdp'), may hold values from 0.5 to 1.5
- weight_query: bfloat16 [768, 768], P('fsdp'), may hold values from -0.02734375 to 0.02734375
- weight_key: bfloat16 [768, 768], P('fsdp'), may hold values from -0.21875 to 0.21875
- weight_value: bfloat16 [768, 768], P('fsdp'), may hold values from -0.21875 to 0.21875
- weight_out: bfloat16 [768, 768], P('fsdp'), may hold values from -0.875 to 0.875
- gain_ffn: bfloat16 [768], P('fsdp'), may hold values from 0.5 to 1.5
- weight_in: bfloat16 [768, 3072], P('fsdp'), may hold values from -0.21875 to 0.21875
- weight_back: bfloat16 [3072, 768], P('fsdp'), may hold values from -0.109375 to 0.109375
- gain_final: bfloat16 [768], P('fsdp'), may hold values from 0.5 to 1.5
- weight_embed: bfloat16 [768, 128], P('fsdp'), may hold values from -0.21875 to 0.21875
- bias_table: bfloat16 [32, 12], P('fsdp'), may hold values from -4 to 4
- cotangent: bfloat16 [2, 32768, 128], P(None, ('grp', 'fsdp')), may hold values from -6 to 6
Outputs:
- states: float32 [2, 32768, 128], P(None, ('grp', 'fsdp'))
- grad_input: float32 [2, 32768, 768], P(None, ('grp', 'fsdp'))
- grad_gain_attn: float32 [768], P('fsdp')
- grad_query: float32 [768, 768], P('fsdp')
- grad_key: float32 [768, 768], P('fsdp')
- grad_value: float32 [768, 768], P('fsdp')
- grad_out: float32 [768, 768], P('fsdp')
- grad_gain_ffn: float32 [768], P('fsdp')
- grad_in: float32 [768, 3072], P('fsdp')
- grad_back: float32 [3072, 768], P('fsdp')
- grad_gain_final: float32 [768], P('fsdp')
- grad_embed: float32 [768, 128], P('fsdp')
- grad_table: float32 [32, 12], P('fsdp')
The draws below stay inside these ranges and needn't reach their ends.
Inputs may be any that keep to these rules, and one draw needn't show every extreme that they name: `bucket_table`: entry 1024 + r is the bucket of a key r positions after its query (before it where r < 0); it is 0 for r = 0, below 16 for r <= 0, at least 16 for r > 0, and never falls as |r| grows on either side. `segment_ids`: along each micro-batch's row the ids never fall; a document spans 1 to 1024 positions and one spans exactly 1024.
All inputs are finite; a program needn't handle non-finite values.
Results may differ from the reference program's by a relative error of at most 0.018.
Values may be sent and summed in bfloat16 or wider, within the bound.
No kernel may reach another device: no remote copies, remote signals or barrier semaphores. Data moves between devices by JAX's collectives and lax.ppermute only.
A program may use at most 384 MiB of HBM per device.

```python
import math
import jax
import jax.numpy as jnp
import numpy as np
from jax import lax

D = 768
H = 12
DH = 64
FF = 3072
E = 128
NB = 32
SEQ = 1024
MICRO = 2
ROWS = 32768
N_GRP = 8
N_FSDP = 4


def draw_bucket_table(key, part):
    half = NB // 2
    picks = jax.random.permutation(key, SEQ - 1)[:half - 1].astype(jnp.int32) + 1
    offsets = jnp.arange(2 * SEQ, dtype=jnp.int32) - SEQ
    distance = jnp.abs(offsets)
    level = jnp.sum((picks[None, :] <= distance[:, None]).astype(jnp.int32), axis=1)
    return (level + half * (offsets > 0).astype(jnp.int32)).astype(jnp.int32)


def steps_of(key, shape, split, smallest, largest):
    def one(position, blocks):
        draws = jax.random.uniform(jax.random.fold_in(jax.random.fold_in(key, 6), position), (blocks,), jnp.float32, smallest / len(split), largest / len(split))
        return jnp.repeat(jnp.exp(draws), shape[position] // blocks).reshape((-1,) + (1,) * (len(shape) - position - 1))

    level = one(*split[0])
    for cut in split[1:]:
        level = level * one(*cut)
    return level


def profile(amount, total, limit, lean):
    loads = [(1 << 20) // math.isqrt(rank ** lean) + 1 for rank in range(2, amount + 1)]
    spare, counts = total - limit - (amount - 1), [1] * (amount - 1)
    while spare > 0:
        movable = [i for i in range(amount - 1) if counts[i] < limit]
        whole, left = sum([loads[i] for i in movable]), spare
        for i in movable:
            more = min(limit - counts[i], max(1, left * loads[i] // whole), spare)
            counts[i] = counts[i] + more
            spare = spare - more
    return np.array([limit] + counts)


def ragged(stream_key, count, total, reach, slope):
    if count == 2:
        one = jax.random.randint(stream_key, (), max(1, total - reach), min(reach, total - 1) + 1)
        return jnp.stack([one, total - one])
    sizes = jnp.asarray(profile(count, total, reach, slope), jnp.int32)
    couples = (count - 1) // 2
    donor, sink = sizes[1:1 + 2 * couples:2], sizes[2:2 + 2 * couples:2]
    room = jnp.minimum(donor - 1, reach - sink)
    moved = jax.random.randint(jax.random.fold_in(stream_key, 1), (couples,), 0, 1 << 20) % (room + 1)
    sizes = sizes.at[1:1 + 2 * couples:2].set(donor - moved).at[2:2 + 2 * couples:2].set(sink + moved)
    return sizes[jax.random.permutation(jax.random.fold_in(stream_key, 2), count)]


def noise(stream_key, dims, width, bound, pieces=(), kind=jnp.bfloat16):
    level = steps_of(stream_key, dims, pieces, -0.22, 0.18) if pieces else 1.0
    result = jax.random.normal(stream_key, dims, jnp.float32) * width * level
    return jnp.minimum(jnp.maximum(result, -bound), bound).astype(kind)


def setup_inputs(seed: int = 0) -> dict:
    key_of = jax.random.split(jax.random.key(seed), 16)
    layer_input = noise(key_of[0], (MICRO, ROWS, D), 1.0, 6.0, ((1, 32),))
    segment_ids = jax.vmap(lambda own: jnp.searchsorted(jnp.cumsum(ragged(own, ROWS // min(128, SEQ // 2), ROWS, SEQ, 2)), jnp.arange(ROWS), side="right"))(jax.random.split(key_of[1], MICRO)).reshape((MICRO, ROWS)).astype(jnp.int32)
    bucket_table = draw_bucket_table(jax.random.fold_in(key_of[15], 71), 0)
    gain_attn = jnp.clip(1.0 + 0.1 * jax.random.normal(key_of[3], (D,), jnp.float32), 0.5, 1.5).astype(jnp.bfloat16)
    weight_query = noise(key_of[4], (D, D), (D * DH) ** -0.5, 0.02734375, ((0, 4),))
    weight_key = noise(key_of[5], (D, D), D ** -0.5, 0.21875, ((0, 4),))
    weight_value = noise(key_of[6], (D, D), D ** -0.5, 0.21875, ((0, 4),))
    weight_out = noise(key_of[7], (D, D), (D // 16) ** -0.5, 0.875, ((0, 4),))
    gain_ffn = jnp.clip(1.0 + 0.1 * jax.random.normal(key_of[8], (D,), jnp.float32), 0.5, 1.5).astype(jnp.bfloat16)
    weight_in = noise(key_of[9], (D, FF), D ** -0.5, 0.21875, ((0, 4),))
    weight_back = noise(key_of[10], (FF, D), FF ** -0.5, 0.109375, ((0, 4),))
    gain_final = jnp.clip(1.0 + 0.1 * jax.random.normal(key_of[11], (D,), jnp.float32), 0.5, 1.5).astype(jnp.bfloat16)
    weight_embed = noise(key_of[12], (D, E), D ** -0.5, 0.21875, ((0, 4),))
    bias_table = noise(key_of[13], (NB, H), 1.0, 4.0, ((0, 4),))
    cotangent = noise(key_of[14], (MICRO, ROWS, E), 1.0, 6.0, ((1, 32),))
    return dict(layer_input=layer_input, segment_ids=segment_ids, bucket_table=bucket_table, gain_attn=gain_attn, weight_query=weight_query, weight_key=weight_key, weight_value=weight_value, weight_out=weight_out, gain_ffn=gain_ffn, weight_in=weight_in, weight_back=weight_back, gain_final=gain_final, weight_embed=weight_embed, bias_table=bias_table, cotangent=cotangent)


EPS = 1e-06
HIGH = lax.Precision.HIGHEST

@jax.custom_vjp
def low(v):
    return lax.optimization_barrier(v.astype(jnp.bfloat16)).astype(jnp.float32)

@jax.custom_vjp
def low_back(v):
    return v

def low_keep(v):
    return (low(v), None)

def low_pass(kept, grad):
    return (grad,)

def back_keep(v):
    return (v, None)

def back_low(kept, grad):
    return (low(grad),)
low.defvjp(low_keep, low_pass)
low_back.defvjp(back_keep, back_low)

def matmul(left, right):
    return jnp.dot(left, right, precision=HIGH)

def rms_norm(value, gain):
    return value * lax.rsqrt(lax.optimization_barrier(jnp.mean(value * value, axis=-1, keepdims=True)) + EPS) * gain

def sequence(xseq, seg, weights, onehot):
    gain_attn, wq, wk, wv, wo, gain_ffn, wi, wb, gain_final, we, table = weights
    h1 = low(rms_norm(xseq, gain_attn))
    query = low(low_back(matmul(h1, wq))).reshape(SEQ, H, DH)
    key = low(low_back(matmul(h1, wk))).reshape(SEQ, H, DH)
    value = low(low_back(matmul(h1, wv))).reshape(SEQ, H, DH)
    bias_rows = matmul(onehot, table).T
    block = min(512, SEQ)

    def one_block(start):
        rows = start + jnp.arange(block, dtype=jnp.int32)
        offsets = jnp.arange(SEQ, dtype=jnp.int32)[None, :] - rows[:, None] + SEQ
        bias = jnp.take(bias_rows, offsets, axis=1)
        qblock = lax.dynamic_slice_in_dim(query, start, block, 0)
        scores = low_back(jnp.einsum('qhd,khd->hqk', qblock, key, precision=HIGH) + bias)
        seg_rows = lax.dynamic_slice_in_dim(seg, start, block, 0)
        same = seg_rows[:, None] == seg[None, :]
        scores = jnp.where(same[None], scores, -1e+30)
        probs = low(jax.nn.softmax(scores, axis=-1))
        return jnp.einsum('hqk,khd->qhd', probs, value, precision=HIGH)
    starts = jnp.arange(SEQ // block, dtype=jnp.int32) * block
    attn = lax.map(jax.checkpoint(one_block), starts).reshape(SEQ, D)
    attn = low(low_back(attn))
    x2 = xseq + low_back(matmul(attn, wo))
    h2 = low(rms_norm(x2, gain_ffn))
    pre = low_back(matmul(h2, wi))
    hidden = low(jax.nn.gelu(pre, approximate=False))
    x3 = x2 + low_back(matmul(hidden, wb))
    h3 = low(rms_norm(x3, gain_final))
    return matmul(h3, we)

def reference(layer_input, segment_ids, bucket_table, gain_attn, weight_query, weight_key, weight_value, weight_out, gain_ffn, weight_in, weight_back, gain_final, weight_embed, bias_table, cotangent):
    weights = tuple((w.astype(jnp.float32) for w in (gain_attn, weight_query, weight_key, weight_value, weight_out, gain_ffn, weight_in, weight_back, gain_final, weight_embed, bias_table)))
    onehot = (bucket_table[:, None] == jnp.arange(NB, dtype=jnp.int32)[None, :]).astype(jnp.float32)
    count = MICRO * N_GRP * N_FSDP
    segs = segment_ids.reshape(count, SEQ)

    def forward(xs, params):
        step_fn = jax.checkpoint(sequence)

        def one(carry, item):
            return (carry, step_fn(item[0], item[1], params, onehot))
        unused, outs = lax.scan(one, jnp.float32(0.0), (xs.reshape(count, SEQ, D), segs))
        return outs.reshape(MICRO, ROWS, E)
    states, pull = jax.vjp(forward, layer_input.astype(jnp.float32), weights)
    grad_input, grads = pull(cotangent.astype(jnp.float32))
    return (states, grad_input, grads[0], grads[1], grads[2], grads[3], grads[4], grads[5], grads[6], grads[7], grads[8], grads[9], grads[10])
```

```python
import functools
import jax, jax.numpy as jnp
from jax import lax
from jax.experimental import pallas as pl
from jax.experimental.pallas import tpu as pltpu
from jax.sharding import PartitionSpec as P

BQ = 256
STEP = 128
NEGATIVE = -1e30
VMEM_CAP = 60 * 1024 * 1024

NT = (((1,), (1,)), ((), ()))
NN = (((1,), (0,)), ((), ()))


def mm(a, b, dims=NN):
    return lax.dot_general(a, b, dims, preferred_element_type=jnp.float32)


def strip_kernel(rows_ref, strip_ref, *, length):
    rows = jnp.broadcast_to(rows_ref[0], (STEP, 2 * length))
    turned = pltpu.roll(rows, 2 * length - STEP, 1, stride=1, stride_axis=0)
    strip_ref[0] = turned[:, : 2 * length - STEP].T


def bias_strips(rows):
    heads, twice = rows.shape
    return pl.pallas_call(
        functools.partial(strip_kernel, length=twice // 2),
        grid=(heads,),
        in_specs=[pl.BlockSpec((1, 1, twice), lambda h: (h, 0, 0))],
        out_specs=pl.BlockSpec((1, twice - STEP, STEP), lambda h: (h, 0, 0)),
        out_shape=jax.ShapeDtypeStruct((heads, twice - STEP, STEP), jnp.float32),
        name="bias_strips",
        compiler_params=pltpu.CompilerParams(vmem_limit_bytes=VMEM_CAP),
    )(rows.reshape(heads, 1, twice))


def by_width(low_ref, width_ref, length, work):
    step = pl.program_id(0) * pl.num_programs(1) + pl.program_id(1)
    low = pl.multiple_of(low_ref[step], STEP)
    width = width_ref[step]
    for blocks in range(BQ // STEP, length // STEP + 1):

        @pl.when(width == blocks)
        def _(blocks=blocks):
            work(low, blocks * STEP)


def fwd_kernel(low_ref, width_ref, q_ref, k_ref, vt_ref, strip_ref, sk_ref, sq_ref,
               attn_ref, attnt_ref, prob_ref, inv_ref, mask_ref, *, heads, feat, length):
    start = pl.program_id(1) * BQ

    def work(low, width):
        keys = pl.ds(low, width)
        mask_ref[:width] = jnp.where(sk_ref[keys, :] == sq_ref[0], 0.0, NEGATIVE)
        row_a = pl.multiple_of(low - start + length - STEP, STEP)
        row_b = pl.multiple_of(low - start + length - 2 * STEP, STEP)

        def pair(index, carry):
            lanes = pl.ds(pl.multiple_of(index * 2 * feat, 2 * feat), 2 * feat)
            query = q_ref[:, lanes]
            key = k_ref[keys, lanes]
            left = lax.broadcasted_iota(jnp.int32, query.shape, 1) < feat
            outs = []
            for side in range(2):
                head = index * 2 + side
                own = jnp.where(left if side == 0 else ~left, query, jnp.zeros_like(query))
                bias = jnp.concatenate(
                    [strip_ref[head, pl.ds(row_a, width), :], strip_ref[head, pl.ds(row_b, width), :]],
                    axis=1,
                )
                scores = mm(key, own, NT) + bias + mask_ref[:width]
                top = jnp.max(scores, axis=0, keepdims=True)
                expo = jnp.exp(scores - top)
                inverse = 1.0 / jnp.sum(expo, axis=0, keepdims=True)
                prob = expo.astype(jnp.bfloat16)
                prob_ref[0, 0, head, keys, :] = prob
                value = vt_ref[pl.ds(pl.multiple_of(head * feat, feat), feat), keys]
                outs.append(mm(value, prob) * inverse)
                inv_ref[pl.ds(head, 1), :] = inverse
            both = jnp.concatenate(outs, axis=0)
            attnt_ref[pl.ds(pl.multiple_of(index * 2 * feat, 2 * feat), 2 * feat), :] = both.astype(jnp.bfloat16)
            attn_ref[:, lanes] = both.T.astype(jnp.bfloat16)
            return carry

        lax.fori_loop(0, heads // 2, pair, 0)

    by_width(low_ref, width_ref, length, work)


def attention(low, width, q, k, vt, strips, sk, sq, length):
    rows, model = q.shape
    heads = strips.shape[0]
    feat = model // heads
    seqs, blocks = rows // length, length // BQ
    at = lambda s, b, *_: (s * blocks + b, 0)
    whole = lambda s, b, *_: (s, 0)
    at_t = lambda s, b, *_: (0, s * blocks + b)
    spec = pltpu.PrefetchScalarGridSpec(
        num_scalar_prefetch=2,
        grid=(seqs, blocks),
        in_specs=[
            pl.BlockSpec((BQ, model), at),
            pl.BlockSpec((length, model), whole),
            pl.BlockSpec((model, length), lambda s, b, *_: (0, s)),
            pl.BlockSpec(strips.shape, lambda s, b, *_: (0, 0, 0), pipeline_mode=pl.Buffered(1)),
            pl.BlockSpec((length, 1), whole),
            pl.BlockSpec((1, 1, BQ), lambda s, b, *_: (s * blocks + b, 0, 0)),
        ],
        out_specs=[
            pl.BlockSpec((BQ, model), at),
            pl.BlockSpec((model, BQ), at_t),
            pl.BlockSpec((1, 1, heads, length, BQ), lambda s, b, *_: (s, b, 0, 0, 0)),
            pl.BlockSpec((heads, BQ), at_t),
        ],
        scratch_shapes=[pltpu.VMEM((length, BQ), jnp.float32)],
    )
    return pl.pallas_call(
        functools.partial(fwd_kernel, heads=heads, feat=feat, length=length),
        grid_spec=spec,
        out_shape=[
            jax.ShapeDtypeStruct((rows, model), jnp.bfloat16),
            jax.ShapeDtypeStruct((model, rows), jnp.bfloat16),
            jax.ShapeDtypeStruct((seqs, blocks, heads, length, BQ), jnp.bfloat16),
            jax.ShapeDtypeStruct((heads, rows), jnp.float32),
        ],
        name="attend",
        compiler_params=pltpu.CompilerParams(vmem_limit_bytes=VMEM_CAP),
    )(low, width, q, k, vt, strips, sk, sq)


def bwd_kernel(low_ref, width_ref, q_ref, k_ref, kt_ref, v_ref, attnt_ref, dot_ref, prob_ref, inv_ref,
               dq_ref, dk_ref, dv_ref, diag_ref, dka_ref, dva_ref, *, heads, feat, length):
    seq, block = pl.program_id(0), pl.program_id(1)
    start = block * BQ

    @pl.when(jnp.logical_and(seq == 0, block == 0))
    def _():
        diag_ref[...] = jnp.zeros_like(diag_ref)

    @pl.when(block == 0)
    def _():
        dka_ref[...] = jnp.zeros_like(dka_ref)
        dva_ref[...] = jnp.zeros_like(dva_ref)

    def work(low, width):
        keys = pl.ds(low, width)
        row_b = pl.multiple_of(low - start + length - 2 * STEP, STEP)

        def pair(index, carry):
            lanes = pl.ds(pl.multiple_of(index * 2 * feat, 2 * feat), 2 * feat)
            query = q_ref[:, lanes]
            value = v_ref[keys, lanes]
            left = lax.broadcasted_iota(jnp.int32, query.shape, 1) < feat
            dqs = []
            dkey = dval = None
            for side in range(2):
                head = index * 2 + side
                feats = pl.ds(pl.multiple_of(head * feat, feat), feat)
                own = jnp.where(left if side == 0 else ~left, query, jnp.zeros_like(query))
                inverse = inv_ref[pl.ds(head, 1), :]
                scaled = dot_ref[feats, :].astype(jnp.float32) * inverse
                delta = jnp.sum(scaled * attnt_ref[feats, :].astype(jnp.float32), axis=0, keepdims=True)
                scaled = scaled.astype(jnp.bfloat16)
                blank = jnp.zeros_like(scaled)
                padded = jnp.concatenate([scaled, blank] if side == 0 else [blank, scaled], axis=0)
                prob = prob_ref[0, 0, head, keys, :]
                dprob = mm(value, padded)
                dsf = prob.astype(jnp.float32) * (dprob - delta)
                ds = dsf.astype(jnp.bfloat16)
                dv_part = mm(prob, padded, NT)
                dk_part = mm(ds, own)
                dval = dv_part if dval is None else dval + dv_part
                dkey = dk_part if dkey is None else dkey + dk_part
                dqs.append(mm(kt_ref[feats, keys], ds))
                gap = jnp.zeros((STEP, STEP), jnp.float32)
                diag_ref[head, pl.ds(row_b, width + STEP), :] += (
                    jnp.concatenate([gap, dsf[:, :STEP]], axis=0)
                    + jnp.concatenate([dsf[:, STEP:], gap], axis=0)
                )
            dka_ref[keys, lanes] += dkey
            dva_ref[keys, lanes] += dval
            dq_ref[:, lanes] = jnp.concatenate(dqs, axis=0).T.astype(jnp.bfloat16)
            return carry

        lax.fori_loop(0, heads // 2, pair, 0)

    by_width(low_ref, width_ref, length, work)

    @pl.when(block == pl.num_programs(1) - 1)
    def _():
        dk_ref[...] = dka_ref[...].astype(jnp.bfloat16)
        dv_ref[...] = dva_ref[...].astype(jnp.bfloat16)


def attention_back(low, width, q, k, kt, v, attnt, dot, prob, inv, length):
    rows, model = q.shape
    heads = inv.shape[0]
    feat = model // heads
    seqs, blocks = rows // length, length // BQ
    at = lambda s, b, *_: (s * blocks + b, 0)
    whole = lambda s, b, *_: (s, 0)
    at_t = lambda s, b, *_: (0, s * blocks + b)
    strip = (heads, 2 * length - STEP, STEP)
    spec = pltpu.PrefetchScalarGridSpec(
        num_scalar_prefetch=2,
        grid=(seqs, blocks),
        in_specs=[
            pl.BlockSpec((BQ, model), at),
            pl.BlockSpec((length, model), whole),
            pl.BlockSpec((model, length), lambda s, b, *_: (0, s)),
            pl.BlockSpec((length, model), whole),
            pl.BlockSpec((model, BQ), at_t),
            pl.BlockSpec((model, BQ), at_t),
            pl.BlockSpec((1, 1, heads, length, BQ), lambda s, b, *_: (s, b, 0, 0, 0)),
            pl.BlockSpec((heads, BQ), at_t),
        ],
        out_specs=[
            pl.BlockSpec((BQ, model), at),
            pl.BlockSpec((length, model), whole),
            pl.BlockSpec((length, model), whole),
            pl.BlockSpec(strip, lambda s, b, *_: (0, 0, 0)),
        ],
        scratch_shapes=[pltpu.VMEM((length, model), jnp.float32)] * 2,
    )
    return pl.pallas_call(
        functools.partial(bwd_kernel, heads=heads, feat=feat, length=length),
        grid_spec=spec,
        out_shape=[
            jax.ShapeDtypeStruct((rows, model), jnp.bfloat16),
            jax.ShapeDtypeStruct((rows, model), jnp.bfloat16),
            jax.ShapeDtypeStruct((rows, model), jnp.bfloat16),
            jax.ShapeDtypeStruct(strip, jnp.float32),
        ],
        name="attend_back",
        compiler_params=pltpu.CompilerParams(vmem_limit_bytes=VMEM_CAP),
    )(low, width, q, k, kt, v, attnt, dot, prob, inv)


def key_ranges(seg, length):
    firsts, lasts = seg[:, ::BQ], seg[:, BQ - 1 :: BQ]
    low = jnp.sum((seg[:, None, :] < firsts[:, :, None]).astype(jnp.int32), axis=-1)
    high = jnp.sum((seg[:, None, :] <= lasts[:, :, None]).astype(jnp.int32), axis=-1)
    low = low // STEP
    width = (high + STEP - 1) // STEP - low
    return (low * STEP).reshape(-1), width.reshape(-1)


def unskew_kernel(strip_ref, out_ref, *, length):
    data = strip_ref[0]
    data = jnp.concatenate([data, jnp.zeros((STEP, STEP), jnp.float32)], axis=0)
    rows = lax.broadcasted_iota(jnp.int32, (STEP, STEP), 0)
    cols = lax.broadcasted_iota(jnp.int32, (STEP, STEP), 1)
    flip = (rows + cols == STEP - 1).astype(jnp.bfloat16)
    high = data.astype(jnp.bfloat16)
    low = (data - high.astype(jnp.float32)).astype(jnp.bfloat16)
    turned = (mm(high, flip) + mm(low, flip)).T
    out_ref[0] = jnp.sum(pltpu.roll(turned, 1, 1, stride=1, stride_axis=0), axis=0, keepdims=True)


def diagonal_sums(strips):
    heads, rows, _ = strips.shape
    length = (rows + STEP) // 2
    out = pl.pallas_call(
        functools.partial(unskew_kernel, length=length),
        grid=(heads,),
        in_specs=[pl.BlockSpec((1, rows, STEP), lambda h: (h, 0, 0))],
        out_specs=pl.BlockSpec((1, 1, 2 * length), lambda h: (h, 0, 0)),
        out_shape=jax.ShapeDtypeStruct((heads, 1, 2 * length), jnp.float32),
        name="diagonal_sums",
        compiler_params=pltpu.CompilerParams(vmem_limit_bytes=VMEM_CAP),
    )(strips)
    return out.reshape(heads, 2 * length)


EPS = 1e-06
ROOT_HALF = 0.7071067811865476
INV_ROOT_TWO_PI = 0.3989422804014327
BF = jnp.bfloat16
F32 = jnp.float32


def bits_of(axis):
    size = lax.axis_size(axis)
    count = size.bit_length() - 1
    assert size == 1 << count
    return count


def swap(value, axis, bit):
    size = lax.axis_size(axis)
    return lax.ppermute(value, axis, [(i, i ^ (1 << bit)) for i in range(size)])


def collect(shard):
    me = lax.axis_index("fsdp")
    held = {0: shard}
    for bit in reversed(range(bits_of("fsdp"))):
        got = {k ^ (1 << bit): swap(v, "fsdp", bit) for k, v in held.items()}
        held.update(got)
    rows = shard.shape[0]
    whole = jnp.zeros((rows * len(held),) + shard.shape[1:], shard.dtype)
    for k, v in held.items():
        whole = lax.dynamic_update_slice_in_dim(whole, v, (me ^ k) * rows, 0)
    return whole


def share_out(grad):
    me = lax.axis_index("fsdp")
    size = lax.axis_size("fsdp")
    rows = grad.shape[0] // size
    part = {k: lax.dynamic_slice_in_dim(grad, (me ^ k) * rows, rows, 0) for k in range(size)}
    for bit in range(bits_of("fsdp")):
        step = 1 << bit
        kept = {}
        for k in part:
            if not k & step:
                kept[k] = part[k] + swap(part[k ^ step].astype(BF), "fsdp", bit).astype(F32)
        part = kept
    return part[0]


def halves(value, axis, side):
    size = value.shape[axis] // 2
    return (
        lax.dynamic_slice_in_dim(value, side * size, size, axis),
        lax.dynamic_slice_in_dim(value, (1 - side) * size, size, axis),
    )


def total(value):
    me = lax.axis_index("grp")
    count = bits_of("grp")
    trail = []
    for bit in range(count):
        axis = 1 if bit == 0 else 0
        side = (me >> bit) & 1
        mine, other = halves(value, axis, side)
        value = mine + swap(other.astype(BF), "grp", bit).astype(F32)
        trail.append((axis, side))
    value = value.astype(BF)
    for bit in reversed(range(count)):
        axis, side = trail[bit]
        other = swap(value, "grp", bit)
        value = jnp.where(
            side == 0,
            jnp.concatenate([value, other], axis=axis),
            jnp.concatenate([other, value], axis=axis),
        )
    return value.astype(F32)


def total_small(value):
    for axis in ("fsdp", "grp"):
        for bit in range(bits_of(axis)):
            value = value + swap(value, axis, bit)
    return value


def forward_dot(value, weight):
    return mm(value, weight)


def outer(left, right):
    return mm(left, right, (((0,), (0,)), ((), ())))


def backward_dot(grad, weight):
    return mm(grad, weight, NT)


def norm_scale(value):
    return lax.rsqrt(jnp.mean(value * value, axis=-1, keepdims=True) + EPS)


def norm_back(grad, value, scale, gain):
    weighted = grad * gain
    inner = jnp.mean(weighted * value, axis=-1, keepdims=True)
    dvalue = scale * weighted - value * (scale * scale * scale) * inner
    dgain = jnp.sum(grad * value * scale, axis=0)
    return (dvalue, dgain)


def gelu_slope(value):
    cdf = 0.5 * (1.0 + lax.erf(value * ROOT_HALF))
    return cdf + value * jnp.exp(-0.5 * value * value) * INV_ROOT_TWO_PI


def body(
    layer_input,
    segment_ids,
    bucket_table,
    gain_attn,
    weight_query,
    weight_key,
    weight_value,
    weight_out,
    gain_ffn,
    weight_in,
    weight_back,
    gain_final,
    weight_embed,
    bias_table,
    cotangent,
):
    micro, length, width = layer_input.shape
    heads = bias_table.shape[1]
    size = lax.axis_size("fsdp")
    me = lax.axis_index("fsdp")
    buckets = bias_table.shape[0] * size
    rows = micro * length
    small = jnp.concatenate([gain_attn, gain_ffn, gain_final, bias_table.reshape(-1)]).reshape(1, -1)
    small = collect(small)
    part = width // size
    g_one = small[:, :part].reshape(width).astype(F32)
    g_two = small[:, part : 2 * part].reshape(width).astype(F32)
    g_three = small[:, 2 * part : 3 * part].reshape(width).astype(F32)
    table = small[:, 3 * part :].reshape(buckets, heads)
    wq, wk, wv = collect(weight_query), collect(weight_key), collect(weight_value)
    wo, wi, wb, we = collect(weight_out), collect(weight_in), collect(weight_back), collect(weight_embed)

    onehot = (bucket_table[:, None] == lax.iota(jnp.int32, buckets)[None, :]).astype(BF)
    bias_rows = lax.dot_general(table, onehot, (((0,), (1,)), ((), ())), preferred_element_type=F32)
    strips = bias_strips(bias_rows)
    low, wide = key_ranges(segment_ids, length)
    seg_col = segment_ids.reshape(rows, 1)
    seg_row = segment_ids.reshape(rows // BQ, 1, BQ)

    xs = layer_input.reshape(rows, width).astype(F32)
    scale1 = norm_scale(xs)
    h1 = (xs * scale1 * g_one).astype(BF)
    query, key, value = (forward_dot(h1, w).astype(BF) for w in (wq, wk, wv))
    key_t = mm(wk, h1, (((0,), (1,)), ((), ()))).astype(BF)
    value_t = mm(wv, h1, (((0,), (1,)), ((), ()))).astype(BF)
    attn, attn_t, probs, inverse = attention(
        low, wide, query, key, value_t, strips, seg_col, seg_row, length
    )
    x2 = xs + forward_dot(attn, wo)
    scale2 = norm_scale(x2)
    h2 = (x2 * scale2 * g_two).astype(BF)
    pre = forward_dot(h2, wi)
    hidden = jax.nn.gelu(pre, approximate=False).astype(BF)
    slope = gelu_slope(pre).astype(BF)
    x3 = x2 + forward_dot(hidden, wb)
    scale3 = norm_scale(x3)
    h3 = (x3 * scale3 * g_three).astype(BF)
    states = forward_dot(h3, we)

    upstream = cotangent.reshape(rows, -1)
    d_embed = outer(h3, upstream)
    dx3, dg_three = norm_back(backward_dot(upstream, we), x3, scale3, g_three)
    d_branch = dx3.astype(BF)
    d_back = outer(hidden, d_branch)
    d_pre = (backward_dot(d_branch, wb) * slope.astype(F32)).astype(BF)
    d_in = outer(h2, d_pre)
    ffn_part, dg_two = norm_back(backward_dot(d_pre, wi), x2, scale2, g_two)
    dx2 = dx3 + ffn_part
    d_attn_out = dx2.astype(BF)
    d_out = outer(attn, d_attn_out)
    d_attn_t = mm(wo, d_attn_out, NT).astype(BF)
    dq, dk, dv, diag = attention_back(
        low, wide, query, key, key_t, value, attn_t, d_attn_t, probs, inverse, length
    )
    d_query, d_key, d_value = outer(h1, dq), outer(h1, dk), outer(h1, dv)
    dh1 = backward_dot(dq, wq) + backward_dot(dk, wk) + backward_dot(dv, wv)
    attn_part, dg_one = norm_back(dh1, xs, scale1, g_one)
    d_input = dx2 + attn_part
    d_table = jnp.dot(
        diagonal_sums(diag), onehot.astype(F32), precision=lax.Precision.HIGHEST
    ).T

    g_embed, g_back, g_in, g_out, g_query, g_key, g_value = (
        total(share_out(g)) for g in (d_embed, d_back, d_in, d_out, d_query, d_key, d_value)
    )
    tiny = jnp.concatenate([dg_one, dg_two, dg_three, d_table.reshape(-1)]).reshape(-1, 128)
    tiny = total_small(tiny).reshape(-1)

    def own(vector, count):
        return lax.dynamic_slice_in_dim(vector, me * count, count, 0)

    gain_grads = [own(tiny[k * width : (k + 1) * width], part) for k in range(3)]
    g_table = own(tiny[3 * width :].reshape(buckets, heads), buckets // size)
    return (
        states.reshape(micro, length, -1),
        d_input.reshape(micro, length, width),
        gain_grads[0],
        g_query,
        g_key,
        g_value,
        g_out,
        gain_grads[1],
        g_in,
        g_back,
        gain_grads[2],
        g_embed,
        g_table,
    )


def solution(mesh):
    placed = (
        P(None, ("grp", "fsdp"), None),
        P(None, ("grp", "fsdp")),
        P(),
        P("fsdp"),
        P("fsdp", None),
        P("fsdp", None),
        P("fsdp", None),
        P("fsdp", None),
        P("fsdp"),
        P("fsdp", None),
        P("fsdp", None),
        P("fsdp"),
        P("fsdp", None),
        P("fsdp", None),
        P(None, ("grp", "fsdp"), None),
    )
    return jax.shard_map(
        body,
        mesh=mesh,
        in_specs=placed,
        out_specs=(
            P(None, ("grp", "fsdp"), None),
            P(None, ("grp", "fsdp"), None),
            P("fsdp"),
            P("fsdp", None),
            P("fsdp", None),
            P("fsdp", None),
            P("fsdp", None),
            P("fsdp"),
            P("fsdp", None),
            P("fsdp", None),
            P("fsdp"),
            P("fsdp", None),
            P("fsdp", None),
        ),
        check_vma=False,
    )
```

```python
import functools
import jax
import jax.numpy as jnp
from jax import lax
from jax.experimental import pallas as pl
from jax.experimental.pallas import tpu as pltpu
from jax.sharding import PartitionSpec as P

BQ = 256
STEP = 128
NEGATIVE = -1e30
VMEM_CAP = 60 * 1024 * 1024
EPS = 1e-06
INV_ROOT_TWO_PI = 0.3989422804014327
BF = jnp.bfloat16
F32 = jnp.float32
NT = (((1,), (1,)), ((), ()))
NN = (((1,), (0,)), ((), ()))
S = jax.ShapeDtypeStruct
ANY = pl.BlockSpec(memory_space=pl.ANY)
PARAMS = pltpu.CompilerParams(vmem_limit_bytes=VMEM_CAP)


def cost(flops, moved, special=0):
    return pl.CostEstimate(flops=flops, bytes_accessed=moved, transcendentals=special)


def mm(a, b, dims=NN):
    return lax.dot_general(a, b, dims, preferred_element_type=F32)


def norm_scale(value):
    return lax.rsqrt(jnp.mean(value * value, axis=-1, keepdims=True) + EPS)


def norm_back(grad, value, scale, gain):
    weighted = grad * gain
    inner = jnp.mean(weighted * value, axis=-1, keepdims=True)
    dvalue = scale * weighted - value * (scale * scale * scale) * inner
    return dvalue


def gelu_parts(value):
    t = 1.0 / (1.0 + (0.3275911 * 0.7071067811865476) * jnp.abs(value))
    poly = 0.5307027145
    for factor in (-0.7265760135, 0.7107068705, -0.142248368, 0.127414796):
        poly = poly * t + factor
    bell = jnp.exp(-0.5 * value * value)
    tail = poly * t * bell
    cdf = jnp.where(value < 0.0, tail, 1.0 - tail)
    return value * cdf, cdf + value * bell * INV_ROOT_TWO_PI


def run_copies(jobs, sems):
    copies = [pltpu.make_async_copy(a, b, sems.at[i]) for i, (a, b) in enumerate(jobs)]
    for copy in copies:
        copy.start()
    for copy in copies:
        copy.wait()


def place(me, k, rows):
    return pl.multiple_of(jnp.bitwise_xor(me, k) * rows, 16)


def placing(me, pieces, target, lanes=slice(None)):
    rows = pieces[0].shape[0]
    return [
        (piece.at[:, lanes], target.at[pl.ds(place(me, k, rows), rows), :]) for k, piece in enumerate(pieces)
    ]


def project_kernel(me_ref, x_ref, gain_ref, *refs, count, first, lanes):
    pieces, refs = refs[:count], refs[count:]
    if first:
        q_ref, k_ref, v_ref, kt_ref, vt_ref, ht_ref, weight_ref, sems = refs
    else:
        q_ref, k_ref, v_ref, kt_ref, vt_ref, weight_ref, sems = refs

    @pl.when(pl.program_id(0) == 0)
    def _():
        run_copies(placing(me_ref[0], pieces, weight_ref, lanes), sems)

    value = x_ref[...].astype(F32)
    h = (value * norm_scale(value) * gain_ref[...]).astype(BF)
    if first:
        ht_ref[...] = h.T
    part = q_ref.shape[1]
    out = mm(h, weight_ref[...]).astype(BF)
    q_ref[...] = out[:, :part]
    k_ref[...] = out[:, part : 2 * part]
    kt_ref[...] = out[:, part : 2 * part].T
    v_ref[...] = out[:, 2 * part :]
    vt_ref[...] = out[:, 2 * part :].T


def project(me, x, gain, pieces, wide, at, first, block=256):
    rows, width = x.shape
    part = wide // 3
    natural = lambda cols: pl.BlockSpec((block, cols), lambda i, *_: (i, 0))
    turned = lambda cols: pl.BlockSpec((cols, block), lambda i, *_: (0, i))
    return pl.pallas_call(
        functools.partial(project_kernel, count=len(pieces), first=first, lanes=slice(at, at + wide)),
        grid_spec=pltpu.PrefetchScalarGridSpec(
            num_scalar_prefetch=1,
            grid=(rows // block,),
            in_specs=[natural(width), pl.BlockSpec((1, width), lambda i, *_: (0, 0))] + [ANY] * len(pieces),
            out_specs=[natural(part)] * 3 + [turned(part)] * 2 + [turned(width)] * first,
            scratch_shapes=[pltpu.VMEM((width, wide), BF), pltpu.SemaphoreType.DMA((len(pieces),))],
        ),
        out_shape=[S((rows, part), BF)] * 3 + [S((part, rows), BF)] * 2 + [S((width, rows), BF)] * first,
        name="project",
        cost_estimate=cost(2 * rows * width * wide, 4 * rows * (width + wide)),
        compiler_params=PARAMS,
    )(me, x, gain, *pieces)


def strip_kernel(rows_ref, strip_ref, *, length):
    rows = jnp.broadcast_to(rows_ref[0], (STEP, 2 * length))
    turned = pltpu.roll(rows, 2 * length - STEP, 1, stride=1, stride_axis=0)
    strip_ref[0] = turned[:, : 2 * length - STEP].T


def bias_strips(rows):
    heads, twice = rows.shape
    return pl.pallas_call(
        functools.partial(strip_kernel, length=twice // 2),
        grid=(heads,),
        in_specs=[pl.BlockSpec((1, 1, twice), lambda h: (h, 0, 0))],
        out_specs=pl.BlockSpec((1, twice - STEP, STEP), lambda h: (h, 0, 0)),
        out_shape=S((heads, twice - STEP, STEP), F32),
        name="bias_strips",
        cost_estimate=cost(heads * twice * STEP * 20, heads * twice * STEP * 4),
        compiler_params=PARAMS,
    )(rows.reshape(heads, 1, twice))


def by_width(low_ref, width_ref, length, work):
    step = pl.program_id(0) * pl.num_programs(1) + pl.program_id(1)
    low = pl.multiple_of(low_ref[step], STEP)
    width = width_ref[step]
    for blocks in range(BQ // STEP, length // STEP + 1):

        @pl.when(width == blocks)
        def _(blocks=blocks):
            work(low, blocks * STEP)


def half_of(query, side, feat):
    left = lax.broadcasted_iota(jnp.int32, query.shape, 1) < feat
    return jnp.where(left if side == 0 else ~left, query, jnp.zeros_like(query))


def attend_kernel(
    low_ref, width_ref, q_ref, k_ref, vt_ref, strip_ref, sk_ref, sq_ref,
    attn_ref, attnt_ref, prob_ref, inv_ref, mask_ref, *, heads, feat, length,
):
    start = pl.program_id(1) * BQ

    def work(low, width):
        keys = pl.ds(low, width)
        mask_ref[:width] = jnp.where(sk_ref[keys, :] == sq_ref[0], 0.0, NEGATIVE)
        row_a = pl.multiple_of(low - start + length - STEP, STEP)
        row_b = pl.multiple_of(low - start + length - 2 * STEP, STEP)
        for index in range(heads // 2):
            lanes = slice(index * 2 * feat, (index + 1) * 2 * feat)
            query = q_ref[:, lanes]
            key = k_ref[keys, lanes]
            outs = []
            for side in range(2):
                head = index * 2 + side
                bias = jnp.concatenate(
                    [strip_ref[head, pl.ds(row_a, width), :], strip_ref[head, pl.ds(row_b, width), :]],
                    axis=1,
                )
                scores = mm(key, half_of(query, side, feat), NT) + bias + mask_ref[:width]
                top = jnp.max(scores, axis=0, keepdims=True)
                expo = jnp.exp(scores - top)
                inverse = 1.0 / jnp.sum(expo, axis=0, keepdims=True)
                prob = expo.astype(BF)
                prob_ref[0, 0, head, keys, :] = prob
                outs.append(mm(vt_ref[head * feat : (head + 1) * feat, keys], prob) * inverse)
                inv_ref[0, head : head + 1, :] = inverse
            both = jnp.concatenate(outs, axis=0)
            attnt_ref[lanes, :] = both.astype(BF)
            attn_ref[:, lanes] = both.T.astype(BF)

    by_width(low_ref, width_ref, length, work)


def attend(low, width, q, k, vt, strips, sk, sq, length, heads, group):
    rows, part = q.shape
    feat = part // heads
    seqs, blocks = rows // length, length // BQ
    at = lambda s, b, *_: (s * blocks + b, 0)
    whole = lambda s, b, *_: (s, 0)
    at_t = lambda s, b, *_: (0, s * blocks + b)
    return pl.pallas_call(
        functools.partial(attend_kernel, heads=heads, feat=feat, length=length),
        grid_spec=pltpu.PrefetchScalarGridSpec(
            num_scalar_prefetch=2,
            grid=(seqs, blocks),
            in_specs=[
                pl.BlockSpec((BQ, part), at),
                pl.BlockSpec((length, part), whole),
                pl.BlockSpec((part, length), lambda s, b, *_: (0, s)),
                pl.BlockSpec(
                    (heads,) + strips.shape[1:], lambda s, b, *_: (group, 0, 0), pipeline_mode=pl.Buffered(1)
                ),
                pl.BlockSpec((length, 1), whole),
                pl.BlockSpec((1, 1, BQ), lambda s, b, *_: (s * blocks + b, 0, 0)),
            ],
            out_specs=[
                pl.BlockSpec((BQ, part), at),
                pl.BlockSpec((part, BQ), at_t),
                pl.BlockSpec((1, 1, heads, length, BQ), lambda s, b, *_: (s, b, 0, 0, 0)),
                pl.BlockSpec((1, heads, BQ), lambda s, b, *_: (0, 0, s * blocks + b)),
            ],
            scratch_shapes=[pltpu.VMEM((length, BQ), F32)],
        ),
        out_shape=[
            S((rows, part), BF),
            S((part, rows), BF),
            S((seqs, blocks, heads, length, BQ), BF),
            S((1, heads, rows), F32),
        ],
        name="attend",
        cost_estimate=cost(16 * rows * length * part, 2 * rows * heads * length, rows * heads * length),
        compiler_params=PARAMS,
    )(low, width, q, k, vt, strips, sk, sq)


def unskew(data):
    data = jnp.concatenate([data, jnp.zeros((STEP, STEP), F32)], axis=0)
    rows = lax.broadcasted_iota(jnp.int32, (STEP, STEP), 0)
    cols = lax.broadcasted_iota(jnp.int32, (STEP, STEP), 1)
    flip = (rows + cols == STEP - 1).astype(BF)
    high = data.astype(BF)
    low = (data - high.astype(F32)).astype(BF)
    turned = (mm(high, flip) + mm(low, flip)).T
    return jnp.sum(pltpu.roll(turned, 1, 1, stride=1, stride_axis=0), axis=0, keepdims=True)


def attend_back_kernel(
    low_ref, width_ref, q_ref, k_ref, kt_ref, v_ref, attnt_ref, dot_ref, prob_ref, inv_ref,
    dq_ref, dk_ref, dv_ref, sum_ref, diag_ref, dka_ref, dva_ref, *, heads, feat, length,
):
    seq, block = pl.program_id(0), pl.program_id(1)
    start = block * BQ

    @pl.when(jnp.logical_and(seq == 0, block == 0))
    def _():
        diag_ref[...] = jnp.zeros_like(diag_ref)

    @pl.when(block == 0)
    def _():
        dka_ref[...] = jnp.zeros_like(dka_ref)
        dva_ref[...] = jnp.zeros_like(dva_ref)

    def work(low, width):
        keys = pl.ds(low, width)
        row_b = pl.multiple_of(low - start + length - 2 * STEP, STEP)
        for index in range(heads // 2):
            lanes = slice(index * 2 * feat, (index + 1) * 2 * feat)
            query = q_ref[:, lanes]
            value = v_ref[keys, lanes]
            dqs = []
            dkey = dval = None
            for side in range(2):
                head = index * 2 + side
                feats = slice(head * feat, (head + 1) * feat)
                inverse = inv_ref[0, head : head + 1, :]
                scaled = dot_ref[feats, :].astype(F32) * inverse
                delta = jnp.sum(scaled * attnt_ref[feats, :].astype(F32), axis=0, keepdims=True)
                scaled = scaled.astype(BF)
                blank = jnp.zeros_like(scaled)
                padded = jnp.concatenate([scaled, blank] if side == 0 else [blank, scaled], axis=0)
                prob = prob_ref[0, 0, head, keys, :]
                dprob = mm(value, padded)
                wide = prob.astype(F32) * (dprob - delta)
                ds = wide.astype(BF)
                dv_part = mm(prob, padded, NT)
                dk_part = mm(ds, half_of(query, side, feat))
                dval = dv_part if dval is None else dval + dv_part
                dkey = dk_part if dkey is None else dkey + dk_part
                dqs.append(mm(kt_ref[feats, keys], ds))
                gap = jnp.zeros((STEP, STEP), F32)
                diag_ref[head, pl.ds(row_b, width + STEP), :] += jnp.concatenate(
                    [gap, wide[:, :STEP]], axis=0
                ) + jnp.concatenate([wide[:, STEP:], gap], axis=0)
            dka_ref[keys, lanes] += dkey
            dva_ref[keys, lanes] += dval
            dq_ref[:, lanes] = jnp.concatenate(dqs, axis=0).T.astype(BF)

    by_width(low_ref, width_ref, length, work)

    @pl.when(block == pl.num_programs(1) - 1)
    def _():
        dk_ref[...] = dka_ref[...].astype(BF)
        dv_ref[...] = dva_ref[...].astype(BF)

    @pl.when(jnp.logical_and(seq == pl.num_programs(0) - 1, block == pl.num_programs(1) - 1))
    def _():
        for head in range(heads):
            sum_ref[head : head + 1, :] = unskew(diag_ref[head])


def attend_back(low, width, q, k, kt, v, attnt, dot, prob, inv, length, group):
    rows, part = q.shape
    heads = inv.shape[1]
    feat = part // heads
    seqs, blocks = rows // length, length // BQ
    at = lambda s, b, *_: (s * blocks + b, 0)
    whole = lambda s, b, *_: (s, 0)
    at_t = lambda s, b, *_: (0, s * blocks + b)
    return pl.pallas_call(
        functools.partial(attend_back_kernel, heads=heads, feat=feat, length=length),
        grid_spec=pltpu.PrefetchScalarGridSpec(
            num_scalar_prefetch=2,
            grid=(seqs, blocks),
            in_specs=[
                pl.BlockSpec((BQ, part), at),
                pl.BlockSpec((length, part), whole),
                pl.BlockSpec((part, length), lambda s, b, *_: (0, s)),
                pl.BlockSpec((length, part), whole),
                pl.BlockSpec((part, BQ), at_t),
                pl.BlockSpec((part, BQ), lambda s, b, *_: (group, s * blocks + b)),
                pl.BlockSpec((1, 1, heads, length, BQ), lambda s, b, *_: (s, b, 0, 0, 0)),
                pl.BlockSpec((1, heads, BQ), lambda s, b, *_: (0, 0, s * blocks + b)),
            ],
            out_specs=[
                pl.BlockSpec((BQ, part), at),
                pl.BlockSpec((length, part), whole),
                pl.BlockSpec((length, part), whole),
                pl.BlockSpec((heads, 2 * length), lambda s, b, *_: (0, 0)),
            ],
            scratch_shapes=[
                pltpu.VMEM((heads, 2 * length - STEP, STEP), F32),
                pltpu.VMEM((length, part), F32),
                pltpu.VMEM((length, part), F32),
            ],
        ),
        out_shape=[S((rows, part), BF)] * 3 + [S((heads, 2 * length), F32)],
        name="attend_back",
        cost_estimate=cost(32 * rows * length * part, 2 * rows * heads * length),
        compiler_params=PARAMS,
    )(low, width, q, k, kt, v, attnt, dot, prob, inv)


def key_ranges(seg):
    firsts, lasts = seg[:, ::BQ], seg[:, BQ - 1 :: BQ]
    low = jnp.sum((seg[:, None, :] < firsts[:, :, None]).astype(jnp.int32), axis=-1)
    high = jnp.sum((seg[:, None, :] <= lasts[:, :, None]).astype(jnp.int32), axis=-1)
    low = low // STEP
    width = (high + STEP - 1) // STEP - low
    return (low * STEP).reshape(-1), width.reshape(-1)


def ffn_kernel(me_ref, x_ref, up_ref, gain_ref, *refs, chunk, count, groups):
    attns, refs = refs[:groups], refs[groups:]
    pieces, refs = refs[:count], refs[count:]
    (states_ref, dx2_ref, dot_ref, da_ref, h2t_ref, h3t_ref, dbt_ref, hid_ref, dpre_ref,
     slope_ref, wo_ref, wi_ref, wb_ref, we_ref, sems) = refs
    width, wide = wi_ref.shape
    embed = we_ref.shape[1]

    @pl.when(pl.program_id(0) == 0)
    def _():
        me, rows = me_ref[0], pieces[0].shape[0]
        copies = placing(me, pieces, wo_ref, slice(0, width))
        copies += placing(me, pieces, wi_ref, slice(width, width + wide))
        copies += placing(me, pieces, we_ref, slice(width + wide, width + wide + embed))
        parts = wide // width
        for k, piece in enumerate(pieces):
            for q in range(parts):
                at = width + wide + embed + q * width
                spot = pl.ds(place(me, k, parts * rows) + q * rows, rows)
                copies.append((piece.at[:, at : at + width], wb_ref.at[spot, :]))
        run_copies(copies, sems)

    g_two, g_three = gain_ref[0:1, :], gain_ref[1:2, :]
    attn = jnp.concatenate([a[...] for a in attns], axis=1)
    x2 = x_ref[...].astype(F32) + mm(attn, wo_ref[...])
    scale2 = norm_scale(x2)
    h2 = (x2 * scale2 * g_two).astype(BF)
    x3 = x2
    for at in range(0, wide, chunk):
        cols = slice(at, at + chunk)
        hidden, slope = gelu_parts(mm(h2, wi_ref[:, cols]))
        hidden = hidden.astype(BF)
        hid_ref[:, cols] = hidden
        slope_ref[:, cols] = slope.astype(BF)
        x3 = x3 + mm(hidden, wb_ref[cols, :])
    scale3 = norm_scale(x3)
    h3 = (x3 * scale3 * g_three).astype(BF)
    states_ref[...] = mm(h3, we_ref[...])
    dx3 = norm_back(mm(up_ref[...], we_ref[...], NT), x3, scale3, g_three)
    db = dx3.astype(BF)
    dh2 = None
    for at in range(0, wide, chunk):
        cols = slice(at, at + chunk)
        dpre = (mm(db, wb_ref[cols, :], NT) * slope_ref[:, cols].astype(F32)).astype(BF)
        dpre_ref[:, cols] = dpre
        part = mm(dpre, wi_ref[:, cols], NT)
        dh2 = part if dh2 is None else dh2 + part
    part = norm_back(dh2, x2, scale2, g_two)
    dx2 = dx3 + part
    da = dx2.astype(BF)
    dx2_ref[...] = dx2
    da_ref[...] = da
    dot_ref[...] = mm(wo_ref[...], da, NT).astype(BF)
    h2t_ref[...] = h2.T
    h3t_ref[...] = h3.T
    dbt_ref[...] = db.T


def feed_forward(me, x, attns, up, gains, pieces, block=256, chunk=768):
    rows, width = x.shape
    count = len(pieces)
    embed = up.shape[1]
    wide = (pieces[0].shape[1] - width - embed) // 2
    fixed = lambda i, *_: (0, 0)
    natural = lambda cols: pl.BlockSpec((block, cols), lambda i, *_: (i, 0))
    turned = pl.BlockSpec((width, block), lambda i, *_: (0, i))
    return pl.pallas_call(
        functools.partial(ffn_kernel, chunk=chunk, count=count, groups=len(attns)),
        grid_spec=pltpu.PrefetchScalarGridSpec(
            num_scalar_prefetch=1,
            grid=(rows // block,),
            in_specs=[natural(width), natural(embed), pl.BlockSpec(gains.shape, fixed)]
            + [natural(a.shape[1]) for a in attns]
            + [ANY] * len(pieces),
            out_specs=[
                natural(embed), natural(width), turned, natural(width), turned, turned, turned,
                natural(wide), natural(wide),
            ],
            scratch_shapes=[
                pltpu.VMEM((block, wide), BF),
                pltpu.VMEM((width, width), BF),
                pltpu.VMEM((width, wide), BF),
                pltpu.VMEM((wide, width), BF),
                pltpu.VMEM((width, embed), BF),
                pltpu.SemaphoreType.DMA((count * (3 + wide // width),)),
            ],
        ),
        out_shape=[
            S((rows, embed), F32), S((rows, width), F32), S((width, rows), BF), S((rows, width), BF),
            S((width, rows), BF), S((width, rows), BF), S((width, rows), BF),
            S((rows, wide), BF), S((rows, wide), BF),
        ],
        name="feed_forward",
        cost_estimate=cost(4 * rows * width * (4 * wide + 2 * width), 20 * rows * wide, 2 * rows * wide),
        compiler_params=PARAMS,
    )(me, x, up, gains, *attns, *pieces)


def input_back_kernel(me_ref, x_ref, dx2_ref, gain_ref, *refs, spans, count, threaded):
    groups = len(spans)
    parts, refs = refs[: 3 * groups], refs[3 * groups :]
    pieces, refs = refs[: groups * count], refs[groups * count + threaded :]
    out_ref, weight_ref, sems = refs

    @pl.when(pl.program_id(0) == 0)
    def _():
        copies = []
        for g, lanes in enumerate(spans):
            copies += placing(me_ref[0], pieces[g * count : (g + 1) * count], weight_ref.at[g], lanes)
        run_copies(copies, sems)

    value = x_ref[...].astype(F32)
    scale = norm_scale(value)
    dh = None
    for g in range(groups):
        term = mm(jnp.concatenate([p[...] for p in parts[3 * g : 3 * g + 3]], axis=1), weight_ref[g], NT)
        dh = term if dh is None else dh + term
    out_ref[...] = dx2_ref[...] + norm_back(dh, value, scale, gain_ref[...])


def input_back(me, x, dx2, gain, parts, pieces, spans, first, steps, held, block=256):
    rows, width = x.shape
    natural = lambda cols: pl.BlockSpec((block, cols), lambda i, *_: (i + first, 0))
    fixed = lambda i, *_: (0, 0)
    operands = [me, x, dx2, gain, *parts, *pieces] + ([] if held is None else [held])
    return pl.pallas_call(
        functools.partial(
            input_back_kernel, spans=spans, count=len(pieces) // len(spans), threaded=0 if held is None else 1
        ),
        grid_spec=pltpu.PrefetchScalarGridSpec(
            num_scalar_prefetch=1,
            grid=(steps,),
            in_specs=[natural(width), natural(width), pl.BlockSpec((1, width), fixed)]
            + [natural(p.shape[1]) for p in parts]
            + [ANY] * (len(pieces) + (held is not None)),
            out_specs=natural(width),
            scratch_shapes=[
                pltpu.VMEM((len(spans), width, 3 * parts[0].shape[1]), BF),
                pltpu.SemaphoreType.DMA((len(pieces),)),
            ],
        ),
        out_shape=S((rows, width), F32),
        input_output_aliases={} if held is None else {len(operands) - 1: 0},
        name="input_back",
        cost_estimate=cost(6 * steps * block * width * width, 16 * steps * block * width),
        compiler_params=PARAMS,
    )(*operands)


def grad_rows_kernel(me_ref, *refs, count, lefts):
    lefts, rights, (keep_ref, send_ref, full_ref) = refs[:lefts], refs[lefts:-3], refs[-3:]
    rows = full_ref.shape[0] // count
    down = 0
    for left in lefts:
        at = 0
        for right in rights:
            cols = slice(at, at + right.shape[1])
            at += right.shape[1]
            full_ref[down : down + left.shape[0], cols] = mm(left[...], right[...])
        down += left.shape[0]
    for k in range(count):
        spot = pl.ds(pl.multiple_of(jnp.bitwise_xor(me_ref[0], k) * rows, 16), rows)
        (send_ref if k & 1 else keep_ref)[k >> 1] = full_ref[spot, :].astype(BF)


def grad_rows(me, lefts, rights, count, tile=768, first=0, tiles=None):
    m, rows = sum(left.shape[0] for left in lefts), lefts[0].shape[1]
    if len(rights) > 1:
        tile, tiles = sum(r.shape[1] for r in rights), 1
        specs = [pl.BlockSpec(r.shape, lambda j, *_: (0, 0)) for r in rights]
    else:
        tile = min(tile, rights[0].shape[1])
        tiles = rights[0].shape[1] // tile if tiles is None else tiles
        specs = [pl.BlockSpec((rows, tile), lambda j, *_: (0, j + first))]
    out = pl.BlockSpec((count // 2, m // count, tile), lambda j, *_: (0, 0, j))
    shape = S((count // 2, m // count, tile * tiles), BF)
    return pl.pallas_call(
        functools.partial(grad_rows_kernel, count=count, lefts=len(lefts)),
        grid_spec=pltpu.PrefetchScalarGridSpec(
            num_scalar_prefetch=1,
            grid=(tiles,),
            in_specs=[pl.BlockSpec(left.shape, lambda j, *_: (0, 0), pipeline_mode=pl.Buffered(1)) for left in lefts]
            + specs,
            out_specs=[out, out],
            scratch_shapes=[pltpu.VMEM((m, tile), F32)],
        ),
        out_shape=[shape, shape],
        name="weight_grad",
        cost_estimate=cost(2 * m * rows * tile * tiles, 2 * rows * (m + tile * tiles)),
        compiler_params=PARAMS,
    )(me, *lefts, *rights)


def grad_set_kernel(me_ref, *refs, shapes, count, extra):
    operands = sum(a + b for a, b in shapes)
    sources, refs = refs[:operands], refs[operands:]
    if extra:
        extra_ref, refs = refs[0], refs[1:]
    keep_ref, send_ref, full_ref = refs[:3]
    held, sems = refs[3:-1], refs[-1]
    copies = [pltpu.make_async_copy(a, b, sems.at[i]) for i, (a, b) in enumerate(zip(sources, held))]
    for copy in copies:
        copy.start()
    rows = full_ref.shape[0] // count
    index = at = 0
    for lefts, rights in shapes:
        left = held[index : index + lefts]
        right = held[index + lefts : index + lefts + rights]
        for copy in copies[index : index + lefts]:
            copy.wait()
        for n, r in enumerate(right):
            copies[index + lefts + n].wait()
            down = 0
            for part in left:
                full_ref[down : down + part.shape[0], at : at + r.shape[1]] = mm(part[...], r[...])
                down += part.shape[0]
            at += r.shape[1]
        index += lefts + rights
    for k in range(count):
        target = send_ref if k & 1 else keep_ref
        target[k >> 1, :, :at] = full_ref[pl.ds(place(me_ref[0], k, rows), rows), :].astype(BF)
        if extra:
            target[k >> 1, :, at:] = extra_ref[k]


def grad_set(me, jobs, count, extra=None):
    operands = [x for lefts, rights in jobs for x in lefts + rights]
    m, rows = sum(x.shape[0] for x in jobs[0][0]), jobs[0][0][0].shape[1]
    n = sum(r.shape[1] for _, rights in jobs for r in rights)
    wide = n + (0 if extra is None else extra.shape[2])
    shape = S((count // 2, m // count, wide), BF)
    out = pl.BlockSpec(shape.shape, lambda j, *_: (0, 0, 0))
    more = [] if extra is None else [extra]
    return pl.pallas_call(
        functools.partial(
            grad_set_kernel,
            shapes=tuple((len(a), len(b)) for a, b in jobs),
            count=count,
            extra=extra is not None,
        ),
        grid_spec=pltpu.PrefetchScalarGridSpec(
            num_scalar_prefetch=1,
            grid=(1,),
            in_specs=[ANY] * len(operands) + [pl.BlockSpec(e.shape, lambda j, *_: (0, 0, 0)) for e in more],
            out_specs=[out, out],
            scratch_shapes=[pltpu.VMEM((m, n), F32)]
            + [pltpu.VMEM(x.shape, BF) for x in operands]
            + [pltpu.SemaphoreType.DMA((len(operands),))],
        ),
        out_shape=[shape, shape],
        name="weight_grads",
        cost_estimate=cost(2 * m * rows * n, 2 * rows * (m + n)),
        compiler_params=PARAMS,
    )(me, *operands, *more)


def grad_cols_kernel(me_ref, left_ref, right_ref, out_ref):
    out_ref[0] = mm(left_ref[...], right_ref[...]).astype(BF).T


def grad_cols(me, left, right, count, odd, tile=256):
    m, rows = left.shape
    n = right.shape[1]
    part = n // count
    if part % STEP:
        full = lax.dot_general(right, left, (((0,), (1,)), ((), ())), preferred_element_type=F32).astype(BF)
        return jnp.stack(
            [lax.dynamic_slice_in_dim(full, (me[0] ^ k) * part, part, 0) for k in range(odd, count, 2)]
        )
    tile = min(tile, part)
    inner = part // tile
    return pl.pallas_call(
        grad_cols_kernel,
        grid_spec=pltpu.PrefetchScalarGridSpec(
            num_scalar_prefetch=1,
            grid=(count // 2, inner),
            in_specs=[
                pl.BlockSpec((m, rows), lambda k, t, me: (0, 0), pipeline_mode=pl.Buffered(1)),
                pl.BlockSpec((rows, tile), lambda k, t, me: (0, jnp.bitwise_xor(me[0], 2 * k + odd) * inner + t)),
            ],
            out_specs=pl.BlockSpec((1, tile, m), lambda k, t, me: (k, t, 0)),
        ),
        out_shape=S((count // 2, part, m), BF),
        name="weight_grad",
        cost_estimate=cost(m * rows * n, rows * (2 * m + n)),
        compiler_params=PARAMS,
    )(me, left, right)


def bits_of(axis):
    size = lax.axis_size(axis)
    count = size.bit_length() - 1
    assert size == 1 << count
    return count


def swap(value, axis, mask):
    size = lax.axis_size(axis)
    return lax.ppermute(value, axis, [(i, i ^ mask) for i in range(size)])


def gathering(shard):
    held = {0: shard}
    for bit in reversed(range(bits_of("fsdp"))):
        step = 1 << bit
        sent = yield list(held.values())
        held.update({k ^ step: swap(v, "fsdp", step) for k, v in zip(list(held), sent)})
    return [held[k] for k in range(len(held))]


def reorder(parts, index):
    parts = list(parts)
    for bit in range(len(parts).bit_length() - 1):
        flag = (index >> bit) & 1
        parts = [jnp.where(flag == 1, parts[k ^ (1 << bit)], parts[k]) for k in range(len(parts))]
    return parts


def summing(keep, send, halve):
    (sent,) = yield [send]
    got = swap(sent, "fsdp", 1)
    part = {2 * k: keep[k].astype(F32) + got[k].astype(F32) for k in range(keep.shape[0])}
    for bit in range(1, bits_of("fsdp")):
        step = 1 << bit
        sent = yield [part[k].astype(BF) for k in part if k & step]
        got = {k ^ step: swap(s, "fsdp", step) for k, s in zip([k for k in part if k & step], sent)}
        part = {k: part[k] + got[k].astype(F32) for k in got}
    value = part[0]
    if not halve:
        return value
    side = lax.axis_index("grp") & 1
    size = value.shape[1] // 2
    (sent,) = yield [lax.dynamic_slice_in_dim(value, (1 - side) * size, size, 1).astype(BF)]
    return lax.dynamic_slice_in_dim(value, side * size, size, 1) + swap(sent, "grp", 1).astype(F32)


def completing(values):
    me = lax.axis_index("grp")
    side, line = me & 1, me >> 1
    depth = lax.axis_size("grp") // 2
    value = values[0] if len(values) == 1 else jnp.concatenate(values, axis=1)
    rows = value.shape[0] // depth
    block = lambda k: lax.dynamic_slice_in_dim(value, (line ^ k) * rows, rows, 0)
    sent = yield [block(k).astype(BF) for k in range(1, depth)]
    total = block(0)
    for k, s in zip(range(1, depth), sent):
        total = total + swap(s, "grp", 2 * k).astype(F32)
    (total,) = yield [total.astype(BF)]
    got = [total] + [swap(total, "grp", 2 * k) for k in range(1, depth)]
    (mine,) = yield [jnp.concatenate(reorder(got, line), axis=0)]
    other = swap(mine, "grp", 1)
    results, at = [], 0
    for v in values:
        cols = slice(at, at + v.shape[1])
        at += v.shape[1]
        a, b = mine[:, cols].astype(F32), other[:, cols].astype(F32)
        results.append(jnp.concatenate([jnp.where(side == 0, a, b), jnp.where(side == 0, b, a)], axis=1))
    return results


class Flow:
    def __init__(self, stages):
        self.stages, self.ready, self.result = stages, next(stages), None

    def send(self, operands):
        try:
            self.ready = self.stages.send(operands)
        except StopIteration as done:
            self.ready, self.result = None, done.value


def depart(anchor, flows, after=()):
    flows = [f for f in flows if f.ready is not None]
    operands = [x for f in flows for x in f.ready]
    tied = lax.optimization_barrier((anchor, tuple(operands), tuple(after)))
    operands = list(tied[1])
    for f in flows:
        count = len(f.ready)
        f.send(operands[:count])
        operands = operands[count:]
    return tied[0]


def then_complete(flows):
    return Flow(completing([finish(f) for f in flows]))


def finish(flow):
    while flow.ready is not None:
        flow.send(flow.ready)
    return flow.result


def total_small(value):
    for axis in ("fsdp", "grp"):
        size = lax.axis_size(axis)
        others = [swap(value, axis, k) for k in range(1, size)]
        for other in others:
            value = value + other
    return value


def body(
    layer_input,
    segment_ids,
    bucket_table,
    gain_attn,
    weight_query,
    weight_key,
    weight_value,
    weight_out,
    gain_ffn,
    weight_in,
    weight_back,
    gain_final,
    weight_embed,
    bias_table,
    cotangent,
):
    micro, length, width = layer_input.shape
    heads = bias_table.shape[1]
    size = lax.axis_size("fsdp")
    index = lax.axis_index("fsdp")
    me = index.astype(jnp.int32).reshape(1)
    buckets = bias_table.shape[0] * size
    rows = micro * length
    groups = GROUPS

    part = width // size
    span = width // groups
    small = jnp.concatenate([gain_attn, gain_ffn, gain_final, bias_table.reshape(-1)]).reshape(1, -1)
    small = finish(Flow(gathering(small)))
    small = jnp.concatenate(reorder(small, index), axis=0)
    g_one, g_two, g_three = (
        small[:, k * part : (k + 1) * part].reshape(1, width).astype(F32) for k in range(3)
    )
    table = small[:, 3 * part :].reshape(buckets, heads)

    columns = [
        w[:, g * span : (g + 1) * span] for g in range(groups) for w in (weight_query, weight_key, weight_value)
    ]
    near = Flow(gathering(jnp.concatenate(columns[:3], axis=1)))
    later = Flow(gathering(jnp.concatenate(columns[3:], axis=1)))
    back_rows = weight_back.shape[0] // part
    far = Flow(
        gathering(
            jnp.concatenate(
                [weight_out, weight_in, weight_embed]
                + [weight_back[q * part : (q + 1) * part] for q in range(back_rows)],
                axis=1,
            )
        )
    )
    link = depart(me, [near])
    link = depart(link, [later], [near.ready[-1]])

    onehot = (bucket_table[:, None] == lax.iota(jnp.int32, buckets)[None, :]).astype(BF)
    bias_rows = lax.dot_general(table, onehot, (((0,), (1,)), ((), ())), preferred_element_type=F32)
    strips = bias_strips(bias_rows)
    low, wide = key_ranges(segment_ids)
    seg_col = segment_ids.reshape(rows, 1)
    seg_row = segment_ids.reshape(rows // BQ, 1, BQ)

    x = layer_input.reshape(rows, width)
    upstream = cotangent.reshape(rows, -1)
    qkv, seen = [], []
    near = finish(near)
    turn = depart(link, [far], [later.ready[-1], strips])
    for g in range(groups):
        if g == 0:
            made = project(turn, x, g_one, near, 3 * span, 0, True)
        else:
            made = project(turn, x, g_one, later, 3 * span, (g - 1) * 3 * span, False)
        qkv.append(made)
        start = low
        if g == 0:
            start = depart(low, [later], [made[0]])
            later = finish(later)
        if g == groups - 1:
            start = depart(low, [far], [made[0]])
        seen.append(
            attend(start, wide, made[0], made[1], made[4], strips, seg_col, seg_row, length, heads // groups, g)
        )
        turn = lax.optimization_barrier((me, seen[-1][3]))[0]
    far = finish(far)
    h1_t = qkv[0][5]
    gains = jnp.concatenate([g_two, g_three], axis=0)
    states, dx2, dattn_t, da, h2_t, h3_t, db_t, hidden, dpre = feed_forward(
        turn, x, [s[0] for s in seen], upstream, gains, far
    )

    back_send = grad_cols(me, db_t, hidden, size, 1)
    turn = lax.optimization_barrier((me, back_send))[0]
    back_keep = grad_cols(turn, db_t, hidden, size, 0)
    back = Flow(summing(back_keep, back_send, False))
    turn = depart(turn, [back], [back_keep])
    inner = Flow(summing(*grad_rows(turn, [h2_t], [dpre], size), True))

    def back_of(turn, g):
        q, k, v, kt = qkv[g][:4]
        return attend_back(turn, wide, q, k, kt, v, seen[g][1], dattn_t, seen[g][2], seen[g][3], length, g)

    turn = depart(turn, [back, inner], [inner.ready[0]])
    out = grad_set(turn, [([s[1] for s in seen], [da]), ([h3_t], [upstream])], size)
    turn = depart(low, [inner], [out[0]])
    grads = [back_of(turn, 0)]
    g_back = lax.psum(finish(back).astype(BF), "grp").astype(F32)
    out = Flow(summing(*out, True))
    turn = depart(me, [out], [grads[0][3]])
    first = Flow(summing(*grad_set(turn, [([h1_t], list(grads[0][:3]))], size), True))

    turn = depart(low, [inner, out, first])
    grads.append(back_of(turn, 1))
    turn = depart(me, [out, first], [grads[1][3]])
    inner = then_complete([inner])
    second = Flow(summing(*grad_set(turn, [([h1_t], list(grads[1][:3]))], size), True))
    turn = depart(low, [inner, second])
    grads.append(back_of(turn, 2))

    sums = jnp.concatenate([g[3] for g in grads], axis=0)
    d_table = jnp.dot(sums, onehot.astype(F32), precision=lax.Precision.HIGHEST).T.astype(BF)
    d_table = d_table.reshape(size, buckets // size, heads)
    extra = jnp.stack([lax.dynamic_index_in_dim(d_table, index ^ k, 0, False) for k in range(size)])
    extra = jnp.pad(extra, ((0, 0), (0, part - buckets // size), (0, STEP - heads)))
    turn = depart(me, [inner, first, second], [grads[2][3]])
    third = Flow(summing(*grad_set(turn, [([h1_t], list(grads[2][:3]))], size, extra), True))

    pieces, spans = [], []
    for g in range(groups):
        pieces += near if g == 0 else later
        spans.append(slice(0, 3 * span) if g == 0 else slice((g - 1) * 3 * span, g * 3 * span))
    dparts = [p for g in grads for p in g[:3]]
    blocks = rows // 256
    cuts = (blocks - 2 * (blocks // 3), blocks // 3, blocks // 3)
    turn = depart(me, [third, second], [third.ready[0]])
    d_input = input_back(turn, x, dx2, g_one, dparts, pieces, spans, 0, cuts[0], None)
    middle = then_complete([out, first, second])
    turn = depart(me, [inner, third, middle], [d_input])
    d_input = input_back(turn, x, dx2, g_one, dparts, pieces, spans, cuts[0], cuts[1], d_input)
    turn = depart(me, [third, middle], [d_input])
    d_input = input_back(turn, x, dx2, g_one, dparts, pieces, spans, cuts[0] + cuts[1], cuts[2], d_input)
    third = then_complete([third])
    depart(me, [third, middle], [d_input])
    (g_in,) = finish(inner)
    g_oe, *proj = finish(middle) + finish(third)
    g_out, g_embed = g_oe[:, :width], g_oe[:, width:]
    grad_q, grad_k, grad_v = (
        jnp.concatenate([p[:, k * span : (k + 1) * span] for p in proj], axis=1) for k in range(3)
    )
    g_table = proj[-1][: buckets // size, width : width + heads]

    def gain_grad(gain, *pairs):
        return sum(jnp.sum(w.astype(F32) * g, axis=1) for w, g in pairs) / gain.astype(F32)

    gain_grads = (
        gain_grad(gain_attn, (weight_query, grad_q), (weight_key, grad_k), (weight_value, grad_v)),
        gain_grad(gain_ffn, (weight_in, g_in)),
        gain_grad(gain_final, (weight_embed, g_embed)),
    )
    return (
        states.reshape(micro, length, -1),
        d_input.reshape(micro, length, width),
        gain_grads[0],
        grad_q,
        grad_k,
        grad_v,
        g_out,
        gain_grads[1],
        g_in,
        g_back,
        gain_grads[2],
        g_embed,
        g_table,
    )


GROUPS = 3


def solution(mesh):
    placed = (
        P(None, ("grp", "fsdp"), None),
        P(None, ("grp", "fsdp")),
        P(),
        P("fsdp"),
        P("fsdp", None),
        P("fsdp", None),
        P("fsdp", None),
        P("fsdp", None),
        P("fsdp"),
        P("fsdp", None),
        P("fsdp", None),
        P("fsdp"),
        P("fsdp", None),
        P("fsdp", None),
        P(None, ("grp", "fsdp"), None),
    )
    return jax.shard_map(
        body,
        mesh=mesh,
        in_specs=placed,
        out_specs=(
            P(None, ("grp", "fsdp"), None),
            P(None, ("grp", "fsdp"), None),
            P("fsdp"),
            P("fsdp", None),
            P("fsdp", None),
            P("fsdp", None),
            P("fsdp", None),
            P("fsdp"),
            P("fsdp", None),
            P("fsdp", None),
            P("fsdp"),
            P("fsdp", None),
            P("fsdp", None),
        ),
        check_vma=False,
    )
```

```python
import functools
import jax
import jax.numpy as jnp
from jax import lax
from jax.experimental import pallas as pl
from jax.experimental.pallas import tpu as pltpu
from jax.sharding import PartitionSpec as P

BQ = 256
STEP = 128
NEGATIVE = -1e30
VMEM_CAP = 60 * 1024 * 1024
EPS = 1e-06
INV_ROOT_TWO_PI = 0.3989422804014327
BF = jnp.bfloat16
F32 = jnp.float32
NT = (((1,), (1,)), ((), ()))
NN = (((1,), (0,)), ((), ()))
S = jax.ShapeDtypeStruct
ANY = pl.BlockSpec(memory_space=pl.ANY)
PARAMS = pltpu.CompilerParams(vmem_limit_bytes=VMEM_CAP)


def cost(flops, moved, special=0):
    return pl.CostEstimate(flops=flops, bytes_accessed=moved, transcendentals=special)


def mm(a, b, dims=NN):
    return lax.dot_general(a, b, dims, preferred_element_type=F32)


def norm_scale(value):
    return lax.rsqrt(jnp.mean(value * value, axis=-1, keepdims=True) + EPS)


def norm_back(grad, value, scale, gain):
    weighted = grad * gain
    inner = jnp.mean(weighted * value, axis=-1, keepdims=True)
    dvalue = scale * weighted - value * (scale * scale * scale) * inner
    return dvalue


def gelu_parts(value):
    t = 1.0 / (1.0 + (0.3275911 * 0.7071067811865476) * jnp.abs(value))
    poly = 0.5307027145
    for factor in (-0.7265760135, 0.7107068705, -0.142248368, 0.127414796):
        poly = poly * t + factor
    bell = jnp.exp(-0.5 * value * value)
    tail = poly * t * bell
    cdf = jnp.where(value < 0.0, tail, 1.0 - tail)
    return value * cdf, cdf + value * bell * INV_ROOT_TWO_PI


def run_copies(jobs, sems):
    copies = [pltpu.make_async_copy(a, b, sems.at[i]) for i, (a, b) in enumerate(jobs)]
    for copy in copies:
        copy.start()
    for copy in copies:
        copy.wait()


def place(me, k, rows):
    return pl.multiple_of(jnp.bitwise_xor(me, k) * rows, 16)


def placing(me, pieces, target, lanes=slice(None)):
    rows = pieces[0].shape[0]
    return [
        (piece.at[:, lanes], target.at[pl.ds(place(me, k, rows), rows), :]) for k, piece in enumerate(pieces)
    ]


def project_kernel(me_ref, x_ref, gain_ref, *refs, count, groups):
    pieces, refs = refs[:count], refs[count:]
    q_ref, k_ref, v_ref, kt_ref, vt_ref, ht_ref, weight_ref, sems = refs

    @pl.when(pl.program_id(0) == 0)
    def _():
        run_copies(placing(me_ref[0], pieces, weight_ref), sems)

    value = x_ref[...].astype(F32)
    h = (value * norm_scale(value) * gain_ref[...]).astype(BF)
    ht_ref[...] = h.T
    part = h.shape[1] // groups
    for g in range(groups):
        cols = slice(g * part, (g + 1) * part)
        out = mm(h, weight_ref[:, 3 * g * part : 3 * (g + 1) * part]).astype(BF)
        q_ref[:, cols] = out[:, :part]
        k_ref[:, cols] = out[:, part : 2 * part]
        kt_ref[cols, :] = out[:, part : 2 * part].T
        v_ref[:, cols] = out[:, 2 * part :]
        vt_ref[cols, :] = out[:, 2 * part :].T


def project(me, x, gain, pieces, groups, block=256):
    rows, width = x.shape
    natural = pl.BlockSpec((block, width), lambda i, *_: (i, 0))
    turned = pl.BlockSpec((width, block), lambda i, *_: (0, i))
    return pl.pallas_call(
        functools.partial(project_kernel, count=len(pieces), groups=groups),
        grid_spec=pltpu.PrefetchScalarGridSpec(
            num_scalar_prefetch=1,
            grid=(rows // block,),
            in_specs=[natural, pl.BlockSpec((1, width), lambda i, *_: (0, 0))] + [ANY] * len(pieces),
            out_specs=[natural] * 3 + [turned] * 3,
            scratch_shapes=[pltpu.VMEM((width, 3 * width), BF), pltpu.SemaphoreType.DMA((len(pieces),))],
        ),
        out_shape=[S((rows, width), BF)] * 3 + [S((width, rows), BF)] * 3,
        name="project",
        cost_estimate=cost(6 * rows * width * width, 14 * rows * width),
        compiler_params=PARAMS,
    )(me, x, gain, *pieces)


def strip_kernel(rows_ref, strip_ref, *, length):
    rows = jnp.broadcast_to(rows_ref[0], (STEP, 2 * length))
    turned = pltpu.roll(rows, 2 * length - STEP, 1, stride=1, stride_axis=0)
    strip_ref[0] = turned[:, : 2 * length - STEP].T.astype(BF)


def bias_strips(rows):
    heads, twice = rows.shape
    return pl.pallas_call(
        functools.partial(strip_kernel, length=twice // 2),
        grid=(heads,),
        in_specs=[pl.BlockSpec((1, 1, twice), lambda h: (h, 0, 0))],
        out_specs=pl.BlockSpec((1, twice - STEP, STEP), lambda h: (h, 0, 0)),
        out_shape=S((heads, twice - STEP, STEP), BF),
        name="bias_strips",
        cost_estimate=cost(heads * twice * STEP * 20, heads * twice * STEP * 4),
        compiler_params=PARAMS,
    )(rows.reshape(heads, 1, twice))


def by_width(low_ref, width_ref, length, work):
    step = pl.program_id(0) * pl.num_programs(1) + pl.program_id(1)
    low = pl.multiple_of(low_ref[step], STEP)
    width = width_ref[step]
    for blocks in range(BQ // STEP, length // STEP + 1):

        @pl.when(width == blocks)
        def _(blocks=blocks):
            work(low, blocks * STEP)


def half_of(query, side, feat):
    left = lax.broadcasted_iota(jnp.int32, query.shape, 1) < feat
    return jnp.where(left if side == 0 else ~left, query, jnp.zeros_like(query))


def fold(value, combine):
    parts = [value[i : i + 8] for i in range(0, value.shape[0], 8)]
    while len(parts) > 1:
        parts = [combine(*parts[i : i + 2]) if i + 1 < len(parts) else parts[i] for i in range(0, len(parts), 2)]
    return parts[0]


def attend_kernel(
    low_ref, width_ref, q_ref, k_ref, vt_ref, strip_ref, sk_ref, sq_ref,
    attn_ref, attnt_ref, prob_ref, inv_ref, mask_ref, *score_refs, heads, feat, length, group,
):
    start = pl.program_id(1) * BQ
    row = 64

    def work(low, width):
        keys = pl.ds(low, width)
        mask_ref[:width] = jnp.where(sk_ref[keys, :] == sq_ref[0], 0.0, NEGATIVE).astype(BF)
        bases = [low - start + length - (j + 1) * STEP for j in range(BQ // STEP)]

        def one_group(g, carry):
            outs = []

            def lanes_of(head):
                return pl.ds(pl.multiple_of((g * group + head // 2 * 2) * feat, 2 * feat), 2 * feat)

            def score(head):
                lanes = lanes_of(head)
                score_refs[head % len(score_refs)][:width] = mm(
                    k_ref[keys, lanes], half_of(q_ref[:, lanes], head % 2, feat), NT
                )

            def weigh(head):
                ref = score_refs[head % len(score_refs)]
                whole = g * group + head
                top = None
                for at in range(0, width, row):
                    bias = jnp.concatenate(
                        [strip_ref[whole, pl.ds(pl.multiple_of(base + at, row), row), :] for base in bases], axis=1
                    )
                    value = ref[at : at + row] + (bias + mask_ref[at : at + row]).astype(F32)
                    ref[at : at + row] = value
                    value = fold(value, jnp.maximum)
                    top = value if top is None else jnp.maximum(top, value)
                top = jnp.max(top, axis=0, keepdims=True)
                total = None
                for at in range(0, width, row):
                    expo = jnp.exp(ref[at : at + row] - top)
                    prob_ref[0, 0, whole, pl.ds(pl.multiple_of(low + at, row), row), :] = expo.astype(BF)
                    expo = fold(expo, jnp.add)
                    total = expo if total is None else total + expo
                inverse = 1.0 / jnp.sum(total, axis=0, keepdims=True)
                inv_ref[g, head : head + 1, :] = inverse
                return inverse

            def gather(head, inverse):
                whole = g * group + head
                value = vt_ref[pl.ds(pl.multiple_of(whole * feat, feat), feat), keys]
                outs.append(mm(value, prob_ref[0, 0, whole, keys, :]) * inverse)
                if head % 2:
                    lanes = lanes_of(head)
                    both = jnp.concatenate(outs[-2:], axis=0)
                    attnt_ref[lanes, :] = both.astype(BF)
                    attn_ref[:, lanes] = both.T.astype(BF)

            score(0)
            last = None
            for head in range(group):
                if head + 1 < group:
                    score(head + 1)
                inverse = weigh(head)
                if last is not None:
                    gather(*last)
                last = (head, inverse)
            gather(*last)
            return carry

        lax.fori_loop(0, heads // group, one_group, 0)

    by_width(low_ref, width_ref, length, work)


def attend(low, width, q, k, vt, strips, sk, sq, length, groups):
    rows, part = q.shape
    heads = strips.shape[0]
    feat = part // heads
    seqs, blocks = rows // length, length // BQ
    at = lambda s, b, *_: (s * blocks + b, 0)
    whole = lambda s, b, *_: (s, 0)
    at_t = lambda s, b, *_: (0, s * blocks + b)
    return pl.pallas_call(
        functools.partial(attend_kernel, heads=heads, feat=feat, length=length, group=heads // groups),
        grid_spec=pltpu.PrefetchScalarGridSpec(
            num_scalar_prefetch=2,
            grid=(seqs, blocks),
            in_specs=[
                pl.BlockSpec((BQ, part), at),
                pl.BlockSpec((length, part), whole),
                pl.BlockSpec((part, length), lambda s, b, *_: (0, s)),
                pl.BlockSpec(strips.shape, lambda s, b, *_: (0, 0, 0), pipeline_mode=pl.Buffered(1)),
                pl.BlockSpec((length, 1), whole),
                pl.BlockSpec((1, 1, BQ), lambda s, b, *_: (s * blocks + b, 0, 0)),
            ],
            out_specs=[
                pl.BlockSpec((BQ, part), at),
                pl.BlockSpec((part, BQ), at_t),
                pl.BlockSpec((1, 1, heads, length, BQ), lambda s, b, *_: (s, b, 0, 0, 0)),
                pl.BlockSpec((groups, heads // groups, BQ), lambda s, b, *_: (0, 0, s * blocks + b)),
            ],
            scratch_shapes=[pltpu.VMEM((length, BQ), BF)] + [pltpu.VMEM((length, BQ), F32)] * 2,
        ),
        out_shape=[
            S((rows, part), BF),
            S((part, rows), BF),
            S((seqs, blocks, heads, length, BQ), BF),
            S((groups, heads // groups, rows), F32),
        ],
        name="attend",
        cost_estimate=cost(16 * rows * length * part, 2 * rows * heads * length, rows * heads * length),
        compiler_params=PARAMS,
    )(low, width, q, k, vt, strips, sk, sq)


def unskew(data):
    data = jnp.concatenate([data, jnp.zeros((STEP, STEP), F32)], axis=0)
    rows = lax.broadcasted_iota(jnp.int32, (STEP, STEP), 0)
    cols = lax.broadcasted_iota(jnp.int32, (STEP, STEP), 1)
    flip = (rows + cols == STEP - 1).astype(BF)
    high = data.astype(BF)
    low = (data - high.astype(F32)).astype(BF)
    turned = (mm(high, flip) + mm(low, flip)).T
    return jnp.sum(pltpu.roll(turned, 1, 1, stride=1, stride_axis=0), axis=0, keepdims=True)


def attend_back_kernel(
    low_ref, width_ref, q_ref, k_ref, kt_ref, v_ref, attnt_ref, dot_ref, prob_ref, inv_ref,
    dq_ref, dk_ref, dv_ref, sum_ref, diag_ref, dka_ref, dva_ref, *work_refs, heads, feat, length,
):
    seq, block = pl.program_id(0), pl.program_id(1)
    start = block * BQ
    row = 64
    many = len(work_refs) // 2
    dprob_refs, ds_refs = work_refs[:many], work_refs[many:]

    @pl.when(jnp.logical_and(seq == 0, block == 0))
    def _():
        diag_ref[...] = jnp.zeros_like(diag_ref)

    @pl.when(block == 0)
    def _():
        dka_ref[...] = jnp.zeros_like(dka_ref)
        dva_ref[...] = jnp.zeros_like(dva_ref)

    def work(low, width):
        keys = pl.ds(low, width)
        bases = [low - start + length - (j + 1) * STEP for j in range(BQ // STEP)]
        dvals, dqs, dkeys = [], [], []

        def begin(head):
            lanes = slice(head // 2 * 2 * feat, (head // 2 + 1) * 2 * feat)
            feats = slice(head * feat, (head + 1) * feat)
            scaled = dot_ref[feats, :].astype(F32) * inv_ref[0, head : head + 1, :]
            delta = jnp.sum(scaled * attnt_ref[feats, :].astype(F32), axis=0, keepdims=True)
            scaled = scaled.astype(BF)
            blank = jnp.zeros_like(scaled)
            padded = jnp.concatenate([blank, scaled] if head % 2 else [scaled, blank], axis=0)
            dprob_refs[head % many][:width] = mm(v_ref[keys, lanes], padded)
            dvals.append(mm(prob_ref[0, 0, head, keys, :], padded, NT))
            if head % 2:
                dva_ref[keys, lanes] += dvals[-2] + dvals[-1]
            return delta

        def middle(head, delta):
            dprob, ds = dprob_refs[head % many], ds_refs[head % many]
            for at in range(0, width, row):
                prob = prob_ref[0, 0, head, pl.ds(pl.multiple_of(low + at, row), row), :]
                value = prob.astype(F32) * (dprob[at : at + row] - delta)
                ds[at : at + row] = value.astype(BF)
                for j, base in enumerate(bases):
                    diag_ref[head, pl.ds(pl.multiple_of(base + at, row), row), :] += value[:, j * STEP : (j + 1) * STEP]

        def end(head):
            lanes = slice(head // 2 * 2 * feat, (head // 2 + 1) * 2 * feat)
            ds = ds_refs[head % many]
            dkey = mm(ds[:width], half_of(q_ref[:, lanes], head % 2, feat))
            dkeys.append(dkey)
            dqs.append(mm(kt_ref[head * feat : (head + 1) * feat, keys], ds[:width]))
            if head % 2:
                dka_ref[keys, lanes] += dkeys[-2] + dkeys[-1]
                dq_ref[:, lanes] = jnp.concatenate(dqs[-2:], axis=0).T.astype(BF)

        delta = begin(0)
        for head in range(heads):
            following = begin(head + 1) if head + 1 < heads else None
            middle(head, delta)
            if head:
                end(head - 1)
            delta = following
        end(heads - 1)

    by_width(low_ref, width_ref, length, work)

    @pl.when(block == pl.num_programs(1) - 1)
    def _():
        dk_ref[...] = dka_ref[...].astype(BF)
        dv_ref[...] = dva_ref[...].astype(BF)

    @pl.when(jnp.logical_and(seq == pl.num_programs(0) - 1, block == pl.num_programs(1) - 1))
    def _():
        for head in range(heads):
            sum_ref[head : head + 1, :] = unskew(diag_ref[head])


def attend_back(low, width, q, k, kt, v, attnt, dot, prob, inv, length, group):
    rows = q.shape[0]
    part = q.shape[1] // inv.shape[0]
    heads = inv.shape[1]
    feat = part // heads
    seqs, blocks = rows // length, length // BQ
    at = lambda s, b, *_: (s * blocks + b, group)
    whole = lambda s, b, *_: (s, group)
    at_t = lambda s, b, *_: (group, s * blocks + b)
    out = lambda s, b, *_: (s, 0)
    return pl.pallas_call(
        functools.partial(attend_back_kernel, heads=heads, feat=feat, length=length),
        grid_spec=pltpu.PrefetchScalarGridSpec(
            num_scalar_prefetch=2,
            grid=(seqs, blocks),
            in_specs=[
                pl.BlockSpec((BQ, part), at),
                pl.BlockSpec((length, part), whole),
                pl.BlockSpec((part, length), lambda s, b, *_: (group, s)),
                pl.BlockSpec((length, part), whole),
                pl.BlockSpec((part, BQ), at_t),
                pl.BlockSpec((part, BQ), at_t),
                pl.BlockSpec((1, 1, heads, length, BQ), lambda s, b, *_: (s, b, group, 0, 0)),
                pl.BlockSpec((1, heads, BQ), lambda s, b, *_: (group, 0, s * blocks + b)),
            ],
            out_specs=[
                pl.BlockSpec((BQ, part), lambda s, b, *_: (s * blocks + b, 0)),
                pl.BlockSpec((length, part), out),
                pl.BlockSpec((length, part), out),
                pl.BlockSpec((heads, 2 * length), lambda s, b, *_: (0, 0)),
            ],
            scratch_shapes=[
                pltpu.VMEM((heads, 2 * length - STEP, STEP), F32),
                pltpu.VMEM((length, part), F32),
                pltpu.VMEM((length, part), F32),
            ]
            + [pltpu.VMEM((length, BQ), F32)] * 2
            + [pltpu.VMEM((length, BQ), BF)] * 2,
        ),
        out_shape=[S((rows, part), BF)] * 3 + [S((heads, 2 * length), F32)],
        name="attend_back",
        cost_estimate=cost(32 * rows * length * part, 2 * rows * heads * length),
        compiler_params=PARAMS,
    )(low, width, q, k, kt, v, attnt, dot, prob, inv)


def key_ranges(seg):
    firsts, lasts = seg[:, ::BQ], seg[:, BQ - 1 :: BQ]
    low = jnp.sum((seg[:, None, :] < firsts[:, :, None]).astype(jnp.int32), axis=-1)
    high = jnp.sum((seg[:, None, :] <= lasts[:, :, None]).astype(jnp.int32), axis=-1)
    low = low // STEP
    width = (high + STEP - 1) // STEP - low
    return (low * STEP).reshape(-1), width.reshape(-1)


def ffn_kernel(me_ref, x_ref, up_ref, gain_ref, *refs, chunk, count, groups):
    attns, refs = refs[:groups], refs[groups:]
    pieces, refs = refs[:count], refs[count:]
    (states_ref, dx2_ref, dot_ref, da_ref, h2t_ref, h3t_ref, dbt_ref, hid_ref, dpre_ref,
     slope_ref, wo_ref, wi_ref, wb_ref, we_ref, sems) = refs
    width, wide = wi_ref.shape
    embed = we_ref.shape[1]

    @pl.when(pl.program_id(0) == 0)
    def _():
        me, rows = me_ref[0], pieces[0].shape[0]
        copies = placing(me, pieces, wo_ref, slice(0, width))
        copies += placing(me, pieces, wi_ref, slice(width, width + wide))
        copies += placing(me, pieces, we_ref, slice(width + wide, width + wide + embed))
        parts = wide // width
        for k, piece in enumerate(pieces):
            for q in range(parts):
                at = width + wide + embed + q * width
                spot = pl.ds(place(me, k, parts * rows) + q * rows, rows)
                copies.append((piece.at[:, at : at + width], wb_ref.at[spot, :]))
        run_copies(copies, sems)

    g_two, g_three = gain_ref[0:1, :], gain_ref[1:2, :]
    attn = jnp.concatenate([a[...] for a in attns], axis=1)
    x2 = x_ref[...].astype(F32) + mm(attn, wo_ref[...])
    scale2 = norm_scale(x2)
    h2 = (x2 * scale2 * g_two).astype(BF)
    x3 = x2
    for at in range(0, wide, chunk):
        cols = slice(at, at + chunk)
        hidden, slope = gelu_parts(mm(h2, wi_ref[:, cols]))
        hidden = hidden.astype(BF)
        hid_ref[:, cols] = hidden
        slope_ref[:, cols] = slope.astype(BF)
        x3 = x3 + mm(hidden, wb_ref[cols, :])
    scale3 = norm_scale(x3)
    h3 = (x3 * scale3 * g_three).astype(BF)
    states_ref[...] = mm(h3, we_ref[...])
    dx3 = norm_back(mm(up_ref[...], we_ref[...], NT), x3, scale3, g_three)
    db = dx3.astype(BF)
    dh2 = None
    for at in range(0, wide, chunk):
        cols = slice(at, at + chunk)
        dpre = (mm(db, wb_ref[cols, :], NT) * slope_ref[:, cols].astype(F32)).astype(BF)
        dpre_ref[:, cols] = dpre
        part = mm(dpre, wi_ref[:, cols], NT)
        dh2 = part if dh2 is None else dh2 + part
    part = norm_back(dh2, x2, scale2, g_two)
    dx2 = dx3 + part
    da = dx2.astype(BF)
    dx2_ref[...] = dx2
    da_ref[...] = da
    dot_ref[...] = mm(wo_ref[...], da, NT).astype(BF)
    h2t_ref[...] = h2.T
    h3t_ref[...] = h3.T
    dbt_ref[...] = db.T


def feed_forward(me, x, attns, up, gains, pieces, block=256, chunk=768):
    rows, width = x.shape
    count = len(pieces)
    embed = up.shape[1]
    wide = (pieces[0].shape[1] - width - embed) // 2
    fixed = lambda i, *_: (0, 0)
    natural = lambda cols: pl.BlockSpec((block, cols), lambda i, *_: (i, 0))
    turned = pl.BlockSpec((width, block), lambda i, *_: (0, i))
    return pl.pallas_call(
        functools.partial(ffn_kernel, chunk=chunk, count=count, groups=len(attns)),
        grid_spec=pltpu.PrefetchScalarGridSpec(
            num_scalar_prefetch=1,
            grid=(rows // block,),
            in_specs=[natural(width), natural(embed), pl.BlockSpec(gains.shape, fixed)]
            + [natural(a.shape[1]) for a in attns]
            + [ANY] * len(pieces),
            out_specs=[
                natural(embed), natural(width), turned, natural(width), turned, turned, turned,
                natural(wide), natural(wide),
            ],
            scratch_shapes=[
                pltpu.VMEM((block, wide), BF),
                pltpu.VMEM((width, width), BF),
                pltpu.VMEM((width, wide), BF),
                pltpu.VMEM((wide, width), BF),
                pltpu.VMEM((width, embed), BF),
                pltpu.SemaphoreType.DMA((count * (3 + wide // width),)),
            ],
        ),
        out_shape=[
            S((rows, embed), F32), S((rows, width), F32), S((width, rows), BF), S((rows, width), BF),
            S((width, rows), BF), S((width, rows), BF), S((width, rows), BF),
            S((rows, wide), BF), S((rows, wide), BF),
        ],
        name="feed_forward",
        cost_estimate=cost(4 * rows * width * (4 * wide + 2 * width), 20 * rows * wide, 2 * rows * wide),
        compiler_params=PARAMS,
    )(me, x, up, gains, *attns, *pieces)


def input_back_kernel(me_ref, x_ref, dx2_ref, gain_ref, *refs, spans, count, threaded):
    groups = len(spans)
    parts, refs = refs[: 3 * groups], refs[3 * groups :]
    pieces, refs = refs[: groups * count], refs[groups * count + threaded :]
    out_ref, weight_ref, sems = refs

    @pl.when(pl.program_id(0) == 0)
    def _():
        copies = []
        for g, lanes in enumerate(spans):
            copies += placing(me_ref[0], pieces[g * count : (g + 1) * count], weight_ref.at[g], lanes)
        run_copies(copies, sems)

    value = x_ref[...].astype(F32)
    scale = norm_scale(value)
    dh = None
    for g in range(groups):
        term = mm(jnp.concatenate([p[...] for p in parts[3 * g : 3 * g + 3]], axis=1), weight_ref[g], NT)
        dh = term if dh is None else dh + term
    out_ref[...] = dx2_ref[...] + norm_back(dh, value, scale, gain_ref[...])


def input_back(me, x, dx2, gain, parts, pieces, spans, first, steps, held, block=256):
    rows, width = x.shape
    natural = lambda cols: pl.BlockSpec((block, cols), lambda i, *_: (i + first, 0))
    fixed = lambda i, *_: (0, 0)
    operands = [me, x, dx2, gain, *parts, *pieces] + ([] if held is None else [held])
    return pl.pallas_call(
        functools.partial(
            input_back_kernel, spans=spans, count=len(pieces) // len(spans), threaded=0 if held is None else 1
        ),
        grid_spec=pltpu.PrefetchScalarGridSpec(
            num_scalar_prefetch=1,
            grid=(steps,),
            in_specs=[natural(width), natural(width), pl.BlockSpec((1, width), fixed)]
            + [natural(p.shape[1]) for p in parts]
            + [ANY] * (len(pieces) + (held is not None)),
            out_specs=natural(width),
            scratch_shapes=[
                pltpu.VMEM((len(spans), width, 3 * parts[0].shape[1]), BF),
                pltpu.SemaphoreType.DMA((len(pieces),)),
            ],
        ),
        out_shape=S((rows, width), F32),
        input_output_aliases={} if held is None else {len(operands) - 1: 0},
        name="input_back",
        cost_estimate=cost(6 * steps * block * width * width, 16 * steps * block * width),
        compiler_params=PARAMS,
    )(*operands)


def grad_rows_kernel(me_ref, *refs, count, lefts):
    lefts, rights, (keep_ref, send_ref, full_ref) = refs[:lefts], refs[lefts:-3], refs[-3:]
    rows = full_ref.shape[0] // count
    down = 0
    for left in lefts:
        at = 0
        for right in rights:
            cols = slice(at, at + right.shape[1])
            at += right.shape[1]
            full_ref[down : down + left.shape[0], cols] = mm(left[...], right[...])
        down += left.shape[0]
    for k in range(count):
        spot = pl.ds(pl.multiple_of(jnp.bitwise_xor(me_ref[0], k) * rows, 16), rows)
        (send_ref if k & 1 else keep_ref)[k >> 1] = full_ref[spot, :].astype(BF)


def grad_rows(me, lefts, rights, count, tile=768, first=0, tiles=None):
    m, rows = sum(left.shape[0] for left in lefts), lefts[0].shape[1]
    if len(rights) > 1:
        tile, tiles = sum(r.shape[1] for r in rights), 1
        specs = [pl.BlockSpec(r.shape, lambda j, *_: (0, 0)) for r in rights]
    else:
        tile = min(tile, rights[0].shape[1])
        tiles = rights[0].shape[1] // tile if tiles is None else tiles
        specs = [pl.BlockSpec((rows, tile), lambda j, *_: (0, j + first))]
    out = pl.BlockSpec((count // 2, m // count, tile), lambda j, *_: (0, 0, j))
    shape = S((count // 2, m // count, tile * tiles), BF)
    return pl.pallas_call(
        functools.partial(grad_rows_kernel, count=count, lefts=len(lefts)),
        grid_spec=pltpu.PrefetchScalarGridSpec(
            num_scalar_prefetch=1,
            grid=(tiles,),
            in_specs=[pl.BlockSpec(left.shape, lambda j, *_: (0, 0), pipeline_mode=pl.Buffered(1)) for left in lefts]
            + specs,
            out_specs=[out, out],
            scratch_shapes=[pltpu.VMEM((m, tile), F32)],
        ),
        out_shape=[shape, shape],
        name="weight_grad",
        cost_estimate=cost(2 * m * rows * tile * tiles, 2 * rows * (m + tile * tiles)),
        compiler_params=PARAMS,
    )(me, *lefts, *rights)


def grad_set_kernel(me_ref, *refs, shapes, count, extra):
    operands = sum(a + b for a, b in shapes)
    sources, refs = refs[:operands], refs[operands:]
    if extra:
        extra_ref, refs = refs[0], refs[1:]
    keep_ref, send_ref, full_ref = refs[:3]
    held, sems = refs[3:-1], refs[-1]
    copies = [pltpu.make_async_copy(a, b, sems.at[i]) for i, (a, b) in enumerate(zip(sources, held))]
    for copy in copies:
        copy.start()
    rows = full_ref.shape[0] // count
    index = at = 0
    for lefts, rights in shapes:
        left = held[index : index + lefts]
        right = held[index + lefts : index + lefts + rights]
        for copy in copies[index : index + lefts]:
            copy.wait()
        for n, r in enumerate(right):
            copies[index + lefts + n].wait()
            down = 0
            for part in left:
                full_ref[down : down + part.shape[0], at : at + r.shape[1]] = mm(part[...], r[...])
                down += part.shape[0]
            at += r.shape[1]
        index += lefts + rights
    for k in range(count):
        target = send_ref if k & 1 else keep_ref
        target[k >> 1, :, :at] = full_ref[pl.ds(place(me_ref[0], k, rows), rows), :].astype(BF)
        if extra:
            target[k >> 1, :, at:] = extra_ref[k]


def grad_set(me, jobs, count, extra=None):
    operands = [x for lefts, rights in jobs for x in lefts + rights]
    m, rows = sum(x.shape[0] for x in jobs[0][0]), jobs[0][0][0].shape[1]
    n = sum(r.shape[1] for _, rights in jobs for r in rights)
    wide = n + (0 if extra is None else extra.shape[2])
    shape = S((count // 2, m // count, wide), BF)
    out = pl.BlockSpec(shape.shape, lambda j, *_: (0, 0, 0))
    more = [] if extra is None else [extra]
    return pl.pallas_call(
        functools.partial(
            grad_set_kernel,
            shapes=tuple((len(a), len(b)) for a, b in jobs),
            count=count,
            extra=extra is not None,
        ),
        grid_spec=pltpu.PrefetchScalarGridSpec(
            num_scalar_prefetch=1,
            grid=(1,),
            in_specs=[ANY] * len(operands) + [pl.BlockSpec(e.shape, lambda j, *_: (0, 0, 0)) for e in more],
            out_specs=[out, out],
            scratch_shapes=[pltpu.VMEM((m, n), F32)]
            + [pltpu.VMEM(x.shape, BF) for x in operands]
            + [pltpu.SemaphoreType.DMA((len(operands),))],
        ),
        out_shape=[shape, shape],
        name="weight_grads",
        cost_estimate=cost(2 * m * rows * n, 2 * rows * (m + n)),
        compiler_params=PARAMS,
    )(me, *operands, *more)


def grad_cols_kernel(me_ref, left_ref, right_ref, out_ref):
    out_ref[0] = mm(left_ref[...], right_ref[...]).astype(BF).T


def grad_cols(me, left, right, count, odd, tile=256):
    m, rows = left.shape
    n = right.shape[1]
    part = n // count
    if part % STEP:
        full = lax.dot_general(right, left, (((0,), (1,)), ((), ())), preferred_element_type=F32).astype(BF)
        return jnp.stack(
            [lax.dynamic_slice_in_dim(full, (me[0] ^ k) * part, part, 0) for k in range(odd, count, 2)]
        )
    tile = min(tile, part)
    inner = part // tile
    return pl.pallas_call(
        grad_cols_kernel,
        grid_spec=pltpu.PrefetchScalarGridSpec(
            num_scalar_prefetch=1,
            grid=(count // 2, inner),
            in_specs=[
                pl.BlockSpec((m, rows), lambda k, t, me: (0, 0), pipeline_mode=pl.Buffered(1)),
                pl.BlockSpec((rows, tile), lambda k, t, me: (0, jnp.bitwise_xor(me[0], 2 * k + odd) * inner + t)),
            ],
            out_specs=pl.BlockSpec((1, tile, m), lambda k, t, me: (k, t, 0)),
        ),
        out_shape=S((count // 2, part, m), BF),
        name="weight_grad",
        cost_estimate=cost(m * rows * n, rows * (2 * m + n)),
        compiler_params=PARAMS,
    )(me, left, right)


def bits_of(axis):
    size = lax.axis_size(axis)
    count = size.bit_length() - 1
    assert size == 1 << count
    return count


def swap(value, axis, mask):
    size = lax.axis_size(axis)
    return lax.ppermute(value, axis, [(i, i ^ mask) for i in range(size)])


def gathering(shard):
    held = {0: shard}
    for bit in reversed(range(1, bits_of("fsdp"))):
        step = 1 << bit
        sent = yield list(held.values())
        held.update({k ^ step: swap(v, "fsdp", step) for k, v in zip(list(held), sent)})
    (own,) = yield [shard]
    others = [k for k in held if k]
    first = swap(own, "fsdp", 1)
    sent = yield [held[k] for k in others]
    held.update({k ^ 1: swap(v, "fsdp", 1) for k, v in zip(others, sent)})
    held[1] = first
    return [held[k] for k in range(len(held))]


def reorder(parts, index):
    parts = list(parts)
    for bit in range(len(parts).bit_length() - 1):
        flag = (index >> bit) & 1
        parts = [jnp.where(flag == 1, parts[k ^ (1 << bit)], parts[k]) for k in range(len(parts))]
    return parts


def summing(keep, send, halve):
    (sent,) = yield [send]
    got = swap(sent, "fsdp", 1)
    part = {2 * k: keep[k].astype(F32) + got[k].astype(F32) for k in range(keep.shape[0])}
    for bit in range(1, bits_of("fsdp")):
        step = 1 << bit
        sent = yield [part[k].astype(BF) for k in part if k & step]
        got = {k ^ step: swap(s, "fsdp", step) for k, s in zip([k for k in part if k & step], sent)}
        if not halve and len(got) == 1:
            (got[0],) = yield [got[0]]
        part = {k: part[k] + got[k].astype(F32) for k in got}
    value = part[0]
    if not halve:
        return value
    side = lax.axis_index("grp") & 1
    size = value.shape[1] // 2
    (sent,) = yield [lax.dynamic_slice_in_dim(value, (1 - side) * size, size, 1).astype(BF)]
    return lax.dynamic_slice_in_dim(value, side * size, size, 1) + swap(sent, "grp", 1).astype(F32)


def completing(values):
    me = lax.axis_index("grp")
    side, line = me & 1, me >> 1
    depth = lax.axis_size("grp") // 2
    value = values[0] if len(values) == 1 else jnp.concatenate(values, axis=1)
    rows = value.shape[0] // depth
    block = lambda k: lax.dynamic_slice_in_dim(value, (line ^ k) * rows, rows, 0)
    sent = yield [block(k).astype(BF) for k in range(1, depth)]
    total = block(0)
    for k, s in zip(range(1, depth), sent):
        total = total + swap(s, "grp", 2 * k).astype(F32)
    (total,) = yield [total.astype(BF)]
    got = [total] + [swap(total, "grp", 2 * k) for k in range(1, depth)]
    (mine,) = yield [jnp.concatenate(reorder(got, line), axis=0)]
    other = swap(mine, "grp", 1)
    results, at = [], 0
    for v in values:
        cols = slice(at, at + v.shape[1])
        at += v.shape[1]
        a, b = mine[:, cols].astype(F32), other[:, cols].astype(F32)
        results.append(jnp.concatenate([jnp.where(side == 0, a, b), jnp.where(side == 0, b, a)], axis=1))
    return results


class Flow:
    def __init__(self, stages):
        self.stages, self.ready, self.result = stages, next(stages), None

    def send(self, operands):
        try:
            self.ready = self.stages.send(operands)
        except StopIteration as done:
            self.ready, self.result = None, done.value


def depart(anchor, flows, after=()):
    flows = [f for f in flows if f.ready is not None]
    operands = [x for f in flows for x in f.ready]
    tied = lax.optimization_barrier((anchor, tuple(operands), tuple(after)))
    operands = list(tied[1])
    for f in flows:
        count = len(f.ready)
        f.send(operands[:count])
        operands = operands[count:]
    return tied[0]


def then_complete(flows):
    return Flow(completing([finish(f) for f in flows]))


def finish(flow):
    while flow.ready is not None:
        flow.send(flow.ready)
    return flow.result


def total_small(value):
    for axis in ("fsdp", "grp"):
        size = lax.axis_size(axis)
        others = [swap(value, axis, k) for k in range(1, size)]
        for other in others:
            value = value + other
    return value


def body(
    layer_input,
    segment_ids,
    bucket_table,
    gain_attn,
    weight_query,
    weight_key,
    weight_value,
    weight_out,
    gain_ffn,
    weight_in,
    weight_back,
    gain_final,
    weight_embed,
    bias_table,
    cotangent,
):
    micro, length, width = layer_input.shape
    heads = bias_table.shape[1]
    size = lax.axis_size("fsdp")
    index = lax.axis_index("fsdp")
    me = index.astype(jnp.int32).reshape(1)
    buckets = bias_table.shape[0] * size
    rows = micro * length
    groups = GROUPS

    part = width // size
    span = width // groups
    small = jnp.concatenate([gain_attn, gain_ffn, gain_final, bias_table.reshape(-1)]).reshape(1, -1)
    small = finish(Flow(gathering(small)))
    small = jnp.concatenate(reorder(small, index), axis=0)
    g_one, g_two, g_three = (
        small[:, k * part : (k + 1) * part].reshape(1, width).astype(F32) for k in range(3)
    )
    table = small[:, 3 * part :].reshape(buckets, heads)

    near = Flow(
        gathering(
            jnp.concatenate(
                [
                    w[:, g * span : (g + 1) * span]
                    for g in range(groups)
                    for w in (weight_query, weight_key, weight_value)
                ],
                axis=1,
            )
        )
    )
    back_rows = weight_back.shape[0] // part
    far = Flow(
        gathering(
            jnp.concatenate(
                [weight_out, weight_in, weight_embed]
                + [weight_back[q * part : (q + 1) * part] for q in range(back_rows)],
                axis=1,
            )
        )
    )
    link = depart(me, [near])
    link = depart(link, [near])

    onehot = (bucket_table[:, None] == lax.iota(jnp.int32, buckets)[None, :]).astype(BF)
    bias_rows = lax.dot_general(table, onehot, (((0,), (1,)), ((), ())), preferred_element_type=F32)
    strips = bias_strips(bias_rows)
    low, wide = key_ranges(segment_ids)
    seg_col = segment_ids.reshape(rows, 1)
    seg_row = segment_ids.reshape(rows // BQ, 1, BQ)

    x = layer_input.reshape(rows, width)
    upstream = cotangent.reshape(rows, -1)
    turn = depart(link, [near, far], [strips])
    near = finish(near)
    query, key, value, key_t, value_t, h1_t = project(turn, x, g_one, near, groups)
    start = depart(low, [far], [query])
    attn, attn_t, probs, inverse = attend(
        start, wide, query, key, value_t, strips, seg_col, seg_row, length, groups
    )
    turn = depart(me, [far], [inverse])
    far = finish(far)
    gains = jnp.concatenate([g_two, g_three], axis=0)
    states, dx2, dattn_t, da, h2_t, h3_t, db_t, hidden, dpre = feed_forward(
        turn, x, [attn], upstream, gains, far
    )

    back_send = grad_cols(me, db_t, hidden, size, 1)
    turn = lax.optimization_barrier((me, back_send))[0]
    back_keep = grad_cols(turn, db_t, hidden, size, 0)
    back = Flow(summing(back_keep, back_send, False))
    turn = depart(turn, [back], [back_keep])
    inner = Flow(summing(*grad_rows(turn, [h2_t], [dpre], size), False))

    def back_of(turn, g):
        return attend_back(
            turn, wide, query, key, key_t, value, attn_t, dattn_t, probs, inverse, length, g
        )

    def project_grad(turn, parts, extra=None):
        return Flow(summing(*grad_set(turn, [([h1_t], list(parts[:3]))], size, extra), True))

    turn = depart(turn, [back, inner], [inner.ready[0]])
    out = grad_set(turn, [([attn_t], [da]), ([h3_t], [upstream])], size)
    turn = depart(low, [inner], [out[0]])
    grads = [back_of(turn, 0)]
    out = Flow(summing(*out, True))
    turn = depart(me, [out, back], [grads[0][3]])
    first = project_grad(turn, grads[0])
    turn = depart(low, [out, first, inner], [first.ready[0]])
    g_back, g_in = (
        lax.psum(v.astype(BF), "grp").astype(F32) for v in (finish(back), finish(inner))
    )
    grads.append(back_of(turn, 1))
    turn = depart(me, [out, first], [grads[1][3]])
    second = project_grad(turn, grads[1])
    out = then_complete([out])
    turn = depart(low, [out, first, second])
    grads.append(back_of(turn, 2))
    turn = depart(me, [out, second], [grads[2][3], finish(first)])

    sums = lax.optimization_barrier((tuple(g[3] for g in grads), turn))[0]
    d_table = jnp.dot(
        jnp.concatenate(sums, axis=0), onehot.astype(F32), precision=lax.Precision.HIGHEST
    ).T.astype(BF)
    d_table = d_table.reshape(size, buckets // size, heads)
    extra = jnp.stack([lax.dynamic_index_in_dim(d_table, index ^ k, 0, False) for k in range(size)])
    extra = jnp.pad(extra, ((0, 0), (0, part - buckets // size), (0, STEP - heads)))
    third = project_grad(turn, grads[2], extra)

    pieces = near * groups
    spans = [slice(3 * span * g, 3 * span * (g + 1)) for g in range(groups)]
    dparts = [p for g in grads for p in g[:3]]
    blocks = rows // 256
    cuts = (blocks - 2 * (blocks // 3), blocks // 3, blocks // 3)
    turn = depart(me, [third, second, out], [third.ready[0]])
    d_input = input_back(turn, x, dx2, g_one, dparts, pieces, spans, 0, cuts[0], None)
    middle = then_complete([first, second])
    turn = depart(me, [third, middle], [d_input] + finish(out))
    d_input = input_back(turn, x, dx2, g_one, dparts, pieces, spans, cuts[0], cuts[1], d_input)
    turn = depart(me, [third, middle], [d_input])
    d_input = input_back(turn, x, dx2, g_one, dparts, pieces, spans, cuts[0] + cuts[1], cuts[2], d_input)
    third = then_complete([third])
    depart(me, [third, middle], [d_input])
    (g_oe,) = finish(out)
    proj = finish(middle) + finish(third)
    g_out, g_embed = g_oe[:, :width], g_oe[:, width:]
    grad_q, grad_k, grad_v = (
        jnp.concatenate([p[:, k * span : (k + 1) * span] for p in proj], axis=1) for k in range(3)
    )
    g_table = proj[-1][: buckets // size, width : width + heads]

    def gain_grad(gain, *pairs):
        return sum(jnp.sum(w.astype(F32) * g, axis=1) for w, g in pairs) / gain.astype(F32)

    gain_grads = (
        gain_grad(gain_attn, (weight_query, grad_q), (weight_key, grad_k), (weight_value, grad_v)),
        gain_grad(gain_ffn, (weight_in, g_in)),
        gain_grad(gain_final, (weight_embed, g_embed)),
    )
    return (
        states.reshape(micro, length, -1),
        d_input.reshape(micro, length, width),
        gain_grads[0],
        grad_q,
        grad_k,
        grad_v,
        g_out,
        gain_grads[1],
        g_in,
        g_back,
        gain_grads[2],
        g_embed,
        g_table,
    )


GROUPS = 3


def solution(mesh):
    placed = (
        P(None, ("grp", "fsdp"), None),
        P(None, ("grp", "fsdp")),
        P(),
        P("fsdp"),
        P("fsdp", None),
        P("fsdp", None),
        P("fsdp", None),
        P("fsdp", None),
        P("fsdp"),
        P("fsdp", None),
        P("fsdp", None),
        P("fsdp"),
        P("fsdp", None),
        P("fsdp", None),
        P(None, ("grp", "fsdp"), None),
    )
    return jax.shard_map(
        body,
        mesh=mesh,
        in_specs=placed,
        out_specs=(
            P(None, ("grp", "fsdp"), None),
            P(None, ("grp", "fsdp"), None),
            P("fsdp"),
            P("fsdp", None),
            P("fsdp", None),
            P("fsdp", None),
            P("fsdp", None),
            P("fsdp"),
            P("fsdp", None),
            P("fsdp", None),
            P("fsdp"),
            P("fsdp", None),
            P("fsdp", None),
        ),
        check_vma=False,
    )
```

```python
import functools
import jax
import jax.numpy as jnp
from jax import lax
from jax.experimental import pallas as pl
from jax.experimental.pallas import tpu as pltpu
from jax.sharding import PartitionSpec as P

BQ = 256
STEP = 128
NEGATIVE = -1e30
VMEM_CAP = 60 * 1024 * 1024
EPS = 1e-06
INV_ROOT_TWO_PI = 0.3989422804014327
BF = jnp.bfloat16
F32 = jnp.float32
NT = (((1,), (1,)), ((), ()))
NN = (((1,), (0,)), ((), ()))
S = jax.ShapeDtypeStruct
ANY = pl.BlockSpec(memory_space=pl.ANY)
PARAMS = pltpu.CompilerParams(vmem_limit_bytes=VMEM_CAP)


def cost(flops, moved, special=0):
    return pl.CostEstimate(flops=flops // 16, bytes_accessed=moved // 16, transcendentals=special // 16)


def mm(a, b, dims=NN):
    return lax.dot_general(a, b, dims, preferred_element_type=F32)


def norm_scale(value):
    return lax.rsqrt(jnp.mean(value * value, axis=-1, keepdims=True) + EPS)


def norm_back(grad, value, scale, gain):
    weighted = grad * gain
    inner = jnp.mean(weighted * value, axis=-1, keepdims=True)
    dvalue = scale * weighted - value * (scale * scale * scale) * inner
    return dvalue


def gelu_parts(value):
    t = 1.0 / (1.0 + (0.3275911 * 0.7071067811865476) * jnp.abs(value))
    poly = 0.5307027145
    for factor in (-0.7265760135, 0.7107068705, -0.142248368, 0.127414796):
        poly = poly * t + factor
    bell = jnp.exp(-0.5 * value * value)
    tail = poly * t * bell
    cdf = jnp.where(value < 0.0, tail, 1.0 - tail)
    return value * cdf, cdf + value * bell * INV_ROOT_TWO_PI


def run_copies(jobs, sems):
    copies = [pltpu.make_async_copy(a, b, sems.at[i]) for i, (a, b) in enumerate(jobs)]
    for copy in copies:
        copy.start()
    for copy in copies:
        copy.wait()


def place(me, k, rows):
    return pl.multiple_of(jnp.bitwise_xor(me, k) * rows, 16)


def placing(me, pieces, target, lanes=slice(None)):
    rows = pieces[0].shape[0]
    return [
        (piece.at[:, lanes], target.at[pl.ds(place(me, k, rows), rows), :]) for k, piece in enumerate(pieces)
    ]


def pack_kernel(*refs, spots):
    sources, out_ref = refs[:-1], refs[-1]
    at = 0
    for index, rows, cols in spots:
        wide = cols.stop - cols.start
        out_ref[:, at : at + wide] = sources[index][rows, cols]
        at += wide


def pack(arrays, spots):
    rows = spots[0][1].stop - spots[0][1].start
    wide = sum(cols.stop - cols.start for _, _, cols in spots)
    return pl.pallas_call(
        functools.partial(pack_kernel, spots=tuple(spots)),
        out_shape=S((rows, wide), BF),
        name="pack",
        cost_estimate=cost(0, 4 * rows * wide),
        compiler_params=PARAMS,
    )(*arrays)


def project_kernel(me_ref, x_ref, gain_ref, *refs, count, groups):
    pieces, refs = refs[:count], refs[count:]
    q_ref, k_ref, v_ref, kt_ref, vt_ref, ht_ref, weight_ref, sems = refs

    @pl.when(pl.program_id(0) == 0)
    def _():
        run_copies(placing(me_ref[0], pieces, weight_ref), sems)

    value = x_ref[...].astype(F32)
    h = (value * norm_scale(value) * gain_ref[...]).astype(BF)
    ht_ref[...] = h.T
    part = h.shape[1] // groups
    for g in range(groups):
        cols = slice(g * part, (g + 1) * part)
        out = mm(h, weight_ref[:, 3 * g * part : 3 * (g + 1) * part]).astype(BF)
        q_ref[:, cols] = out[:, :part]
        k_ref[:, cols] = out[:, part : 2 * part]
        kt_ref[cols, :] = out[:, part : 2 * part].T
        v_ref[:, cols] = out[:, 2 * part :]
        vt_ref[cols, :] = out[:, 2 * part :].T


def project(me, x, gain, pieces, groups, block=256):
    rows, width = x.shape
    natural = pl.BlockSpec((block, width), lambda i, *_: (i, 0))
    turned = pl.BlockSpec((width, block), lambda i, *_: (0, i))
    return pl.pallas_call(
        functools.partial(project_kernel, count=len(pieces), groups=groups),
        grid_spec=pltpu.PrefetchScalarGridSpec(
            num_scalar_prefetch=1,
            grid=(rows // block,),
            in_specs=[natural, pl.BlockSpec((1, width), lambda i, *_: (0, 0))] + [ANY] * len(pieces),
            out_specs=[natural] * 3 + [turned] * 3,
            scratch_shapes=[pltpu.VMEM((width, 3 * width), BF), pltpu.SemaphoreType.DMA((len(pieces),))],
        ),
        out_shape=[S((rows, width), BF)] * 3 + [S((width, rows), BF)] * 3,
        name="project",
        cost_estimate=cost(6 * rows * width * width, 14 * rows * width),
        compiler_params=PARAMS,
    )(me, x, gain, *pieces)


def strip_kernel(rows_ref, strip_ref, *, length):
    rows = jnp.broadcast_to(rows_ref[0], (STEP, 2 * length))
    turned = pltpu.roll(rows, 2 * length - STEP, 1, stride=1, stride_axis=0)
    strip_ref[0] = turned[:, : 2 * length - STEP].T.astype(BF)


def bias_strips(rows):
    heads, twice = rows.shape
    return pl.pallas_call(
        functools.partial(strip_kernel, length=twice // 2),
        grid=(heads,),
        in_specs=[pl.BlockSpec((1, 1, twice), lambda h: (h, 0, 0))],
        out_specs=pl.BlockSpec((1, twice - STEP, STEP), lambda h: (h, 0, 0)),
        out_shape=S((heads, twice - STEP, STEP), BF),
        name="bias_strips",
        cost_estimate=cost(heads * twice * STEP * 20, heads * twice * STEP * 4),
        compiler_params=PARAMS,
    )(rows.reshape(heads, 1, twice))


def by_width(low_ref, width_ref, length, work):
    step = pl.program_id(0) * pl.num_programs(1) + pl.program_id(1)
    low = pl.multiple_of(low_ref[step], STEP)
    width = width_ref[step]
    for blocks in range(BQ // STEP, length // STEP + 1):

        @pl.when(width == blocks)
        def _(blocks=blocks):
            work(low, blocks * STEP)


def half_of(query, side, feat):
    left = lax.broadcasted_iota(jnp.int32, query.shape, 1) < feat
    return jnp.where(left if side == 0 else ~left, query, jnp.zeros_like(query))


def fold(value, combine):
    parts = [value[i : i + 8] for i in range(0, value.shape[0], 8)]
    while len(parts) > 1:
        parts = [combine(*parts[i : i + 2]) if i + 1 < len(parts) else parts[i] for i in range(0, len(parts), 2)]
    return parts[0]


def attend_kernel(
    low_ref, width_ref, q_ref, k_ref, vt_ref, strip_ref, sk_ref, sq_ref,
    attn_ref, attnt_ref, prob_ref, inv_ref, mask_ref, *score_refs, heads, feat, length, group,
):
    start = pl.program_id(1) * BQ
    row = 64

    def work(low, width):
        keys = pl.ds(low, width)
        mask_ref[:width] = jnp.where(sk_ref[keys, :] == sq_ref[0], 0.0, NEGATIVE).astype(BF)
        bases = [low - start + length - (j + 1) * STEP for j in range(BQ // STEP)]

        def one_group(g, carry):
            outs = []

            def lanes_of(head):
                return pl.ds(pl.multiple_of((g * group + head // 2 * 2) * feat, 2 * feat), 2 * feat)

            def score(head):
                lanes = lanes_of(head)
                score_refs[head % len(score_refs)][:width] = mm(
                    k_ref[keys, lanes], half_of(q_ref[:, lanes], head % 2, feat), NT
                )

            def weigh(head):
                ref = score_refs[head % len(score_refs)]
                whole = g * group + head
                top = None
                for at in range(0, width, row):
                    bias = jnp.concatenate(
                        [strip_ref[whole, pl.ds(pl.multiple_of(base + at, row), row), :] for base in bases], axis=1
                    )
                    value = ref[at : at + row] + (bias + mask_ref[at : at + row]).astype(F32)
                    ref[at : at + row] = value
                    value = fold(value, jnp.maximum)
                    top = value if top is None else jnp.maximum(top, value)
                top = jnp.max(top, axis=0, keepdims=True)
                total = None
                for at in range(0, width, row):
                    expo = jnp.exp(ref[at : at + row] - top)
                    prob_ref[0, 0, whole, pl.ds(pl.multiple_of(low + at, row), row), :] = expo.astype(BF)
                    expo = fold(expo, jnp.add)
                    total = expo if total is None else total + expo
                inverse = 1.0 / jnp.sum(total, axis=0, keepdims=True)
                inv_ref[g, head : head + 1, :] = inverse
                return inverse

            def gather(head, inverse):
                whole = g * group + head
                value = vt_ref[pl.ds(pl.multiple_of(whole * feat, feat), feat), keys]
                outs.append(mm(value, prob_ref[0, 0, whole, keys, :]) * inverse)
                if head % 2:
                    lanes = lanes_of(head)
                    both = jnp.concatenate(outs[-2:], axis=0)
                    attnt_ref[lanes, :] = both.astype(BF)
                    attn_ref[:, lanes] = both.T.astype(BF)

            score(0)
            last = None
            for head in range(group):
                if head + 1 < group:
                    score(head + 1)
                inverse = weigh(head)
                if last is not None:
                    gather(*last)
                last = (head, inverse)
            gather(*last)
            return carry

        lax.fori_loop(0, heads // group, one_group, 0)

    by_width(low_ref, width_ref, length, work)


def attend(low, width, q, k, vt, strips, sk, sq, length, groups):
    rows, part = q.shape
    heads = strips.shape[0]
    feat = part // heads
    seqs, blocks = rows // length, length // BQ
    at = lambda s, b, *_: (s * blocks + b, 0)
    whole = lambda s, b, *_: (s, 0)
    at_t = lambda s, b, *_: (0, s * blocks + b)
    return pl.pallas_call(
        functools.partial(attend_kernel, heads=heads, feat=feat, length=length, group=heads // groups),
        grid_spec=pltpu.PrefetchScalarGridSpec(
            num_scalar_prefetch=2,
            grid=(seqs, blocks),
            in_specs=[
                pl.BlockSpec((BQ, part), at),
                pl.BlockSpec((length, part), whole),
                pl.BlockSpec((part, length), lambda s, b, *_: (0, s)),
                pl.BlockSpec(strips.shape, lambda s, b, *_: (0, 0, 0), pipeline_mode=pl.Buffered(1)),
                pl.BlockSpec((length, 1), whole),
                pl.BlockSpec((1, 1, BQ), lambda s, b, *_: (s * blocks + b, 0, 0)),
            ],
            out_specs=[
                pl.BlockSpec((BQ, part), at),
                pl.BlockSpec((part, BQ), at_t),
                pl.BlockSpec((1, 1, heads, length, BQ), lambda s, b, *_: (s, b, 0, 0, 0)),
                pl.BlockSpec((groups, heads // groups, BQ), lambda s, b, *_: (0, 0, s * blocks + b)),
            ],
            scratch_shapes=[pltpu.VMEM((length, BQ), BF)] + [pltpu.VMEM((length, BQ), F32)] * 2,
        ),
        out_shape=[
            S((rows, part), BF),
            S((part, rows), BF),
            S((seqs, blocks, heads, length, BQ), BF),
            S((groups, heads // groups, rows), F32),
        ],
        name="attend",
        cost_estimate=cost(16 * rows * length * part, 2 * rows * heads * length, rows * heads * length),
        compiler_params=PARAMS,
    )(low, width, q, k, vt, strips, sk, sq)


def unskew(data):
    data = jnp.concatenate([data, jnp.zeros((STEP, STEP), F32)], axis=0)
    rows = lax.broadcasted_iota(jnp.int32, (STEP, STEP), 0)
    cols = lax.broadcasted_iota(jnp.int32, (STEP, STEP), 1)
    flip = (rows + cols == STEP - 1).astype(BF)
    high = data.astype(BF)
    low = (data - high.astype(F32)).astype(BF)
    turned = (mm(high, flip) + mm(low, flip)).T
    return jnp.sum(pltpu.roll(turned, 1, 1, stride=1, stride_axis=0), axis=0, keepdims=True)


def attend_back_kernel(
    low_ref, width_ref, q_ref, k_ref, kt_ref, v_ref, attnt_ref, dot_ref, prob_ref, inv_ref,
    dq_ref, dk_ref, dv_ref, sum_ref, diag_ref, dka_ref, dva_ref, *work_refs, heads, feat, length,
):
    seq, block = pl.program_id(0), pl.program_id(1)
    start = block * BQ
    row = 64
    many = len(work_refs) // 2
    dprob_refs, ds_refs = work_refs[:many], work_refs[many:]

    @pl.when(jnp.logical_and(seq == 0, block == 0))
    def _():
        diag_ref[...] = jnp.zeros_like(diag_ref)

    @pl.when(block == 0)
    def _():
        dka_ref[...] = jnp.zeros_like(dka_ref)
        dva_ref[...] = jnp.zeros_like(dva_ref)

    def work(low, width):
        keys = pl.ds(low, width)
        bases = [low - start + length - (j + 1) * STEP for j in range(BQ // STEP)]
        dvals, dqs, dkeys = [], [], []

        def begin(head):
            lanes = slice(head // 2 * 2 * feat, (head // 2 + 1) * 2 * feat)
            feats = slice(head * feat, (head + 1) * feat)
            scaled = dot_ref[feats, :].astype(F32) * inv_ref[0, head : head + 1, :]
            delta = jnp.sum(scaled * attnt_ref[feats, :].astype(F32), axis=0, keepdims=True)
            scaled = scaled.astype(BF)
            blank = jnp.zeros_like(scaled)
            padded = jnp.concatenate([blank, scaled] if head % 2 else [scaled, blank], axis=0)
            dprob_refs[head % many][:width] = mm(v_ref[keys, lanes], padded)
            dvals.append(mm(prob_ref[0, 0, head, keys, :], padded, NT))
            if head % 2:
                dva_ref[keys, lanes] += dvals[-2] + dvals[-1]
            return delta

        def middle(head, delta):
            dprob, ds = dprob_refs[head % many], ds_refs[head % many]
            for at in range(0, width, row):
                prob = prob_ref[0, 0, head, pl.ds(pl.multiple_of(low + at, row), row), :]
                value = prob.astype(F32) * (dprob[at : at + row] - delta)
                ds[at : at + row] = value.astype(BF)
                for j, base in enumerate(bases):
                    diag_ref[head, pl.ds(pl.multiple_of(base + at, row), row), :] += value[:, j * STEP : (j + 1) * STEP]

        def end(head):
            lanes = slice(head // 2 * 2 * feat, (head // 2 + 1) * 2 * feat)
            ds = ds_refs[head % many]
            dkey = mm(ds[:width], half_of(q_ref[:, lanes], head % 2, feat))
            dkeys.append(dkey)
            dqs.append(mm(kt_ref[head * feat : (head + 1) * feat, keys], ds[:width]))
            if head % 2:
                dka_ref[keys, lanes] += dkeys[-2] + dkeys[-1]
                dq_ref[:, lanes] = jnp.concatenate(dqs[-2:], axis=0).T.astype(BF)

        delta = begin(0)
        for head in range(heads):
            following = begin(head + 1) if head + 1 < heads else None
            middle(head, delta)
            if head:
                end(head - 1)
            delta = following
        end(heads - 1)

    by_width(low_ref, width_ref, length, work)

    @pl.when(block == pl.num_programs(1) - 1)
    def _():
        dk_ref[...] = dka_ref[...].astype(BF)
        dv_ref[...] = dva_ref[...].astype(BF)

    @pl.when(jnp.logical_and(seq == pl.num_programs(0) - 1, block == pl.num_programs(1) - 1))
    def _():
        for head in range(heads):
            sum_ref[head : head + 1, :] = unskew(diag_ref[head])


def attend_back(low, width, q, k, kt, v, attnt, dot, prob, inv, length, group):
    rows = q.shape[0]
    part = q.shape[1] // inv.shape[0]
    heads = inv.shape[1]
    feat = part // heads
    seqs, blocks = rows // length, length // BQ
    at = lambda s, b, *_: (s * blocks + b, group)
    whole = lambda s, b, *_: (s, group)
    at_t = lambda s, b, *_: (group, s * blocks + b)
    out = lambda s, b, *_: (s, 0)
    return pl.pallas_call(
        functools.partial(attend_back_kernel, heads=heads, feat=feat, length=length),
        grid_spec=pltpu.PrefetchScalarGridSpec(
            num_scalar_prefetch=2,
            grid=(seqs, blocks),
            in_specs=[
                pl.BlockSpec((BQ, part), at),
                pl.BlockSpec((length, part), whole),
                pl.BlockSpec((part, length), lambda s, b, *_: (group, s)),
                pl.BlockSpec((length, part), whole),
                pl.BlockSpec((part, BQ), at_t),
                pl.BlockSpec((part, BQ), at_t),
                pl.BlockSpec((1, 1, heads, length, BQ), lambda s, b, *_: (s, b, group, 0, 0)),
                pl.BlockSpec((1, heads, BQ), lambda s, b, *_: (group, 0, s * blocks + b)),
            ],
            out_specs=[
                pl.BlockSpec((BQ, part), lambda s, b, *_: (s * blocks + b, 0)),
                pl.BlockSpec((length, part), out),
                pl.BlockSpec((length, part), out),
                pl.BlockSpec((heads, 2 * length), lambda s, b, *_: (0, 0)),
            ],
            scratch_shapes=[
                pltpu.VMEM((heads, 2 * length - STEP, STEP), F32),
                pltpu.VMEM((length, part), F32),
                pltpu.VMEM((length, part), F32),
            ]
            + [pltpu.VMEM((length, BQ), F32)] * 2
            + [pltpu.VMEM((length, BQ), BF)] * 2,
        ),
        out_shape=[S((rows, part), BF)] * 3 + [S((heads, 2 * length), F32)],
        name="attend_back",
        cost_estimate=cost(32 * rows * length * part, 2 * rows * heads * length),
        compiler_params=PARAMS,
    )(low, width, q, k, kt, v, attnt, dot, prob, inv)


def key_ranges(seg):
    firsts, lasts = seg[:, ::BQ], seg[:, BQ - 1 :: BQ]
    low = jnp.sum((seg[:, None, :] < firsts[:, :, None]).astype(jnp.int32), axis=-1)
    high = jnp.sum((seg[:, None, :] <= lasts[:, :, None]).astype(jnp.int32), axis=-1)
    low = low // STEP
    width = (high + STEP - 1) // STEP - low
    return (low * STEP).reshape(-1), width.reshape(-1)


def ffn_kernel(me_ref, x_ref, up_ref, gain_ref, *refs, chunk, count, groups):
    attns, refs = refs[:groups], refs[groups:]
    pieces, refs = refs[:count], refs[count:]
    (states_ref, dx2_ref, dot_ref, da_ref, h2t_ref, h3t_ref, dbt_ref, hid_ref, dpre_ref,
     slope_ref, wo_ref, wi_ref, wb_ref, we_ref, sems) = refs
    width, wide = wi_ref.shape
    embed = we_ref.shape[1]

    @pl.when(pl.program_id(0) == 0)
    def _():
        me, rows = me_ref[0], pieces[0].shape[0]
        copies = placing(me, pieces, wo_ref, slice(0, width))
        copies += placing(me, pieces, wi_ref, slice(width, width + wide))
        copies += placing(me, pieces, we_ref, slice(width + wide, width + wide + embed))
        parts = wide // width
        for k, piece in enumerate(pieces):
            for q in range(parts):
                at = width + wide + embed + q * width
                spot = pl.ds(place(me, k, parts * rows) + q * rows, rows)
                copies.append((piece.at[:, at : at + width], wb_ref.at[spot, :]))
        run_copies(copies, sems)

    g_two, g_three = gain_ref[0:1, :], gain_ref[1:2, :]
    attn = jnp.concatenate([a[...] for a in attns], axis=1)
    x2 = x_ref[...].astype(F32) + mm(attn, wo_ref[...])
    scale2 = norm_scale(x2)
    h2 = (x2 * scale2 * g_two).astype(BF)
    x3 = x2
    for at in range(0, wide, chunk):
        cols = slice(at, at + chunk)
        hidden, slope = gelu_parts(mm(h2, wi_ref[:, cols]))
        hidden = hidden.astype(BF)
        hid_ref[:, cols] = hidden
        slope_ref[:, cols] = slope.astype(BF)
        x3 = x3 + mm(hidden, wb_ref[cols, :])
    scale3 = norm_scale(x3)
    h3 = (x3 * scale3 * g_three).astype(BF)
    states_ref[...] = mm(h3, we_ref[...])
    dx3 = norm_back(mm(up_ref[...], we_ref[...], NT), x3, scale3, g_three)
    db = dx3.astype(BF)
    dh2 = None
    for at in range(0, wide, chunk):
        cols = slice(at, at + chunk)
        dpre = (mm(db, wb_ref[cols, :], NT) * slope_ref[:, cols].astype(F32)).astype(BF)
        dpre_ref[:, cols] = dpre
        part = mm(dpre, wi_ref[:, cols], NT)
        dh2 = part if dh2 is None else dh2 + part
    part = norm_back(dh2, x2, scale2, g_two)
    dx2 = dx3 + part
    da = dx2.astype(BF)
    dx2_ref[...] = dx2
    da_ref[...] = da
    dot_ref[...] = mm(wo_ref[...], da, NT).astype(BF)
    h2t_ref[...] = h2.T
    h3t_ref[...] = h3.T
    dbt_ref[...] = db.T


def feed_forward(me, x, attns, up, gains, pieces, block=256, chunk=768):
    rows, width = x.shape
    count = len(pieces)
    embed = up.shape[1]
    wide = (pieces[0].shape[1] - width - embed) // 2
    fixed = lambda i, *_: (0, 0)
    natural = lambda cols: pl.BlockSpec((block, cols), lambda i, *_: (i, 0))
    turned = pl.BlockSpec((width, block), lambda i, *_: (0, i))
    return pl.pallas_call(
        functools.partial(ffn_kernel, chunk=chunk, count=count, groups=len(attns)),
        grid_spec=pltpu.PrefetchScalarGridSpec(
            num_scalar_prefetch=1,
            grid=(rows // block,),
            in_specs=[natural(width), natural(embed), pl.BlockSpec(gains.shape, fixed)]
            + [natural(a.shape[1]) for a in attns]
            + [ANY] * len(pieces),
            out_specs=[
                natural(embed), natural(width), turned, natural(width), turned, turned, turned,
                natural(wide), natural(wide),
            ],
            scratch_shapes=[
                pltpu.VMEM((block, wide), BF),
                pltpu.VMEM((width, width), BF),
                pltpu.VMEM((width, wide), BF),
                pltpu.VMEM((wide, width), BF),
                pltpu.VMEM((width, embed), BF),
                pltpu.SemaphoreType.DMA((count * (3 + wide // width),)),
            ],
        ),
        out_shape=[
            S((rows, embed), F32), S((rows, width), F32), S((width, rows), BF), S((rows, width), BF),
            S((width, rows), BF), S((width, rows), BF), S((width, rows), BF),
            S((rows, wide), BF), S((rows, wide), BF),
        ],
        name="feed_forward",
        cost_estimate=cost(4 * rows * width * (4 * wide + 2 * width), 20 * rows * wide, 2 * rows * wide),
        compiler_params=PARAMS,
    )(me, x, up, gains, *attns, *pieces)


def input_back_kernel(me_ref, x_ref, dx2_ref, gain_ref, *refs, spans, count, threaded):
    groups = len(spans)
    parts, refs = refs[: 3 * groups], refs[3 * groups :]
    pieces, refs = refs[: groups * count], refs[groups * count + threaded :]
    out_ref, weight_ref, sems = refs

    @pl.when(pl.program_id(0) == 0)
    def _():
        copies = []
        for g, lanes in enumerate(spans):
            copies += placing(me_ref[0], pieces[g * count : (g + 1) * count], weight_ref.at[g], lanes)
        run_copies(copies, sems)

    value = x_ref[...].astype(F32)
    scale = norm_scale(value)
    dh = None
    for g in range(groups):
        term = mm(jnp.concatenate([p[...] for p in parts[3 * g : 3 * g + 3]], axis=1), weight_ref[g], NT)
        dh = term if dh is None else dh + term
    out_ref[...] = dx2_ref[...] + norm_back(dh, value, scale, gain_ref[...])


def input_back(me, x, dx2, gain, parts, pieces, spans, first, steps, held, block=256):
    rows, width = x.shape
    natural = lambda cols: pl.BlockSpec((block, cols), lambda i, *_: (i + first, 0))
    fixed = lambda i, *_: (0, 0)
    operands = [me, x, dx2, gain, *parts, *pieces] + ([] if held is None else [held])
    return pl.pallas_call(
        functools.partial(
            input_back_kernel, spans=spans, count=len(pieces) // len(spans), threaded=0 if held is None else 1
        ),
        grid_spec=pltpu.PrefetchScalarGridSpec(
            num_scalar_prefetch=1,
            grid=(steps,),
            in_specs=[natural(width), natural(width), pl.BlockSpec((1, width), fixed)]
            + [natural(p.shape[1]) for p in parts]
            + [ANY] * (len(pieces) + (held is not None)),
            out_specs=natural(width),
            scratch_shapes=[
                pltpu.VMEM((len(spans), width, 3 * parts[0].shape[1]), BF),
                pltpu.SemaphoreType.DMA((len(pieces),)),
            ],
        ),
        out_shape=S((rows, width), F32),
        input_output_aliases={} if held is None else {len(operands) - 1: 0},
        name="input_back",
        cost_estimate=cost(6 * steps * block * width * width, 16 * steps * block * width),
        compiler_params=PARAMS,
    )(*operands)


def grad_rows_kernel(me_ref, *refs, count, lefts):
    lefts, rights, (keep_ref, send_ref, full_ref) = refs[:lefts], refs[lefts:-3], refs[-3:]
    rows = full_ref.shape[0] // count
    down = 0
    for left in lefts:
        at = 0
        for right in rights:
            cols = slice(at, at + right.shape[1])
            at += right.shape[1]
            full_ref[down : down + left.shape[0], cols] = mm(left[...], right[...])
        down += left.shape[0]
    for k in range(count):
        spot = pl.ds(pl.multiple_of(jnp.bitwise_xor(me_ref[0], k) * rows, 16), rows)
        (send_ref if k & 1 else keep_ref)[k >> 1] = full_ref[spot, :].astype(BF)


def grad_rows(me, lefts, rights, count, tile=768, first=0, tiles=None):
    m, rows = sum(left.shape[0] for left in lefts), lefts[0].shape[1]
    if len(rights) > 1:
        tile, tiles = sum(r.shape[1] for r in rights), 1
        specs = [pl.BlockSpec(r.shape, lambda j, *_: (0, 0)) for r in rights]
    else:
        tile = min(tile, rights[0].shape[1])
        tiles = rights[0].shape[1] // tile if tiles is None else tiles
        specs = [pl.BlockSpec((rows, tile), lambda j, *_: (0, j + first))]
    out = pl.BlockSpec((count // 2, m // count, tile), lambda j, *_: (0, 0, j))
    shape = S((count // 2, m // count, tile * tiles), BF)
    return pl.pallas_call(
        functools.partial(grad_rows_kernel, count=count, lefts=len(lefts)),
        grid_spec=pltpu.PrefetchScalarGridSpec(
            num_scalar_prefetch=1,
            grid=(tiles,),
            in_specs=[pl.BlockSpec(left.shape, lambda j, *_: (0, 0), pipeline_mode=pl.Buffered(1)) for left in lefts]
            + specs,
            out_specs=[out, out],
            scratch_shapes=[pltpu.VMEM((m, tile), F32)],
        ),
        out_shape=[shape, shape],
        name="weight_grad",
        cost_estimate=cost(2 * m * rows * tile * tiles, 2 * rows * (m + tile * tiles)),
        compiler_params=PARAMS,
    )(me, *lefts, *rights)


def grad_set_kernel(me_ref, *refs, shapes, count, extra):
    operands = sum(a + b for a, b in shapes)
    sources, refs = refs[:operands], refs[operands:]
    if extra:
        (sums_ref, hot_ref), refs, table_ref = refs[:2], refs[2:-1], refs[-1]
    keep_ref, send_ref, full_ref = refs[:3]
    held, sems = refs[3:-1], refs[-1]
    copies = [pltpu.make_async_copy(a, b, sems.at[i]) for i, (a, b) in enumerate(zip(sources, held))]
    for copy in copies:
        copy.start()
    rows = full_ref.shape[0] // count
    index = at = 0
    for lefts, rights in shapes:
        left = held[index : index + lefts]
        right = held[index + lefts : index + lefts + rights]
        for copy in copies[index : index + lefts]:
            copy.wait()
        for n, r in enumerate(right):
            copies[index + lefts + n].wait()
            down = 0
            for part in left:
                full_ref[down : down + part.shape[0], at : at + r.shape[1]] = mm(part[...], r[...])
                down += part.shape[0]
            at += r.shape[1]
        index += lefts + rights
    if extra:
        sums = sums_ref[...]
        high = sums.astype(BF)
        rest = (sums - high.astype(F32)).astype(BF)
        table_ref[...] = jnp.zeros_like(table_ref)
        table_ref[:, : sums.shape[0]] = mm(hot_ref[...], high, NT) + mm(hot_ref[...], rest, NT)
        each = table_ref.shape[0] // count
    for k in range(count):
        target = send_ref if k & 1 else keep_ref
        target[k >> 1, :, :at] = full_ref[pl.ds(place(me_ref[0], k, rows), rows), :].astype(BF)
        if extra:
            target[k >> 1, :, at:] = jnp.zeros((rows, STEP), BF)
            own = pl.ds(jnp.bitwise_xor(me_ref[0], k) * each, each)
            target[k >> 1, :each, at:] = table_ref[own, :].astype(BF)


def grad_set(me, jobs, count, extra=None):
    operands = [x for lefts, rights in jobs for x in lefts + rights]
    m, rows = sum(x.shape[0] for x in jobs[0][0]), jobs[0][0][0].shape[1]
    n = sum(r.shape[1] for _, rights in jobs for r in rights)
    wide = n + (0 if extra is None else STEP)
    shape = S((count // 2, m // count, wide), BF)
    out = pl.BlockSpec(shape.shape, lambda j, *_: (0, 0, 0))
    more = [] if extra is None else list(extra)
    return pl.pallas_call(
        functools.partial(
            grad_set_kernel,
            shapes=tuple((len(a), len(b)) for a, b in jobs),
            count=count,
            extra=extra is not None,
        ),
        grid_spec=pltpu.PrefetchScalarGridSpec(
            num_scalar_prefetch=1,
            grid=(1,),
            in_specs=[ANY] * len(operands) + [pl.BlockSpec(e.shape, lambda j, *_: (0, 0)) for e in more],
            out_specs=[out, out],
            scratch_shapes=[pltpu.VMEM((m, n), F32)]
            + [pltpu.VMEM(x.shape, BF) for x in operands]
            + [pltpu.SemaphoreType.DMA((len(operands),))]
            + ([pltpu.VMEM((extra[1].shape[0], STEP), F32)] if more else []),
        ),
        out_shape=[shape, shape],
        name="weight_grads",
        cost_estimate=cost(2 * m * rows * n, 2 * rows * (m + n)),
        compiler_params=PARAMS,
    )(me, *operands, *more)


def grad_cols_kernel(me_ref, left_ref, right_ref, out_ref):
    out_ref[0] = mm(left_ref[...], right_ref[...]).astype(BF).T


def grad_cols(me, left, right, count, odd, tile=768):
    m, rows = left.shape
    n = right.shape[1]
    part = n // count
    if part % STEP:
        full = lax.dot_general(right, left, (((0,), (1,)), ((), ())), preferred_element_type=F32).astype(BF)
        return jnp.stack(
            [lax.dynamic_slice_in_dim(full, (me[0] ^ k) * part, part, 0) for k in range(odd, count, 2)]
        )
    tile = min(tile, part)
    inner = part // tile
    return pl.pallas_call(
        grad_cols_kernel,
        grid_spec=pltpu.PrefetchScalarGridSpec(
            num_scalar_prefetch=1,
            grid=(count // 2, inner),
            in_specs=[
                pl.BlockSpec((m, rows), lambda k, t, me: (0, 0), pipeline_mode=pl.Buffered(1)),
                pl.BlockSpec((rows, tile), lambda k, t, me: (0, jnp.bitwise_xor(me[0], 2 * k + odd) * inner + t)),
            ],
            out_specs=pl.BlockSpec((1, tile, m), lambda k, t, me: (k, t, 0)),
        ),
        out_shape=S((count // 2, part, m), BF),
        name="weight_grad",
        cost_estimate=cost(m * rows * n, rows * (2 * m + n)),
        compiler_params=PARAMS,
    )(me, left, right)


def bits_of(axis):
    size = lax.axis_size(axis)
    count = size.bit_length() - 1
    assert size == 1 << count
    return count


def swap(value, axis, mask):
    size = lax.axis_size(axis)
    return lax.ppermute(value, axis, [(i, i ^ mask) for i in range(size)])


def gathering(shard):
    held = {0: shard}
    for bit in reversed(range(1, bits_of("fsdp"))):
        step = 1 << bit
        sent = yield list(held.values())
        held.update({k ^ step: swap(v, "fsdp", step) for k, v in zip(list(held), sent)})
    (own,) = yield [shard]
    others = [k for k in held if k]
    first = swap(own, "fsdp", 1)
    sent = yield [held[k] for k in others]
    held.update({k ^ 1: swap(v, "fsdp", 1) for k, v in zip(others, sent)})
    held[1] = first
    return [held[k] for k in range(len(held))]


def reorder(parts, index):
    parts = list(parts)
    for bit in range(len(parts).bit_length() - 1):
        flag = (index >> bit) & 1
        parts = [jnp.where(flag == 1, parts[k ^ (1 << bit)], parts[k]) for k in range(len(parts))]
    return parts


def summing(keep, send, late=False):
    (sent,) = yield [send]
    got = swap(sent, "fsdp", 1)
    if late:
        (got,) = yield [got]
        (keep,) = keep
    part = {2 * k: keep[k].astype(F32) + got[k].astype(F32) for k in range(keep.shape[0])}
    for bit in range(1, bits_of("fsdp")):
        step = 1 << bit
        away = [k for k in part if k & step]
        if late:
            half = part[0].shape[0] // 2
            sent = yield [part[k][:half].astype(BF) for k in away]
            top = [swap(s, "fsdp", step) for s in sent]
            sent = yield [part[k][half:].astype(BF) for k in away] + top
            bottom = [swap(s, "fsdp", step) for s in sent[: len(away)]]
            arrived = [jnp.concatenate(pair, axis=0) for pair in zip(sent[len(away) :], bottom)]
        else:
            sent = yield [part[k].astype(BF) for k in away]
            arrived = [swap(s, "fsdp", step) for s in sent]
        got = {k ^ step: g for k, g in zip(away, arrived)}
        part = {k: part[k] + got[k].astype(F32) for k in got}
    value = part[0]
    side = lax.axis_index("grp") & 1
    size = value.shape[1] // 2
    (sent,) = yield [lax.dynamic_slice_in_dim(value, (1 - side) * size, size, 1).astype(BF)]
    return lax.dynamic_slice_in_dim(value, side * size, size, 1) + swap(sent, "grp", 1).astype(F32)


def completing(values, split=False):
    me = lax.axis_index("grp")
    side, line = me & 1, me >> 1
    depth = lax.axis_size("grp") // 2
    value = values[0] if len(values) == 1 else jnp.concatenate(values, axis=1)
    rows = value.shape[0] // depth
    block = lambda k: lax.dynamic_slice_in_dim(value, (line ^ k) * rows, rows, 0)
    sent = yield [block(k).astype(BF) for k in range(1, depth)]
    total = block(0)
    for k, s in zip(range(1, depth), sent):
        total = total + swap(s, "grp", 2 * k).astype(F32)
    (total,) = yield [total.astype(BF)]
    got = [total] + [swap(total, "grp", 2 * k) for k in range(1, depth)]
    got = reorder(got, line)
    if split:
        half = total.shape[1] // 2
        left, right = (jnp.concatenate([g[:, c] for g in got], axis=0) for c in (slice(0, half), slice(half, None)))
        (left,) = yield [left]
        first = swap(left, "grp", 1)
        (right, first) = yield [right, first]
        mine = jnp.concatenate([left, right], axis=1)
        other = jnp.concatenate([first, swap(right, "grp", 1)], axis=1)
    else:
        (mine,) = yield [jnp.concatenate(got, axis=0)]
        other = swap(mine, "grp", 1)
    results, at = [], 0
    for v in values:
        cols = slice(at, at + v.shape[1])
        at += v.shape[1]
        a, b = mine[:, cols].astype(F32), other[:, cols].astype(F32)
        results.append(jnp.concatenate([jnp.where(side == 0, a, b), jnp.where(side == 0, b, a)], axis=1))
    return results


class Flow:
    def __init__(self, stages):
        self.stages, self.ready, self.result = stages, next(stages), None

    def send(self, operands):
        try:
            self.ready = self.stages.send(operands)
        except StopIteration as done:
            self.ready, self.result = None, done.value


def depart(anchor, flows, after=()):
    flows = [f for f in flows if f.ready is not None]
    operands = [x for f in flows for x in f.ready]
    tied = lax.optimization_barrier((anchor, tuple(operands), tuple(after)))
    operands = list(tied[1])
    for f in flows:
        count = len(f.ready)
        f.send(operands[:count])
        operands = operands[count:]
    return tied[0]


def then_complete(flows):
    return Flow(completing([finish(f) for f in flows]))


def finish(flow):
    while flow.ready is not None:
        flow.send(flow.ready)
    return flow.result


def total_small(value):
    for axis in ("fsdp", "grp"):
        size = lax.axis_size(axis)
        others = [swap(value, axis, k) for k in range(1, size)]
        for other in others:
            value = value + other
    return value


def body(
    layer_input,
    segment_ids,
    bucket_table,
    gain_attn,
    weight_query,
    weight_key,
    weight_value,
    weight_out,
    gain_ffn,
    weight_in,
    weight_back,
    gain_final,
    weight_embed,
    bias_table,
    cotangent,
):
    micro, length, width = layer_input.shape
    heads = bias_table.shape[1]
    size = lax.axis_size("fsdp")
    index = lax.axis_index("fsdp")
    me = index.astype(jnp.int32).reshape(1)
    buckets = bias_table.shape[0] * size
    rows = micro * length
    groups = GROUPS

    part = width // size
    span = width // groups
    own_rows = slice(0, part)
    near = Flow(
        gathering(
            pack(
                [weight_query, weight_key, weight_value],
                [(w, own_rows, slice(g * span, (g + 1) * span)) for g in range(groups) for w in range(3)],
            )
        )
    )
    link = depart(me, [near])
    full = lambda w: (own_rows, slice(0, w.shape[1]))
    far = Flow(
        gathering(
            pack(
                [weight_out, weight_in, weight_embed, weight_back],
                [(0, *full(weight_out)), (1, *full(weight_in)), (2, *full(weight_embed))]
                + [
                    (3, slice(q * part, (q + 1) * part), slice(0, width))
                    for q in range(weight_back.shape[0] // part)
                ],
            )
        )
    )
    small = jnp.concatenate([gain_attn, gain_ffn, gain_final, bias_table.reshape(-1)]).reshape(1, -1)
    small = finish(Flow(gathering(small)))
    small = jnp.concatenate(reorder(small, index), axis=0)
    g_one, g_two, g_three = (
        small[:, k * part : (k + 1) * part].reshape(1, width).astype(F32) for k in range(3)
    )
    table = small[:, 3 * part :].reshape(buckets, heads)

    link = depart(link, [near])

    onehot = (bucket_table[:, None] == lax.iota(jnp.int32, buckets)[None, :]).astype(BF)
    bias_rows = lax.dot_general(table, onehot, (((0,), (1,)), ((), ())), preferred_element_type=F32)
    low, wide = key_ranges(segment_ids)
    seg_col = segment_ids.reshape(rows, 1)
    seg_row = segment_ids.reshape(rows // BQ, 1, BQ)
    gains = jnp.concatenate([g_two, g_three], axis=0)
    bias_rows, low, wide, seg_col, seg_row, gains, g_one = lax.optimization_barrier(
        (bias_rows, low, wide, seg_col, seg_row, gains, g_one)
    )
    strips = bias_strips(bias_rows)

    x = layer_input.reshape(rows, width)
    upstream = cotangent.reshape(rows, -1)
    turn = depart(link, [near, far], [strips])
    near = finish(near)
    query, key, value, key_t, value_t, h1_t = project(turn, x, g_one, near, groups)
    start = depart(low, [far], [query])
    attn, attn_t, probs, inverse = attend(
        start, wide, query, key, value_t, strips, seg_col, seg_row, length, groups
    )
    turn = depart(me, [far], [inverse])
    far = finish(far)
    states, dx2, dattn_t, da, h2_t, h3_t, db_t, hidden, dpre = feed_forward(
        turn, x, [attn], upstream, gains, far
    )

    back_send = grad_cols(me, db_t, hidden, size, 1)
    back_keep = []
    back = Flow(summing(back_keep, back_send, True))
    turn = depart(me, [back])
    back_keep.append(grad_cols(turn, db_t, hidden, size, 0))
    turn = depart(me, [back], back_keep)
    turn = depart(turn, [back])
    inner = Flow(summing(*grad_rows(turn, [h2_t], [dpre], size)))

    def back_of(turn, g):
        return attend_back(
            turn, wide, query, key, key_t, value, attn_t, dattn_t, probs, inverse, length, g
        )

    def project_grad(turn, parts, extra=None):
        return Flow(summing(*grad_set(turn, [([h1_t], list(parts[:3]))], size, extra)))

    turn = depart(turn, [inner, back])
    out = grad_set(turn, [([attn_t], [da]), ([h3_t], [upstream])], size)
    turn = depart(low, [inner, back], [out[0]])
    grads = [back_of(turn, 0)]
    out = Flow(summing(*out))
    turn = depart(me, [out], [grads[0][3]] + inner.ready)
    first = project_grad(turn, grads[0])
    turn = depart(low, [inner, out, first], [finish(back)])
    grads.append(back_of(turn, 1))
    turn = depart(me, [out, first], [grads[1][3]])
    second = project_grad(turn, grads[1])
    fold = back.result.shape[0] // finish(inner).shape[0]
    turned = jnp.concatenate(jnp.split(back.result, fold, axis=0), axis=1)
    wide_flow = Flow(completing([inner.result, turned], True))
    turn = depart(low, [wide_flow, first, second], [finish(out)])
    grads.append(back_of(turn, 2))
    joint = then_complete([out, first])
    turn = depart(me, [wide_flow, second], [grads[2][3]])
    third = project_grad(turn, grads[2], (jnp.concatenate([g[3] for g in grads], axis=0), onehot.T))

    pieces = near * groups
    spans = [slice(3 * span * g, 3 * span * (g + 1)) for g in range(groups)]
    dparts = [p for g in grads for p in g[:3]]
    blocks = rows // 256
    cuts = (blocks - 2 * (blocks // 3), blocks // 3, blocks // 3)
    turn = depart(me, [second, third])
    d_input = input_back(turn, x, dx2, g_one, dparts, pieces, spans, 0, cuts[0], None)
    turn = depart(me, [wide_flow, third, joint], [d_input, finish(second)])
    d_input = input_back(turn, x, dx2, g_one, dparts, pieces, spans, cuts[0], cuts[1], d_input)
    turn = depart(me, [wide_flow, third, joint], [d_input])
    d_input = input_back(turn, x, dx2, g_one, dparts, pieces, spans, cuts[0] + cuts[1], cuts[2], d_input)
    last = then_complete([second, third])
    depart(me, [joint, last], [d_input] + finish(wide_flow))
    g_in, g_back = wide_flow.result
    cut = g_back.shape[1] // fold // 2
    g_back = jnp.concatenate(
        [
            jnp.concatenate([g_back[:, (h * fold + q) * cut : (h * fold + q + 1) * cut] for h in range(2)], axis=1)
            for q in range(fold)
        ],
        axis=0,
    )
    g_oe, *proj = finish(joint) + finish(last)
    g_out, g_embed = g_oe[:, :width], g_oe[:, width:]
    grad_q, grad_k, grad_v = (
        jnp.concatenate([p[:, k * span : (k + 1) * span] for p in proj], axis=1) for k in range(3)
    )
    g_table = proj[-1][: buckets // size, width : width + heads]

    def gain_grad(gain, *pairs):
        return sum(jnp.sum(w.astype(F32) * g, axis=1) for w, g in pairs) / gain.astype(F32)

    gain_grads = (
        gain_grad(gain_attn, (weight_query, grad_q), (weight_key, grad_k), (weight_value, grad_v)),
        gain_grad(gain_ffn, (weight_in, g_in)),
        gain_grad(gain_final, (weight_embed, g_embed)),
    )
    return (
        states.reshape(micro, length, -1),
        d_input.reshape(micro, length, width),
        gain_grads[0],
        grad_q,
        grad_k,
        grad_v,
        g_out,
        gain_grads[1],
        g_in,
        g_back,
        gain_grads[2],
        g_embed,
        g_table,
    )


GROUPS = 3


def solution(mesh):
    placed = (
        P(None, ("grp", "fsdp"), None),
        P(None, ("grp", "fsdp")),
        P(),
        P("fsdp"),
        P("fsdp", None),
        P("fsdp", None),
        P("fsdp", None),
        P("fsdp", None),
        P("fsdp"),
        P("fsdp", None),
        P("fsdp", None),
        P("fsdp"),
        P("fsdp", None),
        P("fsdp", None),
        P(None, ("grp", "fsdp"), None),
    )
    return jax.shard_map(
        body,
        mesh=mesh,
        in_specs=placed,
        out_specs=(
            P(None, ("grp", "fsdp"), None),
            P(None, ("grp", "fsdp"), None),
            P("fsdp"),
            P("fsdp", None),
            P("fsdp", None),
            P("fsdp", None),
            P("fsdp", None),
            P("fsdp"),
            P("fsdp", None),
            P("fsdp", None),
            P("fsdp"),
            P("fsdp", None),
            P("fsdp", None),
        ),
        check_vma=False,
    )
```

```python
import functools
import jax
import jax.numpy as jnp
from jax import lax
from jax.experimental import pallas as pl
from jax.experimental.pallas import tpu as pltpu
from jax.sharding import PartitionSpec as P

BQ = 256
STEP = 128
NEGATIVE = -1e30
VMEM_CAP = 60 * 1024 * 1024
EPS = 1e-06
INV_ROOT_TWO_PI = 0.3989422804014327
BF = jnp.bfloat16
F32 = jnp.float32
NT = (((1,), (1,)), ((), ()))
NN = (((1,), (0,)), ((), ()))
S = jax.ShapeDtypeStruct
ANY = pl.BlockSpec(memory_space=pl.ANY)
PARAMS = pltpu.CompilerParams(vmem_limit_bytes=VMEM_CAP)


def cost(flops, moved, special=0):
    return pl.CostEstimate(flops=flops // 16, bytes_accessed=moved // 16, transcendentals=special // 16)


def mm(a, b, dims=NN):
    return lax.dot_general(a, b, dims, preferred_element_type=F32)


def norm_scale(value):
    return lax.rsqrt(jnp.mean(value * value, axis=-1, keepdims=True) + EPS)


def norm_back(grad, value, scale, gain):
    weighted = grad * gain
    inner = jnp.mean(weighted * value, axis=-1, keepdims=True)
    dvalue = scale * weighted - value * (scale * scale * scale) * inner
    return dvalue


def gelu_parts(value):
    t = 1.0 / (1.0 + (0.3275911 * 0.7071067811865476) * jnp.abs(value))
    poly = 0.5307027145
    for factor in (-0.7265760135, 0.7107068705, -0.142248368, 0.127414796):
        poly = poly * t + factor
    bell = jnp.exp(-0.5 * value * value)
    tail = poly * t * bell
    cdf = jnp.where(value < 0.0, tail, 1.0 - tail)
    return value * cdf, cdf + value * bell * INV_ROOT_TWO_PI


def run_copies(jobs, sems):
    copies = [pltpu.make_async_copy(a, b, sems.at[i]) for i, (a, b) in enumerate(jobs)]
    for copy in copies:
        copy.start()
    for copy in copies:
        copy.wait()


def place(me, k, rows):
    return pl.multiple_of(jnp.bitwise_xor(me, k) * rows, 16)


def placing(me, pieces, target, lanes=slice(None)):
    rows = pieces[0].shape[0]
    return [
        (piece.at[:, lanes], target.at[pl.ds(place(me, k, rows), rows), :]) for k, piece in enumerate(pieces)
    ]


def pack_kernel(*refs, spots):
    sources, out_ref = refs[:-1], refs[-1]
    at = 0
    for index, rows, cols in spots:
        wide = cols.stop - cols.start
        out_ref[:, at : at + wide] = sources[index][rows, cols]
        at += wide


def pack(arrays, spots):
    rows = spots[0][1].stop - spots[0][1].start
    wide = sum(cols.stop - cols.start for _, _, cols in spots)
    return pl.pallas_call(
        functools.partial(pack_kernel, spots=tuple(spots)),
        out_shape=S((rows, wide), BF),
        name="pack",
        cost_estimate=cost(0, 4 * rows * wide),
        compiler_params=PARAMS,
    )(*arrays)


def project_kernel(me_ref, x_ref, gain_ref, *refs, count, groups):
    pieces, refs = refs[:count], refs[count:]
    q_ref, k_ref, v_ref, kt_ref, vt_ref, ht_ref, weight_ref, sems = refs

    @pl.when(pl.program_id(0) == 0)
    def _():
        run_copies(placing(me_ref[0], pieces, weight_ref), sems)

    value = x_ref[...].astype(F32)
    h = (value * norm_scale(value) * gain_ref[...]).astype(BF)
    ht_ref[...] = h.T
    part = h.shape[1] // groups
    for g in range(groups):
        cols = slice(g * part, (g + 1) * part)
        out = mm(h, weight_ref[:, 3 * g * part : 3 * (g + 1) * part]).astype(BF)
        q_ref[:, cols] = out[:, :part]
        k_ref[:, cols] = out[:, part : 2 * part]
        kt_ref[cols, :] = out[:, part : 2 * part].T
        v_ref[:, cols] = out[:, 2 * part :]
        vt_ref[cols, :] = out[:, 2 * part :].T


def project(me, x, gain, pieces, groups, block=256):
    rows, width = x.shape
    natural = pl.BlockSpec((block, width), lambda i, *_: (i, 0))
    turned = pl.BlockSpec((width, block), lambda i, *_: (0, i))
    return pl.pallas_call(
        functools.partial(project_kernel, count=len(pieces), groups=groups),
        grid_spec=pltpu.PrefetchScalarGridSpec(
            num_scalar_prefetch=1,
            grid=(rows // block,),
            in_specs=[natural, pl.BlockSpec((1, width), lambda i, *_: (0, 0))] + [ANY] * len(pieces),
            out_specs=[natural] * 3 + [turned] * 3,
            scratch_shapes=[pltpu.VMEM((width, 3 * width), BF), pltpu.SemaphoreType.DMA((len(pieces),))],
        ),
        out_shape=[S((rows, width), BF)] * 3 + [S((width, rows), BF)] * 3,
        name="project",
        cost_estimate=cost(6 * rows * width * width, 14 * rows * width),
        compiler_params=PARAMS,
    )(me, x, gain, *pieces)


def strip_kernel(rows_ref, strip_ref, *, length):
    rows = jnp.broadcast_to(rows_ref[0], (STEP, 2 * length))
    turned = pltpu.roll(rows, 2 * length - STEP, 1, stride=1, stride_axis=0)
    strip_ref[0] = turned[:, : 2 * length - STEP].T.astype(BF)


def bias_strips(rows):
    heads, twice = rows.shape
    return pl.pallas_call(
        functools.partial(strip_kernel, length=twice // 2),
        grid=(heads,),
        in_specs=[pl.BlockSpec((1, 1, twice), lambda h: (h, 0, 0))],
        out_specs=pl.BlockSpec((1, twice - STEP, STEP), lambda h: (h, 0, 0)),
        out_shape=S((heads, twice - STEP, STEP), BF),
        name="bias_strips",
        cost_estimate=cost(heads * twice * STEP * 20, heads * twice * STEP * 4),
        compiler_params=PARAMS,
    )(rows.reshape(heads, 1, twice))


def by_width(low_ref, width_ref, length, work):
    step = pl.program_id(0) * pl.num_programs(1) + pl.program_id(1)
    low = pl.multiple_of(low_ref[step], STEP)
    width = width_ref[step]
    for blocks in range(BQ // STEP, length // STEP + 1):

        @pl.when(width == blocks)
        def _(blocks=blocks):
            work(low, blocks * STEP)


def half_of(query, side, feat):
    left = lax.broadcasted_iota(jnp.int32, query.shape, 1) < feat
    return jnp.where(left if side == 0 else ~left, query, jnp.zeros_like(query))


def fold(value, combine):
    parts = [value[i : i + 8] for i in range(0, value.shape[0], 8)]
    while len(parts) > 1:
        parts = [combine(*parts[i : i + 2]) if i + 1 < len(parts) else parts[i] for i in range(0, len(parts), 2)]
    return parts[0]


def attend_kernel(
    low_ref, width_ref, q_ref, k_ref, vt_ref, strip_ref, sk_ref, sq_ref,
    attn_ref, attnt_ref, prob_ref, inv_ref, mask_ref, *score_refs, heads, feat, length, group,
):
    start = pl.program_id(1) * BQ
    row = 64

    def work(low, width):
        keys = pl.ds(low, width)
        mask_ref[:width] = jnp.where(sk_ref[keys, :] == sq_ref[0], 0.0, NEGATIVE).astype(BF)
        bases = [low - start + length - (j + 1) * STEP for j in range(BQ // STEP)]

        def one_group(g, carry):
            outs = []

            def lanes_of(head):
                return pl.ds(pl.multiple_of((g * group + head // 2 * 2) * feat, 2 * feat), 2 * feat)

            def score(head):
                lanes = lanes_of(head)
                score_refs[head % len(score_refs)][:width] = mm(
                    k_ref[keys, lanes], half_of(q_ref[:, lanes], head % 2, feat), NT
                )

            def weigh(head):
                ref = score_refs[head % len(score_refs)]
                whole = g * group + head
                top = None
                for at in range(0, width, row):
                    bias = jnp.concatenate(
                        [strip_ref[whole, pl.ds(pl.multiple_of(base + at, row), row), :] for base in bases], axis=1
                    )
                    value = ref[at : at + row] + (bias + mask_ref[at : at + row]).astype(F32)
                    ref[at : at + row] = value
                    value = fold(value, jnp.maximum)
                    top = value if top is None else jnp.maximum(top, value)
                top = jnp.max(top, axis=0, keepdims=True)
                total = None
                for at in range(0, width, row):
                    expo = jnp.exp(ref[at : at + row] - top)
                    prob_ref[0, 0, whole, pl.ds(pl.multiple_of(low + at, row), row), :] = expo.astype(BF)
                    expo = fold(expo, jnp.add)
                    total = expo if total is None else total + expo
                inverse = 1.0 / jnp.sum(total, axis=0, keepdims=True)
                inv_ref[g, head : head + 1, :] = inverse
                return inverse

            def gather(head, inverse):
                whole = g * group + head
                value = vt_ref[pl.ds(pl.multiple_of(whole * feat, feat), feat), keys]
                outs.append(mm(value, prob_ref[0, 0, whole, keys, :]) * inverse)
                if head % 2:
                    lanes = lanes_of(head)
                    both = jnp.concatenate(outs[-2:], axis=0)
                    attnt_ref[lanes, :] = both.astype(BF)
                    attn_ref[:, lanes] = both.T.astype(BF)

            score(0)
            last = None
            for head in range(group):
                if head + 1 < group:
                    score(head + 1)
                inverse = weigh(head)
                if last is not None:
                    gather(*last)
                last = (head, inverse)
            gather(*last)
            return carry

        lax.fori_loop(0, heads // group, one_group, 0)

    by_width(low_ref, width_ref, length, work)


def attend(low, width, q, k, vt, strips, sk, sq, length, groups):
    rows, part = q.shape
    heads = strips.shape[0]
    feat = part // heads
    seqs, blocks = rows // length, length // BQ
    at = lambda s, b, *_: (s * blocks + b, 0)
    whole = lambda s, b, *_: (s, 0)
    at_t = lambda s, b, *_: (0, s * blocks + b)
    return pl.pallas_call(
        functools.partial(attend_kernel, heads=heads, feat=feat, length=length, group=heads // groups),
        grid_spec=pltpu.PrefetchScalarGridSpec(
            num_scalar_prefetch=2,
            grid=(seqs, blocks),
            in_specs=[
                pl.BlockSpec((BQ, part), at),
                pl.BlockSpec((length, part), whole),
                pl.BlockSpec((part, length), lambda s, b, *_: (0, s)),
                pl.BlockSpec(strips.shape, lambda s, b, *_: (0, 0, 0), pipeline_mode=pl.Buffered(1)),
                pl.BlockSpec((length, 1), whole),
                pl.BlockSpec((1, 1, BQ), lambda s, b, *_: (s * blocks + b, 0, 0)),
            ],
            out_specs=[
                pl.BlockSpec((BQ, part), at),
                pl.BlockSpec((part, BQ), at_t),
                pl.BlockSpec((1, 1, heads, length, BQ), lambda s, b, *_: (s, b, 0, 0, 0)),
                pl.BlockSpec((groups, heads // groups, BQ), lambda s, b, *_: (0, 0, s * blocks + b)),
            ],
            scratch_shapes=[pltpu.VMEM((length, BQ), BF)] + [pltpu.VMEM((length, BQ), F32)] * 2,
        ),
        out_shape=[
            S((rows, part), BF),
            S((part, rows), BF),
            S((seqs, blocks, heads, length, BQ), BF),
            S((groups, heads // groups, rows), F32),
        ],
        name="attend",
        cost_estimate=cost(16 * rows * length * part, 2 * rows * heads * length, rows * heads * length),
        compiler_params=PARAMS,
    )(low, width, q, k, vt, strips, sk, sq)


def unskew(data):
    data = jnp.concatenate([data, jnp.zeros((STEP, STEP), F32)], axis=0)
    rows = lax.broadcasted_iota(jnp.int32, (STEP, STEP), 0)
    cols = lax.broadcasted_iota(jnp.int32, (STEP, STEP), 1)
    flip = (rows + cols == STEP - 1).astype(BF)
    high = data.astype(BF)
    low = (data - high.astype(F32)).astype(BF)
    turned = mm(flip, high, NT) + mm(flip, low, NT)
    return jnp.sum(pltpu.roll(turned, 1, 1, stride=1, stride_axis=0), axis=0, keepdims=True)


def attend_back_kernel(
    low_ref, width_ref, q_ref, k_ref, kt_ref, v_ref, attnt_ref, dot_ref, prob_ref, inv_ref,
    dq_ref, dk_ref, dv_ref, sum_ref, diag_ref, dka_ref, dva_ref, *work_refs, heads, feat, length,
):
    seq, block = pl.program_id(0), pl.program_id(1)
    start = block * BQ
    row = 64
    many = len(work_refs) // 2
    dprob_refs, ds_refs = work_refs[:many], work_refs[many:]

    @pl.when(jnp.logical_and(seq == 0, block == 0))
    def _():
        diag_ref[...] = jnp.zeros_like(diag_ref)

    @pl.when(block == 0)
    def _():
        dka_ref[...] = jnp.zeros_like(dka_ref)
        dva_ref[...] = jnp.zeros_like(dva_ref)

    def work(low, width):
        keys = pl.ds(low, width)
        bases = [low - start + length - (j + 1) * STEP for j in range(BQ // STEP)]
        dvals, dqs, dkeys = [], [], []

        def begin(head):
            lanes = slice(head // 2 * 2 * feat, (head // 2 + 1) * 2 * feat)
            feats = slice(head * feat, (head + 1) * feat)
            scaled = dot_ref[feats, :].astype(F32) * inv_ref[0, head : head + 1, :]
            delta = jnp.sum(scaled * attnt_ref[feats, :].astype(F32), axis=0, keepdims=True)
            scaled = scaled.astype(BF)
            blank = jnp.zeros_like(scaled)
            padded = jnp.concatenate([blank, scaled] if head % 2 else [scaled, blank], axis=0)
            dprob_refs[head % many][:width] = mm(v_ref[keys, lanes], padded)
            dvals.append(mm(prob_ref[0, 0, head, keys, :], padded, NT))
            if head % 2:
                dva_ref[keys, lanes] += dvals[-2] + dvals[-1]
            return delta

        def middle(head, delta):
            dprob, ds = dprob_refs[head % many], ds_refs[head % many]
            for at in range(0, width, row):
                prob = prob_ref[0, 0, head, pl.ds(pl.multiple_of(low + at, row), row), :]
                value = prob.astype(F32) * (dprob[at : at + row] - delta)
                ds[at : at + row] = value.astype(BF)
                for j, base in enumerate(bases):
                    diag_ref[head, pl.ds(pl.multiple_of(base + at, row), row), :] += value[:, j * STEP : (j + 1) * STEP]

        def end(head):
            lanes = slice(head // 2 * 2 * feat, (head // 2 + 1) * 2 * feat)
            ds = ds_refs[head % many]
            dkey = mm(ds[:width], half_of(q_ref[:, lanes], head % 2, feat))
            dkeys.append(dkey)
            dqs.append(mm(kt_ref[head * feat : (head + 1) * feat, keys], ds[:width]))
            if head % 2:
                dka_ref[keys, lanes] += dkeys[-2] + dkeys[-1]
                dq_ref[:, lanes] = jnp.concatenate(dqs[-2:], axis=0).T.astype(BF)

        delta = begin(0)
        for head in range(heads):
            following = begin(head + 1) if head + 1 < heads else None
            middle(head, delta)
            if head:
                end(head - 1)
            delta = following
        end(heads - 1)

    by_width(low_ref, width_ref, length, work)

    @pl.when(block == pl.num_programs(1) - 1)
    def _():
        dk_ref[...] = dka_ref[...].astype(BF)
        dv_ref[...] = dva_ref[...].astype(BF)

    @pl.when(jnp.logical_and(seq == pl.num_programs(0) - 1, block == pl.num_programs(1) - 1))
    def _():
        for head in range(heads):
            sum_ref[head : head + 1, :] = unskew(diag_ref[head])


def attend_back(low, width, q, k, kt, v, attnt, dot, prob, inv, length, group):
    rows = q.shape[0]
    part = q.shape[1] // inv.shape[0]
    heads = inv.shape[1]
    feat = part // heads
    seqs, blocks = rows // length, length // BQ
    at = lambda s, b, *_: (s * blocks + b, group)
    whole = lambda s, b, *_: (s, group)
    at_t = lambda s, b, *_: (group, s * blocks + b)
    out = lambda s, b, *_: (s, 0)
    return pl.pallas_call(
        functools.partial(attend_back_kernel, heads=heads, feat=feat, length=length),
        grid_spec=pltpu.PrefetchScalarGridSpec(
            num_scalar_prefetch=2,
            grid=(seqs, blocks),
            in_specs=[
                pl.BlockSpec((BQ, part), at),
                pl.BlockSpec((length, part), whole),
                pl.BlockSpec((part, length), lambda s, b, *_: (group, s)),
                pl.BlockSpec((length, part), whole),
                pl.BlockSpec((part, BQ), at_t),
                pl.BlockSpec((part, BQ), at_t),
                pl.BlockSpec((1, 1, heads, length, BQ), lambda s, b, *_: (s, b, group, 0, 0)),
                pl.BlockSpec((1, heads, BQ), lambda s, b, *_: (group, 0, s * blocks + b)),
            ],
            out_specs=[
                pl.BlockSpec((BQ, part), lambda s, b, *_: (s * blocks + b, 0)),
                pl.BlockSpec((length, part), out),
                pl.BlockSpec((length, part), out),
                pl.BlockSpec((heads, 2 * length), lambda s, b, *_: (0, 0)),
            ],
            scratch_shapes=[
                pltpu.VMEM((heads, 2 * length - STEP, STEP), F32),
                pltpu.VMEM((length, part), F32),
                pltpu.VMEM((length, part), F32),
            ]
            + [pltpu.VMEM((length, BQ), F32)] * 2
            + [pltpu.VMEM((length, BQ), BF)] * 2,
        ),
        out_shape=[S((rows, part), BF)] * 3 + [S((heads, 2 * length), F32)],
        name="attend_back",
        cost_estimate=cost(32 * rows * length * part, 2 * rows * heads * length),
        compiler_params=PARAMS,
    )(low, width, q, k, kt, v, attnt, dot, prob, inv)


def key_ranges(seg):
    firsts, lasts = seg[:, ::BQ], seg[:, BQ - 1 :: BQ]
    low = jnp.sum((seg[:, None, :] < firsts[:, :, None]).astype(jnp.int32), axis=-1)
    high = jnp.sum((seg[:, None, :] <= lasts[:, :, None]).astype(jnp.int32), axis=-1)
    low = low // STEP
    width = (high + STEP - 1) // STEP - low
    return (low * STEP).reshape(-1), width.reshape(-1)


def ffn_kernel(me_ref, x_ref, up_ref, gain_ref, *refs, chunk, count, groups):
    attns, refs = refs[:groups], refs[groups:]
    pieces, refs = refs[:count], refs[count:]
    (states_ref, dx2_ref, dot_ref, da_ref, h2t_ref, h3t_ref, dbt_ref, hid_ref, dpre_ref,
     slope_ref, wo_ref, wi_ref, wb_ref, we_ref, sems) = refs
    width, wide = wi_ref.shape
    embed = we_ref.shape[1]

    @pl.when(pl.program_id(0) == 0)
    def _():
        me, rows = me_ref[0], pieces[0].shape[0]
        copies = placing(me, pieces, wo_ref, slice(0, width))
        copies += placing(me, pieces, wi_ref, slice(width, width + wide))
        copies += placing(me, pieces, we_ref, slice(width + wide, width + wide + embed))
        parts = wide // width
        for k, piece in enumerate(pieces):
            for q in range(parts):
                at = width + wide + embed + q * width
                spot = pl.ds(place(me, k, parts * rows) + q * rows, rows)
                copies.append((piece.at[:, at : at + width], wb_ref.at[spot, :]))
        run_copies(copies, sems)

    g_two, g_three = gain_ref[0:1, :], gain_ref[1:2, :]
    attn = jnp.concatenate([a[...] for a in attns], axis=1)
    x2 = x_ref[...].astype(F32) + mm(attn, wo_ref[...])
    scale2 = norm_scale(x2)
    h2 = (x2 * scale2 * g_two).astype(BF)
    x3 = x2
    for at in range(0, wide, chunk):
        cols = slice(at, at + chunk)
        hidden, slope = gelu_parts(mm(h2, wi_ref[:, cols]))
        hidden = hidden.astype(BF)
        hid_ref[:, cols] = hidden
        slope_ref[:, cols] = slope.astype(BF)
        x3 = x3 + mm(hidden, wb_ref[cols, :])
    scale3 = norm_scale(x3)
    h3 = (x3 * scale3 * g_three).astype(BF)
    states_ref[...] = mm(h3, we_ref[...])
    dx3 = norm_back(mm(up_ref[...], we_ref[...], NT), x3, scale3, g_three)
    db = dx3.astype(BF)
    dh2 = None
    for at in range(0, wide, chunk):
        cols = slice(at, at + chunk)
        dpre = (mm(db, wb_ref[cols, :], NT) * slope_ref[:, cols].astype(F32)).astype(BF)
        dpre_ref[:, cols] = dpre
        part = mm(dpre, wi_ref[:, cols], NT)
        dh2 = part if dh2 is None else dh2 + part
    part = norm_back(dh2, x2, scale2, g_two)
    dx2 = dx3 + part
    da = dx2.astype(BF)
    dx2_ref[...] = dx2
    da_ref[...] = da
    dot_ref[...] = mm(wo_ref[...], da, NT).astype(BF)
    h2t_ref[...] = h2.T
    h3t_ref[...] = h3.T
    dbt_ref[...] = db.T


def feed_forward(me, x, attns, up, gains, pieces, block=256, chunk=768):
    rows, width = x.shape
    count = len(pieces)
    embed = up.shape[1]
    wide = (pieces[0].shape[1] - width - embed) // 2
    fixed = lambda i, *_: (0, 0)
    natural = lambda cols: pl.BlockSpec((block, cols), lambda i, *_: (i, 0))
    turned = pl.BlockSpec((width, block), lambda i, *_: (0, i))
    return pl.pallas_call(
        functools.partial(ffn_kernel, chunk=chunk, count=count, groups=len(attns)),
        grid_spec=pltpu.PrefetchScalarGridSpec(
            num_scalar_prefetch=1,
            grid=(rows // block,),
            in_specs=[natural(width), natural(embed), pl.BlockSpec(gains.shape, fixed)]
            + [natural(a.shape[1]) for a in attns]
            + [ANY] * len(pieces),
            out_specs=[
                natural(embed), natural(width), turned, natural(width), turned, turned, turned,
                natural(wide), natural(wide),
            ],
            scratch_shapes=[
                pltpu.VMEM((block, wide), BF),
                pltpu.VMEM((width, width), BF),
                pltpu.VMEM((width, wide), BF),
                pltpu.VMEM((wide, width), BF),
                pltpu.VMEM((width, embed), BF),
                pltpu.SemaphoreType.DMA((count * (3 + wide // width),)),
            ],
        ),
        out_shape=[
            S((rows, embed), F32), S((rows, width), F32), S((width, rows), BF), S((rows, width), BF),
            S((width, rows), BF), S((width, rows), BF), S((width, rows), BF),
            S((rows, wide), BF), S((rows, wide), BF),
        ],
        name="feed_forward",
        cost_estimate=cost(4 * rows * width * (4 * wide + 2 * width), 20 * rows * wide, 2 * rows * wide),
        compiler_params=PARAMS,
    )(me, x, up, gains, *attns, *pieces)


def input_back_kernel(me_ref, x_ref, dx2_ref, gain_ref, *refs, spans, count, threaded):
    groups = len(spans)
    parts, refs = refs[: 3 * groups], refs[3 * groups :]
    pieces, refs = refs[: groups * count], refs[groups * count + threaded :]
    out_ref, weight_ref, sems = refs

    @pl.when(pl.program_id(0) == 0)
    def _():
        copies = []
        for g, lanes in enumerate(spans):
            copies += placing(me_ref[0], pieces[g * count : (g + 1) * count], weight_ref.at[g], lanes)
        run_copies(copies, sems)

    value = x_ref[...].astype(F32)
    scale = norm_scale(value)
    dh = None
    for g in range(groups):
        term = mm(jnp.concatenate([p[...] for p in parts[3 * g : 3 * g + 3]], axis=1), weight_ref[g], NT)
        dh = term if dh is None else dh + term
    out_ref[...] = dx2_ref[...] + norm_back(dh, value, scale, gain_ref[...])


def input_back(me, x, dx2, gain, parts, pieces, spans, first, steps, held, block=256):
    rows, width = x.shape
    natural = lambda cols: pl.BlockSpec((block, cols), lambda i, *_: (i + first, 0))
    fixed = lambda i, *_: (0, 0)
    operands = [me, x, dx2, gain, *parts, *pieces] + ([] if held is None else [held])
    return pl.pallas_call(
        functools.partial(
            input_back_kernel, spans=spans, count=len(pieces) // len(spans), threaded=0 if held is None else 1
        ),
        grid_spec=pltpu.PrefetchScalarGridSpec(
            num_scalar_prefetch=1,
            grid=(steps,),
            in_specs=[natural(width), natural(width), pl.BlockSpec((1, width), fixed)]
            + [natural(p.shape[1]) for p in parts]
            + [ANY] * (len(pieces) + (held is not None)),
            out_specs=natural(width),
            scratch_shapes=[
                pltpu.VMEM((len(spans), width, 3 * parts[0].shape[1]), BF),
                pltpu.SemaphoreType.DMA((len(pieces),)),
            ],
        ),
        out_shape=S((rows, width), F32),
        input_output_aliases={} if held is None else {len(operands) - 1: 0},
        name="input_back",
        cost_estimate=cost(6 * steps * block * width * width, 16 * steps * block * width),
        compiler_params=PARAMS,
    )(*operands)


def grad_rows_kernel(me_ref, *refs, count, lefts):
    lefts, rights, (keep_ref, send_ref, full_ref) = refs[:lefts], refs[lefts:-3], refs[-3:]
    rows = full_ref.shape[0] // count
    down = 0
    for left in lefts:
        at = 0
        for right in rights:
            cols = slice(at, at + right.shape[1])
            at += right.shape[1]
            full_ref[down : down + left.shape[0], cols] = mm(left[...], right[...])
        down += left.shape[0]
    for k in range(count):
        spot = pl.ds(pl.multiple_of(jnp.bitwise_xor(me_ref[0], k) * rows, 16), rows)
        (send_ref if k & 1 else keep_ref)[k >> 1] = full_ref[spot, :].astype(BF)


def grad_rows(me, lefts, rights, count, tile=768, first=0, tiles=None):
    m, rows = sum(left.shape[0] for left in lefts), lefts[0].shape[1]
    if len(rights) > 1:
        tile, tiles = sum(r.shape[1] for r in rights), 1
        specs = [pl.BlockSpec(r.shape, lambda j, *_: (0, 0)) for r in rights]
    else:
        tile = min(tile, rights[0].shape[1])
        tiles = rights[0].shape[1] // tile if tiles is None else tiles
        specs = [pl.BlockSpec((rows, tile), lambda j, *_: (0, j + first))]
    out = pl.BlockSpec((count // 2, m // count, tile), lambda j, *_: (0, 0, j))
    shape = S((count // 2, m // count, tile * tiles), BF)
    return pl.pallas_call(
        functools.partial(grad_rows_kernel, count=count, lefts=len(lefts)),
        grid_spec=pltpu.PrefetchScalarGridSpec(
            num_scalar_prefetch=1,
            grid=(tiles,),
            in_specs=[pl.BlockSpec(left.shape, lambda j, *_: (0, 0), pipeline_mode=pl.Buffered(1)) for left in lefts]
            + specs,
            out_specs=[out, out],
            scratch_shapes=[pltpu.VMEM((m, tile), F32)],
        ),
        out_shape=[shape, shape],
        name="weight_grad",
        cost_estimate=cost(2 * m * rows * tile * tiles, 2 * rows * (m + tile * tiles)),
        compiler_params=PARAMS,
    )(me, *lefts, *rights)


def grad_set_kernel(me_ref, *refs, shapes, count, extra):
    operands = sum(a + b for a, b in shapes)
    sources, refs = refs[:operands], refs[operands:]
    if extra:
        (sums_ref, hot_ref), refs, table_ref = refs[:2], refs[2:-1], refs[-1]
    keep_ref, send_ref, full_ref = refs[:3]
    held, sems = refs[3:-1], refs[-1]
    copies = [pltpu.make_async_copy(a, b, sems.at[i]) for i, (a, b) in enumerate(zip(sources, held))]
    for copy in copies:
        copy.start()
    rows = full_ref.shape[0] // count
    index = at = 0
    for lefts, rights in shapes:
        left = held[index : index + lefts]
        right = held[index + lefts : index + lefts + rights]
        for copy in copies[index : index + lefts]:
            copy.wait()
        for n, r in enumerate(right):
            copies[index + lefts + n].wait()
            down = 0
            for part in left:
                full_ref[down : down + part.shape[0], at : at + r.shape[1]] = mm(part[...], r[...])
                down += part.shape[0]
            at += r.shape[1]
        index += lefts + rights
    if extra:
        sums = sums_ref[...]
        high = sums.astype(BF)
        rest = (sums - high.astype(F32)).astype(BF)
        table_ref[...] = jnp.zeros_like(table_ref)
        table_ref[:, : sums.shape[0]] = mm(hot_ref[...], high, NT) + mm(hot_ref[...], rest, NT)
        each = table_ref.shape[0] // count
    for k in range(count):
        target = send_ref if k & 1 else keep_ref
        target[k >> 1, :, :at] = full_ref[pl.ds(place(me_ref[0], k, rows), rows), :].astype(BF)
        if extra:
            target[k >> 1, :, at:] = jnp.zeros((rows, STEP), BF)
            own = pl.ds(jnp.bitwise_xor(me_ref[0], k) * each, each)
            target[k >> 1, :each, at:] = table_ref[own, :].astype(BF)


def grad_set(me, jobs, count, extra=None):
    operands = [x for lefts, rights in jobs for x in lefts + rights]
    m, rows = sum(x.shape[0] for x in jobs[0][0]), jobs[0][0][0].shape[1]
    n = sum(r.shape[1] for _, rights in jobs for r in rights)
    wide = n + (0 if extra is None else STEP)
    shape = S((count // 2, m // count, wide), BF)
    out = pl.BlockSpec(shape.shape, lambda j, *_: (0, 0, 0))
    more = [] if extra is None else list(extra)
    return pl.pallas_call(
        functools.partial(
            grad_set_kernel,
            shapes=tuple((len(a), len(b)) for a, b in jobs),
            count=count,
            extra=extra is not None,
        ),
        grid_spec=pltpu.PrefetchScalarGridSpec(
            num_scalar_prefetch=1,
            grid=(1,),
            in_specs=[ANY] * len(operands) + [pl.BlockSpec(e.shape, lambda j, *_: (0, 0)) for e in more],
            out_specs=[out, out],
            scratch_shapes=[pltpu.VMEM((m, n), F32)]
            + [pltpu.VMEM(x.shape, BF) for x in operands]
            + [pltpu.SemaphoreType.DMA((len(operands),))]
            + ([pltpu.VMEM((extra[1].shape[0], STEP), F32)] if more else []),
        ),
        out_shape=[shape, shape],
        name="weight_grads",
        cost_estimate=cost(2 * m * rows * n, 2 * rows * (m + n)),
        compiler_params=PARAMS,
    )(me, *operands, *more)


def grad_cols_kernel(me_ref, left_ref, right_ref, out_ref):
    out_ref[0] = mm(left_ref[...], right_ref[...]).astype(BF).T


def grad_cols(me, left, right, count, odd, tile=768):
    m, rows = left.shape
    n = right.shape[1]
    part = n // count
    if part % STEP:
        full = lax.dot_general(right, left, (((0,), (1,)), ((), ())), preferred_element_type=F32).astype(BF)
        return jnp.stack(
            [lax.dynamic_slice_in_dim(full, (me[0] ^ k) * part, part, 0) for k in range(odd, count, 2)]
        )
    tile = min(tile, part)
    inner = part // tile
    return pl.pallas_call(
        grad_cols_kernel,
        grid_spec=pltpu.PrefetchScalarGridSpec(
            num_scalar_prefetch=1,
            grid=(count // 2, inner),
            in_specs=[
                pl.BlockSpec((m, rows), lambda k, t, me: (0, 0), pipeline_mode=pl.Buffered(1)),
                pl.BlockSpec((rows, tile), lambda k, t, me: (0, jnp.bitwise_xor(me[0], 2 * k + odd) * inner + t)),
            ],
            out_specs=pl.BlockSpec((1, tile, m), lambda k, t, me: (k, t, 0)),
        ),
        out_shape=S((count // 2, part, m), BF),
        name="weight_grad",
        cost_estimate=cost(m * rows * n, rows * (2 * m + n)),
        compiler_params=PARAMS,
    )(me, left, right)


def bits_of(axis):
    size = lax.axis_size(axis)
    count = size.bit_length() - 1
    assert size == 1 << count
    return count


def swap(value, axis, mask):
    size = lax.axis_size(axis)
    return lax.ppermute(value, axis, [(i, i ^ mask) for i in range(size)])


def gathering(shard):
    held = {0: shard}
    for bit in reversed(range(1, bits_of("fsdp"))):
        step = 1 << bit
        sent = yield list(held.values())
        held.update({k ^ step: swap(v, "fsdp", step) for k, v in zip(list(held), sent)})
    (own,) = yield [shard]
    others = [k for k in held if k]
    first = swap(own, "fsdp", 1)
    sent = yield [held[k] for k in others]
    held.update({k ^ 1: swap(v, "fsdp", 1) for k, v in zip(others, sent)})
    held[1] = first
    return [held[k] for k in range(len(held))]


def reorder(parts, index):
    parts = list(parts)
    for bit in range(len(parts).bit_length() - 1):
        flag = (index >> bit) & 1
        parts = [jnp.where(flag == 1, parts[k ^ (1 << bit)], parts[k]) for k in range(len(parts))]
    return parts


def summing(keep, send, late=False):
    (sent,) = yield [send]
    got = swap(sent, "fsdp", 1)
    if late:
        (got,) = yield [got]
        (keep,) = keep
    part = {2 * k: keep[k].astype(F32) + got[k].astype(F32) for k in range(keep.shape[0])}
    for bit in range(1, bits_of("fsdp")):
        step = 1 << bit
        away = [k for k in part if k & step]
        if late:
            half = part[0].shape[0] // 2
            sent = yield [part[k][:half].astype(BF) for k in away]
            top = [swap(s, "fsdp", step) for s in sent]
            sent = yield [part[k][half:].astype(BF) for k in away] + top
            bottom = [swap(s, "fsdp", step) for s in sent[: len(away)]]
            arrived = [jnp.concatenate(pair, axis=0) for pair in zip(sent[len(away) :], bottom)]
        else:
            sent = yield [part[k].astype(BF) for k in away]
            arrived = [swap(s, "fsdp", step) for s in sent]
        got = {k ^ step: g for k, g in zip(away, arrived)}
        part = {k: part[k] + got[k].astype(F32) for k in got}
    value = part[0]
    side = lax.axis_index("grp") & 1
    size = value.shape[1] // 2
    (sent,) = yield [lax.dynamic_slice_in_dim(value, (1 - side) * size, size, 1).astype(BF)]
    return lax.dynamic_slice_in_dim(value, side * size, size, 1) + swap(sent, "grp", 1).astype(F32)


def completing(values, split=False):
    me = lax.axis_index("grp")
    side, line = me & 1, me >> 1
    depth = lax.axis_size("grp") // 2
    value = values[0] if len(values) == 1 else jnp.concatenate(values, axis=1)
    rows = value.shape[0] // depth
    block = lambda k: lax.dynamic_slice_in_dim(value, (line ^ k) * rows, rows, 0)
    sent = yield [block(k).astype(BF) for k in range(1, depth)]
    total = block(0)
    for k, s in zip(range(1, depth), sent):
        total = total + swap(s, "grp", 2 * k).astype(F32)
    (total,) = yield [total.astype(BF)]
    got = [total] + [swap(total, "grp", 2 * k) for k in range(1, depth)]
    if split:
        got = yield got
    got = reorder(got, line)
    if split:
        half = total.shape[1] // 2
        left, right = (jnp.concatenate([g[:, c] for g in got], axis=0) for c in (slice(0, half), slice(half, None)))
        (left,) = yield [left]
        first = swap(left, "grp", 1)
        (right, first) = yield [right, first]
        mine = jnp.concatenate([left, right], axis=1)
        other = jnp.concatenate([first, swap(right, "grp", 1)], axis=1)
    else:
        (mine,) = yield [jnp.concatenate(got, axis=0)]
        other = swap(mine, "grp", 1)
    results, at = [], 0
    for v in values:
        cols = slice(at, at + v.shape[1])
        at += v.shape[1]
        a, b = mine[:, cols].astype(F32), other[:, cols].astype(F32)
        results.append(jnp.concatenate([jnp.where(side == 0, a, b), jnp.where(side == 0, b, a)], axis=1))
    return results


class Flow:
    def __init__(self, stages):
        self.stages, self.ready, self.result = stages, next(stages), None

    def send(self, operands):
        try:
            self.ready = self.stages.send(operands)
        except StopIteration as done:
            self.ready, self.result = None, done.value


def depart(anchor, flows, after=(), hold=()):
    flows = [f for f in flows if f.ready is not None]
    operands = [x for f in flows for x in f.ready]
    kept = tuple(f.result if f.ready is None else f.ready for f in hold)
    anchor, operands, kept, _ = lax.optimization_barrier((anchor, tuple(operands), kept, tuple(after)))
    for f, k in zip(hold, kept):
        if f.ready is None:
            f.result = k
        else:
            f.ready = k
    operands = list(operands)
    for f in flows:
        count = len(f.ready)
        f.send(operands[:count])
        operands = operands[count:]
    return anchor


class Held:
    def __init__(self, value):
        self.ready, self.result = None, value


def then_complete(flows):
    return Flow(completing([finish(f) for f in flows]))


def finish(flow):
    while flow.ready is not None:
        flow.send(flow.ready)
    return flow.result


def total_small(value):
    for axis in ("fsdp", "grp"):
        size = lax.axis_size(axis)
        others = [swap(value, axis, k) for k in range(1, size)]
        for other in others:
            value = value + other
    return value


def body(
    layer_input,
    segment_ids,
    bucket_table,
    gain_attn,
    weight_query,
    weight_key,
    weight_value,
    weight_out,
    gain_ffn,
    weight_in,
    weight_back,
    gain_final,
    weight_embed,
    bias_table,
    cotangent,
):
    micro, length, width = layer_input.shape
    heads = bias_table.shape[1]
    size = lax.axis_size("fsdp")
    index = lax.axis_index("fsdp")
    me = index.astype(jnp.int32).reshape(1)
    buckets = bias_table.shape[0] * size
    rows = micro * length
    groups = GROUPS

    part = width // size
    span = width // groups
    own_rows = slice(0, part)
    near = Flow(
        gathering(
            pack(
                [weight_query, weight_key, weight_value],
                [(w, own_rows, slice(g * span, (g + 1) * span)) for g in range(groups) for w in range(3)],
            )
        )
    )
    link = depart(me, [near])
    full = lambda w: (own_rows, slice(0, w.shape[1]))
    far = Flow(
        gathering(
            pack(
                [weight_out, weight_in, weight_embed, weight_back],
                [(0, *full(weight_out)), (1, *full(weight_in)), (2, *full(weight_embed))]
                + [
                    (3, slice(q * part, (q + 1) * part), slice(0, width))
                    for q in range(weight_back.shape[0] // part)
                ],
            )
        )
    )
    small = jnp.concatenate([gain_attn, gain_ffn, gain_final, bias_table.reshape(-1)]).reshape(1, -1)
    small = finish(Flow(gathering(small)))
    small = jnp.concatenate(reorder(small, index), axis=0)
    g_one, g_two, g_three = (
        small[:, k * part : (k + 1) * part].reshape(1, width).astype(F32) for k in range(3)
    )
    table = small[:, 3 * part :].reshape(buckets, heads)

    link = depart(link, [near])

    onehot = (bucket_table[:, None] == lax.iota(jnp.int32, buckets)[None, :]).astype(BF)
    bias_rows = lax.dot_general(table, onehot, (((0,), (1,)), ((), ())), preferred_element_type=F32)
    low, wide = key_ranges(segment_ids)
    seg_col = segment_ids.reshape(rows, 1)
    seg_row = segment_ids.reshape(rows // BQ, 1, BQ)
    gains = jnp.concatenate([g_two, g_three], axis=0)
    bias_rows, low, wide, seg_col, seg_row, gains, g_one = lax.optimization_barrier(
        (bias_rows, low, wide, seg_col, seg_row, gains, g_one)
    )
    strips = bias_strips(bias_rows)

    x = layer_input.reshape(rows, width)
    upstream = cotangent.reshape(rows, -1)
    turn = depart(link, [near, far], [strips])
    near = finish(near)
    query, key, value, key_t, value_t, h1_t = project(turn, x, g_one, near, groups)
    start = depart(low, [far], [query])
    attn, attn_t, probs, inverse = attend(
        start, wide, query, key, value_t, strips, seg_col, seg_row, length, groups
    )
    turn = depart(me, [far], [inverse])
    far = finish(far)
    states, dx2, dattn_t, da, h2_t, h3_t, db_t, hidden, dpre = feed_forward(
        turn, x, [attn], upstream, gains, far
    )

    back_send = grad_cols(me, db_t, hidden, size, 1)
    back_keep = []
    back = Flow(summing(back_keep, back_send, True))
    turn = depart(me, [back])
    back_keep.append(grad_cols(turn, db_t, hidden, size, 0))
    turn = depart(me, [back], back_keep)
    turn = depart(turn, [back])
    inner = Flow(summing(*grad_rows(turn, [h2_t], [dpre], size)))

    def back_of(turn, g):
        return attend_back(
            turn, wide, query, key, key_t, value, attn_t, dattn_t, probs, inverse, length, g
        )

    def project_grad(turn, parts, extra=None):
        return Flow(summing(*grad_set(turn, [([h1_t], list(parts[:3]))], size, extra)))

    turn = depart(turn, [inner, back])
    out = grad_set(turn, [([attn_t], [da]), ([h3_t], [upstream])], size)
    turn = depart(low, [inner, back], [out[0]])
    grads = [back_of(turn, 0)]
    out = Flow(summing(*out))
    turn = depart(me, [out], [grads[0][3]] + inner.ready)
    first = project_grad(turn, grads[0])
    turn = depart(low, [inner, out, first], [finish(back)])
    grads.append(back_of(turn, 1))
    turn = depart(me, [out, first], [grads[1][3]])
    second = project_grad(turn, grads[1])
    fold = back.result.shape[0] // finish(inner).shape[0]
    turned = jnp.concatenate(jnp.split(back.result, fold, axis=0), axis=1)
    wide_flow = Flow(completing([inner.result, turned], True))
    finish(out)
    turn = depart(low, [wide_flow, first, second], hold=[out])
    grads.append(back_of(turn, 2))
    finish(first)
    turn = depart(me, [wide_flow, second], [grads[2][3]], [first])
    third = project_grad(turn, grads[2], (jnp.concatenate([g[3] for g in grads], axis=0), onehot.T))

    pieces = near * groups
    spans = [slice(3 * span * g, 3 * span * (g + 1)) for g in range(groups)]
    dparts = [p for g in grads for p in g[:3]]
    blocks = rows // 256
    cuts = (blocks - 2 * (blocks // 3), blocks // 3, blocks // 3)
    turn = depart(me, [second, third])
    d_input = input_back(turn, x, dx2, g_one, dparts, pieces, spans, 0, cuts[0], None)
    joint = then_complete([out, first, second])
    d_input = Held(d_input)
    turn = depart(me, [wide_flow], hold=[d_input])
    turn = depart(turn, [wide_flow, third, joint])
    d_input = Held(
        input_back(turn, x, dx2, g_one, dparts, pieces, spans, cuts[0], cuts[1], d_input.result)
    )
    turn = depart(me, [wide_flow, third, joint], hold=[d_input])
    d_input = Held(
        input_back(turn, x, dx2, g_one, dparts, pieces, spans, cuts[0] + cuts[1], cuts[2], d_input.result)
    )
    last = then_complete([third])
    finish(wide_flow)
    depart(me, [joint, last], hold=[d_input, wide_flow])
    g_in, g_back = wide_flow.result
    cut = g_back.shape[1] // fold // 2
    g_back = jnp.concatenate(
        [
            jnp.concatenate([g_back[:, (h * fold + q) * cut : (h * fold + q + 1) * cut] for h in range(2)], axis=1)
            for q in range(fold)
        ],
        axis=0,
    )
    g_oe, *proj = finish(joint) + finish(last)
    g_out, g_embed = g_oe[:, :width], g_oe[:, width:]
    grad_q, grad_k, grad_v = (
        jnp.concatenate([p[:, k * span : (k + 1) * span] for p in proj], axis=1) for k in range(3)
    )
    g_table = proj[-1][: buckets // size, width : width + heads]

    def gain_grad(gain, *pairs):
        return sum(jnp.sum(w.astype(F32) * g, axis=1) for w, g in pairs) / gain.astype(F32)

    gain_grads = (
        gain_grad(
            gain_attn,
            *((near[0][:, 3 * span * g : 3 * span * (g + 1)], p[:, : 3 * span]) for g, p in enumerate(proj)),
        ),
        gain_grad(gain_ffn, (weight_in, g_in)),
        gain_grad(gain_final, (weight_embed, g_embed)),
    )
    return (
        states.reshape(micro, length, -1),
        d_input.result.reshape(micro, length, width),
        gain_grads[0],
        grad_q,
        grad_k,
        grad_v,
        g_out,
        gain_grads[1],
        g_in,
        g_back,
        gain_grads[2],
        g_embed,
        g_table,
    )


GROUPS = 3


def solution(mesh):
    placed = (
        P(None, ("grp", "fsdp"), None),
        P(None, ("grp", "fsdp")),
        P(),
        P("fsdp"),
        P("fsdp", None),
        P("fsdp", None),
        P("fsdp", None),
        P("fsdp", None),
        P("fsdp"),
        P("fsdp", None),
        P("fsdp", None),
        P("fsdp"),
        P("fsdp", None),
        P("fsdp", None),
        P(None, ("grp", "fsdp"), None),
    )
    return jax.shard_map(
        body,
        mesh=mesh,
        in_specs=placed,
        out_specs=(
            P(None, ("grp", "fsdp"), None),
            P(None, ("grp", "fsdp"), None),
            P("fsdp"),
            P("fsdp", None),
            P("fsdp", None),
            P("fsdp", None),
            P("fsdp", None),
            P("fsdp"),
            P("fsdp", None),
            P("fsdp", None),
            P("fsdp"),
            P("fsdp", None),
            P("fsdp", None),
        ),
        check_vma=False,
    )
```

```python
import functools
import jax
import jax.numpy as jnp
from jax import lax
from jax.experimental import pallas as pl
from jax.experimental.pallas import tpu as pltpu
from jax.sharding import PartitionSpec as P

BQ = 256
STEP = 128
NEGATIVE = -1e30
VMEM_CAP = 60 * 1024 * 1024
EPS = 1e-06
INV_ROOT_TWO_PI = 0.3989422804014327
BF = jnp.bfloat16
F32 = jnp.float32
NT = (((1,), (1,)), ((), ()))
NN = (((1,), (0,)), ((), ()))
S = jax.ShapeDtypeStruct
ANY = pl.BlockSpec(memory_space=pl.ANY)
PARAMS = pltpu.CompilerParams(vmem_limit_bytes=VMEM_CAP)


def cost(flops, moved, special=0):
    return pl.CostEstimate(flops=flops // 16, bytes_accessed=moved // 16, transcendentals=special // 16)


def mm(a, b, dims=NN):
    return lax.dot_general(a, b, dims, preferred_element_type=F32)


def norm_scale(value):
    return lax.rsqrt(jnp.mean(value * value, axis=-1, keepdims=True) + EPS)


def norm_back(grad, value, scale, gain):
    weighted = grad * gain
    inner = jnp.mean(weighted * value, axis=-1, keepdims=True)
    dvalue = scale * weighted - value * (scale * scale * scale) * inner
    return dvalue


def gelu_parts(value):
    t = 1.0 / (1.0 + (0.3275911 * 0.7071067811865476) * jnp.abs(value))
    poly = 0.5307027145
    for factor in (-0.7265760135, 0.7107068705, -0.142248368, 0.127414796):
        poly = poly * t + factor
    bell = jnp.exp(-0.5 * value * value)
    tail = poly * t * bell
    cdf = jnp.where(value < 0.0, tail, 1.0 - tail)
    return value * cdf, cdf + value * bell * INV_ROOT_TWO_PI


def run_copies(jobs, sems):
    copies = [pltpu.make_async_copy(a, b, sems.at[i]) for i, (a, b) in enumerate(jobs)]
    for copy in copies:
        copy.start()
    for copy in copies:
        copy.wait()


def place(me, k, rows):
    return pl.multiple_of(jnp.bitwise_xor(me, k) * rows, 16)


def placing(me, pieces, target, lanes=slice(None)):
    rows = pieces[0].shape[0]
    return [
        (piece.at[:, lanes], target.at[pl.ds(place(me, k, rows), rows), :]) for k, piece in enumerate(pieces)
    ]


def pack_kernel(*refs, spots):
    sources, out_ref = refs[:-1], refs[-1]
    at = 0
    for index, rows, cols in spots:
        wide = cols.stop - cols.start
        out_ref[:, at : at + wide] = sources[index][rows, cols]
        at += wide


def pack(arrays, spots):
    rows = spots[0][1].stop - spots[0][1].start
    wide = sum(cols.stop - cols.start for _, _, cols in spots)
    return pl.pallas_call(
        functools.partial(pack_kernel, spots=tuple(spots)),
        out_shape=S((rows, wide), BF),
        name="pack",
        cost_estimate=cost(0, 4 * rows * wide),
        compiler_params=PARAMS,
    )(*arrays)


def project_kernel(me_ref, x_ref, gain_ref, *refs, count, groups):
    pieces, refs = refs[:count], refs[count:]
    q_ref, k_ref, v_ref, kt_ref, vt_ref, ht_ref, weight_ref, sems = refs

    @pl.when(pl.program_id(0) == 0)
    def _():
        run_copies(placing(me_ref[0], pieces, weight_ref), sems)

    value = x_ref[...].astype(F32)
    h = (value * norm_scale(value) * gain_ref[...]).astype(BF)
    ht_ref[...] = h.T
    part = h.shape[1] // groups
    for g in range(groups):
        cols = slice(g * part, (g + 1) * part)
        out = mm(h, weight_ref[:, 3 * g * part : 3 * (g + 1) * part]).astype(BF)
        q_ref[:, cols] = out[:, :part]
        k_ref[:, cols] = out[:, part : 2 * part]
        kt_ref[cols, :] = out[:, part : 2 * part].T
        v_ref[:, cols] = out[:, 2 * part :]
        vt_ref[cols, :] = out[:, 2 * part :].T


def project(me, x, gain, pieces, groups, block=256):
    rows, width = x.shape
    natural = pl.BlockSpec((block, width), lambda i, *_: (i, 0))
    turned = pl.BlockSpec((width, block), lambda i, *_: (0, i))
    return pl.pallas_call(
        functools.partial(project_kernel, count=len(pieces), groups=groups),
        grid_spec=pltpu.PrefetchScalarGridSpec(
            num_scalar_prefetch=1,
            grid=(rows // block,),
            in_specs=[natural, pl.BlockSpec((1, width), lambda i, *_: (0, 0))] + [ANY] * len(pieces),
            out_specs=[natural] * 3 + [turned] * 3,
            scratch_shapes=[pltpu.VMEM((width, 3 * width), BF), pltpu.SemaphoreType.DMA((len(pieces),))],
        ),
        out_shape=[S((rows, width), BF)] * 3 + [S((width, rows), BF)] * 3,
        name="project",
        cost_estimate=cost(6 * rows * width * width, 14 * rows * width),
        compiler_params=PARAMS,
    )(me, x, gain, *pieces)


def strip_kernel(rows_ref, strip_ref, *, length):
    rows = jnp.broadcast_to(rows_ref[0], (STEP, 2 * length))
    turned = pltpu.roll(rows, 2 * length - STEP, 1, stride=1, stride_axis=0)
    strip_ref[0] = turned[:, : 2 * length - STEP].T.astype(BF)


def bias_strips(rows):
    heads, twice = rows.shape
    return pl.pallas_call(
        functools.partial(strip_kernel, length=twice // 2),
        grid=(heads,),
        in_specs=[pl.BlockSpec((1, 1, twice), lambda h: (h, 0, 0))],
        out_specs=pl.BlockSpec((1, twice - STEP, STEP), lambda h: (h, 0, 0)),
        out_shape=S((heads, twice - STEP, STEP), BF),
        name="bias_strips",
        cost_estimate=cost(heads * twice * STEP * 20, heads * twice * STEP * 4),
        compiler_params=PARAMS,
    )(rows.reshape(heads, 1, twice))


def by_width(low_ref, width_ref, length, work):
    step = pl.program_id(0) * pl.num_programs(1) + pl.program_id(1)
    low = pl.multiple_of(low_ref[step], STEP)
    width = width_ref[step]
    for blocks in range(BQ // STEP, length // STEP + 1):

        @pl.when(width == blocks)
        def _(blocks=blocks):
            work(low, blocks * STEP)


def half_of(query, side, feat):
    left = lax.broadcasted_iota(jnp.int32, query.shape, 1) < feat
    return jnp.where(left if side == 0 else ~left, query, jnp.zeros_like(query))


def fold(value, combine):
    parts = [value[i : i + 8] for i in range(0, value.shape[0], 8)]
    while len(parts) > 1:
        parts = [combine(*parts[i : i + 2]) if i + 1 < len(parts) else parts[i] for i in range(0, len(parts), 2)]
    return parts[0]


def attend_kernel(
    low_ref, width_ref, q_ref, k_ref, vt_ref, strip_ref, sk_ref, sq_ref,
    attn_ref, attnt_ref, prob_ref, inv_ref, mask_ref, *score_refs, heads, feat, length, group,
):
    start = pl.program_id(1) * BQ
    row = 128

    def work(low, width):
        keys = pl.ds(low, width)
        mask_ref[:width] = jnp.where(sk_ref[keys, :] == sq_ref[0], 0.0, NEGATIVE).astype(BF)
        bases = [low - start + length - (j + 1) * STEP for j in range(BQ // STEP)]

        def one_group(g, carry):
            outs = []

            def lanes_of(head):
                return pl.ds(pl.multiple_of((g * group + head // 2 * 2) * feat, 2 * feat), 2 * feat)

            def score(head):
                lanes = lanes_of(head)
                score_refs[head % len(score_refs)][:width] = mm(
                    k_ref[keys, lanes], half_of(q_ref[:, lanes], head % 2, feat), NT
                )

            def weigh(head):
                ref = score_refs[head % len(score_refs)]
                whole = g * group + head
                top = None
                for at in range(0, width, row):
                    bias = jnp.concatenate(
                        [strip_ref[whole, pl.ds(pl.multiple_of(base + at, row), row), :] for base in bases], axis=1
                    )
                    value = ref[at : at + row] + (bias + mask_ref[at : at + row]).astype(F32)
                    ref[at : at + row] = value
                    value = fold(value, jnp.maximum)
                    top = value if top is None else jnp.maximum(top, value)
                top = jnp.max(top, axis=0, keepdims=True)
                total = None
                for at in range(0, width, row):
                    expo = jnp.exp(ref[at : at + row] - top)
                    prob_ref[0, 0, whole, pl.ds(pl.multiple_of(low + at, row), row), :] = expo.astype(BF)
                    expo = fold(expo, jnp.add)
                    total = expo if total is None else total + expo
                inverse = 1.0 / jnp.sum(total, axis=0, keepdims=True)
                inv_ref[g, head : head + 1, :] = inverse
                return inverse

            def gather(head, inverse):
                whole = g * group + head
                value = vt_ref[pl.ds(pl.multiple_of(whole * feat, feat), feat), keys]
                outs.append(mm(value, prob_ref[0, 0, whole, keys, :]) * inverse)
                if head % 2:
                    lanes = lanes_of(head)
                    both = jnp.concatenate(outs[-2:], axis=0)
                    attnt_ref[lanes, :] = both.astype(BF)
                    attn_ref[:, lanes] = both.T.astype(BF)

            score(0)
            last = None
            for head in range(group):
                if head + 1 < group:
                    score(head + 1)
                inverse = weigh(head)
                if last is not None:
                    gather(*last)
                last = (head, inverse)
            gather(*last)
            return carry

        lax.fori_loop(0, heads // group, one_group, 0)

    by_width(low_ref, width_ref, length, work)


def attend(low, width, q, k, vt, strips, sk, sq, length, groups):
    rows, part = q.shape
    heads = strips.shape[0]
    feat = part // heads
    seqs, blocks = rows // length, length // BQ
    at = lambda s, b, *_: (s * blocks + b, 0)
    whole = lambda s, b, *_: (s, 0)
    at_t = lambda s, b, *_: (0, s * blocks + b)
    return pl.pallas_call(
        functools.partial(attend_kernel, heads=heads, feat=feat, length=length, group=heads // groups),
        grid_spec=pltpu.PrefetchScalarGridSpec(
            num_scalar_prefetch=2,
            grid=(seqs, blocks),
            in_specs=[
                pl.BlockSpec((BQ, part), at),
                pl.BlockSpec((length, part), whole),
                pl.BlockSpec((part, length), lambda s, b, *_: (0, s)),
                pl.BlockSpec(strips.shape, lambda s, b, *_: (0, 0, 0), pipeline_mode=pl.Buffered(1)),
                pl.BlockSpec((length, 1), whole),
                pl.BlockSpec((1, 1, BQ), lambda s, b, *_: (s * blocks + b, 0, 0)),
            ],
            out_specs=[
                pl.BlockSpec((BQ, part), at),
                pl.BlockSpec((part, BQ), at_t),
                pl.BlockSpec((1, 1, heads, length, BQ), lambda s, b, *_: (s, b, 0, 0, 0)),
                pl.BlockSpec((groups, heads // groups, BQ), lambda s, b, *_: (0, 0, s * blocks + b)),
            ],
            scratch_shapes=[pltpu.VMEM((length, BQ), BF)] + [pltpu.VMEM((length, BQ), F32)] * 4,
        ),
        out_shape=[
            S((rows, part), BF),
            S((part, rows), BF),
            S((seqs, blocks, heads, length, BQ), BF),
            S((groups, heads // groups, rows), F32),
        ],
        name="attend",
        cost_estimate=cost(16 * rows * length * part, 2 * rows * heads * length, rows * heads * length),
        compiler_params=PARAMS,
    )(low, width, q, k, vt, strips, sk, sq)


def unskew(data):
    data = jnp.concatenate([data, jnp.zeros((STEP, STEP), F32)], axis=0)
    rows = lax.broadcasted_iota(jnp.int32, (STEP, STEP), 0)
    cols = lax.broadcasted_iota(jnp.int32, (STEP, STEP), 1)
    flip = (rows + cols == STEP - 1).astype(BF)
    high = data.astype(BF)
    low = (data - high.astype(F32)).astype(BF)
    turned = mm(flip, high, NT) + mm(flip, low, NT)
    return jnp.sum(pltpu.roll(turned, 1, 1, stride=1, stride_axis=0), axis=0, keepdims=True)


def attend_back_kernel(
    low_ref, width_ref, q_ref, k_ref, kt_ref, v_ref, attnt_ref, dot_ref, prob_ref, inv_ref,
    dq_ref, dk_ref, dv_ref, sum_ref, diag_ref, dka_ref, dva_ref, *work_refs, heads, feat, length,
):
    seq, block = pl.program_id(0), pl.program_id(1)
    start = block * BQ
    row = 64
    many = len(work_refs) // 2
    dprob_refs, ds_refs = work_refs[:many], work_refs[many:]

    @pl.when(jnp.logical_and(seq == 0, block == 0))
    def _():
        diag_ref[...] = jnp.zeros_like(diag_ref)

    @pl.when(block == 0)
    def _():
        dka_ref[...] = jnp.zeros_like(dka_ref)
        dva_ref[...] = jnp.zeros_like(dva_ref)

    def work(low, width):
        keys = pl.ds(low, width)
        bases = [low - start + length - (j + 1) * STEP for j in range(BQ // STEP)]
        dvals, dqs, dkeys = [], [], []

        def begin(head):
            lanes = slice(head // 2 * 2 * feat, (head // 2 + 1) * 2 * feat)
            feats = slice(head * feat, (head + 1) * feat)
            scaled = dot_ref[feats, :].astype(F32) * inv_ref[0, head : head + 1, :]
            delta = jnp.sum(scaled * attnt_ref[feats, :].astype(F32), axis=0, keepdims=True)
            scaled = scaled.astype(BF)
            blank = jnp.zeros_like(scaled)
            padded = jnp.concatenate([blank, scaled] if head % 2 else [scaled, blank], axis=0)
            dprob_refs[head % many][:width] = mm(v_ref[keys, lanes], padded)
            dvals.append(mm(prob_ref[0, 0, head, keys, :], padded, NT))
            if head % 2:
                dva_ref[keys, lanes] += dvals[-2] + dvals[-1]
            return delta

        def middle(head, delta):
            dprob, ds = dprob_refs[head % many], ds_refs[head % many]
            for at in range(0, width, row):
                prob = prob_ref[0, 0, head, pl.ds(pl.multiple_of(low + at, row), row), :]
                value = prob.astype(F32) * (dprob[at : at + row] - delta)
                ds[at : at + row] = value.astype(BF)
                for j, base in enumerate(bases):
                    diag_ref[head, pl.ds(pl.multiple_of(base + at, row), row), :] += value[:, j * STEP : (j + 1) * STEP]

        def end(head):
            lanes = slice(head // 2 * 2 * feat, (head // 2 + 1) * 2 * feat)
            ds = ds_refs[head % many]
            dkey = mm(ds[:width], half_of(q_ref[:, lanes], head % 2, feat))
            dkeys.append(dkey)
            dqs.append(mm(kt_ref[head * feat : (head + 1) * feat, keys], ds[:width]))
            if head % 2:
                dka_ref[keys, lanes] += dkeys[-2] + dkeys[-1]
                dq_ref[:, lanes] = jnp.concatenate(dqs[-2:], axis=0).T.astype(BF)

        delta = begin(0)
        for head in range(heads):
            following = begin(head + 1) if head + 1 < heads else None
            middle(head, delta)
            if head:
                end(head - 1)
            delta = following
        end(heads - 1)

    by_width(low_ref, width_ref, length, work)

    @pl.when(block == pl.num_programs(1) - 1)
    def _():
        dk_ref[...] = dka_ref[...].astype(BF)
        dv_ref[...] = dva_ref[...].astype(BF)

    @pl.when(jnp.logical_and(seq == pl.num_programs(0) - 1, block == pl.num_programs(1) - 1))
    def _():
        for head in range(heads):
            sum_ref[head : head + 1, :] = unskew(diag_ref[head])


def attend_back(low, width, q, k, kt, v, attnt, dot, prob, inv, length, group):
    rows = q.shape[0]
    part = q.shape[1] // inv.shape[0]
    heads = inv.shape[1]
    feat = part // heads
    seqs, blocks = rows // length, length // BQ
    at = lambda s, b, *_: (s * blocks + b, group)
    whole = lambda s, b, *_: (s, group)
    at_t = lambda s, b, *_: (group, s * blocks + b)
    out = lambda s, b, *_: (s, 0)
    return pl.pallas_call(
        functools.partial(attend_back_kernel, heads=heads, feat=feat, length=length),
        grid_spec=pltpu.PrefetchScalarGridSpec(
            num_scalar_prefetch=2,
            grid=(seqs, blocks),
            in_specs=[
                pl.BlockSpec((BQ, part), at),
                pl.BlockSpec((length, part), whole),
                pl.BlockSpec((part, length), lambda s, b, *_: (group, s)),
                pl.BlockSpec((length, part), whole),
                pl.BlockSpec((part, BQ), at_t),
                pl.BlockSpec((part, BQ), at_t),
                pl.BlockSpec((1, 1, heads, length, BQ), lambda s, b, *_: (s, b, group, 0, 0)),
                pl.BlockSpec((1, heads, BQ), lambda s, b, *_: (group, 0, s * blocks + b)),
            ],
            out_specs=[
                pl.BlockSpec((BQ, part), lambda s, b, *_: (s * blocks + b, 0)),
                pl.BlockSpec((length, part), out),
                pl.BlockSpec((length, part), out),
                pl.BlockSpec((heads, 2 * length), lambda s, b, *_: (0, 0)),
            ],
            scratch_shapes=[
                pltpu.VMEM((heads, 2 * length - STEP, STEP), F32),
                pltpu.VMEM((length, part), F32),
                pltpu.VMEM((length, part), F32),
            ]
            + [pltpu.VMEM((length, BQ), F32)] * 2
            + [pltpu.VMEM((length, BQ), BF)] * 2,
        ),
        out_shape=[S((rows, part), BF)] * 3 + [S((heads, 2 * length), F32)],
        name="attend_back",
        cost_estimate=cost(32 * rows * length * part, 2 * rows * heads * length),
        compiler_params=PARAMS,
    )(low, width, q, k, kt, v, attnt, dot, prob, inv)


def key_ranges(seg):
    firsts, lasts = seg[:, ::BQ], seg[:, BQ - 1 :: BQ]
    low = jnp.sum((seg[:, None, :] < firsts[:, :, None]).astype(jnp.int32), axis=-1)
    high = jnp.sum((seg[:, None, :] <= lasts[:, :, None]).astype(jnp.int32), axis=-1)
    low = low // STEP
    width = (high + STEP - 1) // STEP - low
    return (low * STEP).reshape(-1), width.reshape(-1)


def ffn_kernel(me_ref, x_ref, up_ref, gain_ref, *refs, chunk, count, groups):
    attns, refs = refs[:groups], refs[groups:]
    pieces, refs = refs[:count], refs[count:]
    (states_ref, dx2_ref, dot_ref, da_ref, h2t_ref, h3t_ref, dbt_ref, hid_ref, dpre_ref,
     slope_ref, wo_ref, wi_ref, wb_ref, we_ref, sems) = refs
    width, wide = wi_ref.shape
    embed = we_ref.shape[1]

    @pl.when(pl.program_id(0) == 0)
    def _():
        me, rows = me_ref[0], pieces[0].shape[0]
        copies = placing(me, pieces, wo_ref, slice(0, width))
        copies += placing(me, pieces, wi_ref, slice(width, width + wide))
        copies += placing(me, pieces, we_ref, slice(width + wide, width + wide + embed))
        parts = wide // width
        for k, piece in enumerate(pieces):
            for q in range(parts):
                at = width + wide + embed + q * width
                spot = pl.ds(place(me, k, parts * rows) + q * rows, rows)
                copies.append((piece.at[:, at : at + width], wb_ref.at[spot, :]))
        run_copies(copies, sems)

    g_two, g_three = gain_ref[0:1, :], gain_ref[1:2, :]
    attn = jnp.concatenate([a[...] for a in attns], axis=1)
    x2 = x_ref[...].astype(F32) + mm(attn, wo_ref[...])
    scale2 = norm_scale(x2)
    h2 = (x2 * scale2 * g_two).astype(BF)
    x3 = x2
    for at in range(0, wide, chunk):
        cols = slice(at, at + chunk)
        hidden, slope = gelu_parts(mm(h2, wi_ref[:, cols]))
        hidden = hidden.astype(BF)
        hid_ref[:, cols] = hidden
        slope_ref[:, cols] = slope.astype(BF)
        x3 = x3 + mm(hidden, wb_ref[cols, :])
    scale3 = norm_scale(x3)
    h3 = (x3 * scale3 * g_three).astype(BF)
    states_ref[...] = mm(h3, we_ref[...])
    dx3 = norm_back(mm(up_ref[...], we_ref[...], NT), x3, scale3, g_three)
    db = dx3.astype(BF)
    dh2 = None
    for at in range(0, wide, chunk):
        cols = slice(at, at + chunk)
        dpre = (mm(db, wb_ref[cols, :], NT) * slope_ref[:, cols].astype(F32)).astype(BF)
        dpre_ref[:, cols] = dpre
        part = mm(dpre, wi_ref[:, cols], NT)
        dh2 = part if dh2 is None else dh2 + part
    part = norm_back(dh2, x2, scale2, g_two)
    dx2 = dx3 + part
    da = dx2.astype(BF)
    dx2_ref[...] = dx2
    da_ref[...] = da
    dot_ref[...] = mm(wo_ref[...], da, NT).astype(BF)
    h2t_ref[...] = h2.T
    h3t_ref[...] = h3.T
    dbt_ref[...] = db.T


def feed_forward(me, x, attns, up, gains, pieces, block=256, chunk=768):
    rows, width = x.shape
    count = len(pieces)
    embed = up.shape[1]
    wide = (pieces[0].shape[1] - width - embed) // 2
    fixed = lambda i, *_: (0, 0)
    natural = lambda cols: pl.BlockSpec((block, cols), lambda i, *_: (i, 0))
    turned = pl.BlockSpec((width, block), lambda i, *_: (0, i))
    return pl.pallas_call(
        functools.partial(ffn_kernel, chunk=chunk, count=count, groups=len(attns)),
        grid_spec=pltpu.PrefetchScalarGridSpec(
            num_scalar_prefetch=1,
            grid=(rows // block,),
            in_specs=[natural(width), natural(embed), pl.BlockSpec(gains.shape, fixed)]
            + [natural(a.shape[1]) for a in attns]
            + [ANY] * len(pieces),
            out_specs=[
                natural(embed), natural(width), turned, natural(width), turned, turned, turned,
                natural(wide), natural(wide),
            ],
            scratch_shapes=[
                pltpu.VMEM((block, wide), BF),
                pltpu.VMEM((width, width), BF),
                pltpu.VMEM((width, wide), BF),
                pltpu.VMEM((wide, width), BF),
                pltpu.VMEM((width, embed), BF),
                pltpu.SemaphoreType.DMA((count * (3 + wide // width),)),
            ],
        ),
        out_shape=[
            S((rows, embed), F32), S((rows, width), F32), S((width, rows), BF), S((rows, width), BF),
            S((width, rows), BF), S((width, rows), BF), S((width, rows), BF),
            S((rows, wide), BF), S((rows, wide), BF),
        ],
        name="feed_forward",
        cost_estimate=cost(4 * rows * width * (4 * wide + 2 * width), 20 * rows * wide, 2 * rows * wide),
        compiler_params=PARAMS,
    )(me, x, up, gains, *attns, *pieces)


def input_back_kernel(me_ref, x_ref, dx2_ref, gain_ref, *refs, spans, count, threaded):
    groups = len(spans)
    parts, refs = refs[: 3 * groups], refs[3 * groups :]
    pieces, refs = refs[: groups * count], refs[groups * count + threaded :]
    out_ref, weight_ref, sems = refs

    @pl.when(pl.program_id(0) == 0)
    def _():
        copies = []
        for g, lanes in enumerate(spans):
            copies += placing(me_ref[0], pieces[g * count : (g + 1) * count], weight_ref.at[g], lanes)
        run_copies(copies, sems)

    value = x_ref[...].astype(F32)
    scale = norm_scale(value)
    dh = None
    for g in range(groups):
        term = mm(jnp.concatenate([p[...] for p in parts[3 * g : 3 * g + 3]], axis=1), weight_ref[g], NT)
        dh = term if dh is None else dh + term
    out_ref[...] = dx2_ref[...] + norm_back(dh, value, scale, gain_ref[...])


def input_back(me, x, dx2, gain, parts, pieces, spans, first, steps, held, block=256):
    rows, width = x.shape
    natural = lambda cols: pl.BlockSpec((block, cols), lambda i, *_: (i + first, 0))
    fixed = lambda i, *_: (0, 0)
    operands = [me, x, dx2, gain, *parts, *pieces] + ([] if held is None else [held])
    return pl.pallas_call(
        functools.partial(
            input_back_kernel, spans=spans, count=len(pieces) // len(spans), threaded=0 if held is None else 1
        ),
        grid_spec=pltpu.PrefetchScalarGridSpec(
            num_scalar_prefetch=1,
            grid=(steps,),
            in_specs=[natural(width), natural(width), pl.BlockSpec((1, width), fixed)]
            + [natural(p.shape[1]) for p in parts]
            + [ANY] * (len(pieces) + (held is not None)),
            out_specs=natural(width),
            scratch_shapes=[
                pltpu.VMEM((len(spans), width, 3 * parts[0].shape[1]), BF),
                pltpu.SemaphoreType.DMA((len(pieces),)),
            ],
        ),
        out_shape=S((rows, width), F32),
        input_output_aliases={} if held is None else {len(operands) - 1: 0},
        name="input_back",
        cost_estimate=cost(6 * steps * block * width * width, 16 * steps * block * width),
        compiler_params=PARAMS,
    )(*operands)


def grad_rows_kernel(me_ref, *refs, count, lefts):
    lefts, rights, (keep_ref, send_ref, full_ref) = refs[:lefts], refs[lefts:-3], refs[-3:]
    rows = full_ref.shape[0] // count
    down = 0
    for left in lefts:
        at = 0
        for right in rights:
            cols = slice(at, at + right.shape[1])
            at += right.shape[1]
            full_ref[down : down + left.shape[0], cols] = mm(left[...], right[...])
        down += left.shape[0]
    for k in range(count):
        spot = pl.ds(pl.multiple_of(jnp.bitwise_xor(me_ref[0], k) * rows, 16), rows)
        (send_ref if k & 1 else keep_ref)[k >> 1] = full_ref[spot, :].astype(BF)


def grad_rows(me, lefts, rights, count, tile=768, first=0, tiles=None):
    m, rows = sum(left.shape[0] for left in lefts), lefts[0].shape[1]
    if len(rights) > 1:
        tile, tiles = sum(r.shape[1] for r in rights), 1
        specs = [pl.BlockSpec(r.shape, lambda j, *_: (0, 0)) for r in rights]
    else:
        tile = min(tile, rights[0].shape[1])
        tiles = rights[0].shape[1] // tile if tiles is None else tiles
        specs = [pl.BlockSpec((rows, tile), lambda j, *_: (0, j + first))]
    out = pl.BlockSpec((count // 2, m // count, tile), lambda j, *_: (0, 0, j))
    shape = S((count // 2, m // count, tile * tiles), BF)
    return pl.pallas_call(
        functools.partial(grad_rows_kernel, count=count, lefts=len(lefts)),
        grid_spec=pltpu.PrefetchScalarGridSpec(
            num_scalar_prefetch=1,
            grid=(tiles,),
            in_specs=[pl.BlockSpec(left.shape, lambda j, *_: (0, 0), pipeline_mode=pl.Buffered(1)) for left in lefts]
            + specs,
            out_specs=[out, out],
            scratch_shapes=[pltpu.VMEM((m, tile), F32)],
        ),
        out_shape=[shape, shape],
        name="weight_grad",
        cost_estimate=cost(2 * m * rows * tile * tiles, 2 * rows * (m + tile * tiles)),
        compiler_params=PARAMS,
    )(me, *lefts, *rights)


def grad_set_kernel(me_ref, *refs, shapes, count, extra):
    operands = sum(a + b for a, b in shapes)
    sources, refs = refs[:operands], refs[operands:]
    if extra:
        (sums_ref, hot_ref), refs, table_ref = refs[:2], refs[2:-1], refs[-1]
    keep_ref, send_ref, full_ref = refs[:3]
    held, sems = refs[3:-1], refs[-1]
    copies = [pltpu.make_async_copy(a, b, sems.at[i]) for i, (a, b) in enumerate(zip(sources, held))]
    for copy in copies:
        copy.start()
    rows = full_ref.shape[0] // count
    index = at = 0
    for lefts, rights in shapes:
        left = held[index : index + lefts]
        right = held[index + lefts : index + lefts + rights]
        for copy in copies[index : index + lefts]:
            copy.wait()
        for n, r in enumerate(right):
            copies[index + lefts + n].wait()
            down = 0
            for part in left:
                full_ref[down : down + part.shape[0], at : at + r.shape[1]] = mm(part[...], r[...])
                down += part.shape[0]
            at += r.shape[1]
        index += lefts + rights
    if extra:
        sums = sums_ref[...]
        high = sums.astype(BF)
        rest = (sums - high.astype(F32)).astype(BF)
        table_ref[...] = jnp.zeros_like(table_ref)
        table_ref[:, : sums.shape[0]] = mm(hot_ref[...], high, NT) + mm(hot_ref[...], rest, NT)
        each = table_ref.shape[0] // count
    for k in range(count):
        target = send_ref if k & 1 else keep_ref
        target[k >> 1, :, :at] = full_ref[pl.ds(place(me_ref[0], k, rows), rows), :].astype(BF)
        if extra:
            target[k >> 1, :, at:] = jnp.zeros((rows, STEP), BF)
            own = pl.ds(jnp.bitwise_xor(me_ref[0], k) * each, each)
            target[k >> 1, :each, at:] = table_ref[own, :].astype(BF)


def grad_set(me, jobs, count, extra=None):
    operands = [x for lefts, rights in jobs for x in lefts + rights]
    m, rows = sum(x.shape[0] for x in jobs[0][0]), jobs[0][0][0].shape[1]
    n = sum(r.shape[1] for _, rights in jobs for r in rights)
    wide = n + (0 if extra is None else STEP)
    shape = S((count // 2, m // count, wide), BF)
    out = pl.BlockSpec(shape.shape, lambda j, *_: (0, 0, 0))
    more = [] if extra is None else list(extra)
    return pl.pallas_call(
        functools.partial(
            grad_set_kernel,
            shapes=tuple((len(a), len(b)) for a, b in jobs),
            count=count,
            extra=extra is not None,
        ),
        grid_spec=pltpu.PrefetchScalarGridSpec(
            num_scalar_prefetch=1,
            grid=(1,),
            in_specs=[ANY] * len(operands) + [pl.BlockSpec(e.shape, lambda j, *_: (0, 0)) for e in more],
            out_specs=[out, out],
            scratch_shapes=[pltpu.VMEM((m, n), F32)]
            + [pltpu.VMEM(x.shape, BF) for x in operands]
            + [pltpu.SemaphoreType.DMA((len(operands),))]
            + ([pltpu.VMEM((extra[1].shape[0], STEP), F32)] if more else []),
        ),
        out_shape=[shape, shape],
        name="weight_grads",
        cost_estimate=cost(2 * m * rows * n, 2 * rows * (m + n)),
        compiler_params=PARAMS,
    )(me, *operands, *more)


def grad_cols_kernel(me_ref, left_ref, right_ref, out_ref):
    out_ref[0] = mm(left_ref[...], right_ref[...]).astype(BF).T


def grad_cols(me, left, right, count, odd, tile=768):
    m, rows = left.shape
    n = right.shape[1]
    part = n // count
    if part % STEP:
        full = lax.dot_general(right, left, (((0,), (1,)), ((), ())), preferred_element_type=F32).astype(BF)
        return jnp.stack(
            [lax.dynamic_slice_in_dim(full, (me[0] ^ k) * part, part, 0) for k in range(odd, count, 2)]
        )
    tile = min(tile, part)
    inner = part // tile
    return pl.pallas_call(
        grad_cols_kernel,
        grid_spec=pltpu.PrefetchScalarGridSpec(
            num_scalar_prefetch=1,
            grid=(count // 2, inner),
            in_specs=[
                pl.BlockSpec((m, rows), lambda k, t, me: (0, 0), pipeline_mode=pl.Buffered(1)),
                pl.BlockSpec((rows, tile), lambda k, t, me: (0, jnp.bitwise_xor(me[0], 2 * k + odd) * inner + t)),
            ],
            out_specs=pl.BlockSpec((1, tile, m), lambda k, t, me: (k, t, 0)),
        ),
        out_shape=S((count // 2, part, m), BF),
        name="weight_grad",
        cost_estimate=cost(m * rows * n, rows * (2 * m + n)),
        compiler_params=PARAMS,
    )(me, left, right)


def bits_of(axis):
    size = lax.axis_size(axis)
    count = size.bit_length() - 1
    assert size == 1 << count
    return count


def swap(value, axis, mask):
    size = lax.axis_size(axis)
    return lax.ppermute(value, axis, [(i, i ^ mask) for i in range(size)])


def gathering(shard):
    held = {0: shard}
    for bit in reversed(range(1, bits_of("fsdp"))):
        step = 1 << bit
        sent = yield list(held.values())
        held.update({k ^ step: swap(v, "fsdp", step) for k, v in zip(list(held), sent)})
    (own,) = yield [shard]
    others = [k for k in held if k]
    first = swap(own, "fsdp", 1)
    sent = yield [held[k] for k in others]
    held.update({k ^ 1: swap(v, "fsdp", 1) for k, v in zip(others, sent)})
    held[1] = first
    return [held[k] for k in range(len(held))]


def reorder(parts, index):
    parts = list(parts)
    for bit in range(len(parts).bit_length() - 1):
        flag = (index >> bit) & 1
        parts = [jnp.where(flag == 1, parts[k ^ (1 << bit)], parts[k]) for k in range(len(parts))]
    return parts


def summing(keep, send, late=False):
    (sent,) = yield [send]
    got = swap(sent, "fsdp", 1)
    if late:
        (got,) = yield [got]
        (keep,) = keep
    part = {2 * k: keep[k].astype(F32) + got[k].astype(F32) for k in range(keep.shape[0])}
    for bit in range(1, bits_of("fsdp")):
        step = 1 << bit
        away = [k for k in part if k & step]
        if late:
            half = part[0].shape[0] // 2
            sent = yield [part[k][:half].astype(BF) for k in away]
            top = [swap(s, "fsdp", step) for s in sent]
            sent = yield [part[k][half:].astype(BF) for k in away] + top
            bottom = [swap(s, "fsdp", step) for s in sent[: len(away)]]
            arrived = [jnp.concatenate(pair, axis=0) for pair in zip(sent[len(away) :], bottom)]
        else:
            sent = yield [part[k].astype(BF) for k in away]
            arrived = [swap(s, "fsdp", step) for s in sent]
        got = {k ^ step: g for k, g in zip(away, arrived)}
        part = {k: part[k] + got[k].astype(F32) for k in got}
    value = part[0]
    side = lax.axis_index("grp") & 1
    size = value.shape[1] // 2
    (sent,) = yield [lax.dynamic_slice_in_dim(value, (1 - side) * size, size, 1).astype(BF)]
    return lax.dynamic_slice_in_dim(value, side * size, size, 1) + swap(sent, "grp", 1).astype(F32)


def completing(values, split=False):
    me = lax.axis_index("grp")
    side, line = me & 1, me >> 1
    depth = lax.axis_size("grp") // 2
    value = values[0] if len(values) == 1 else jnp.concatenate(values, axis=1)
    rows = value.shape[0] // depth
    block = lambda k: lax.dynamic_slice_in_dim(value, (line ^ k) * rows, rows, 0)
    sent = yield [block(k).astype(BF) for k in range(1, depth)]
    total = block(0)
    for k, s in zip(range(1, depth), sent):
        total = total + swap(s, "grp", 2 * k).astype(F32)
    (total,) = yield [total.astype(BF)]
    got = [total] + [swap(total, "grp", 2 * k) for k in range(1, depth)]
    if split:
        got = yield got
    got = reorder(got, line)
    if split:
        half = total.shape[1] // 2
        left, right = (jnp.concatenate([g[:, c] for g in got], axis=0) for c in (slice(0, half), slice(half, None)))
        (left,) = yield [left]
        first = swap(left, "grp", 1)
        (right, first) = yield [right, first]
        mine = jnp.concatenate([left, right], axis=1)
        other = jnp.concatenate([first, swap(right, "grp", 1)], axis=1)
    else:
        (mine,) = yield [jnp.concatenate(got, axis=0)]
        other = swap(mine, "grp", 1)
    results, at = [], 0
    for v in values:
        cols = slice(at, at + v.shape[1])
        at += v.shape[1]
        a, b = mine[:, cols].astype(F32), other[:, cols].astype(F32)
        results.append(jnp.concatenate([jnp.where(side == 0, a, b), jnp.where(side == 0, b, a)], axis=1))
    return results


class Flow:
    def __init__(self, stages):
        self.stages, self.ready, self.result = stages, next(stages), None

    def send(self, operands):
        try:
            self.ready = self.stages.send(operands)
        except StopIteration as done:
            self.ready, self.result = None, done.value


def depart(anchor, flows, after=(), hold=()):
    flows = [f for f in flows if f.ready is not None]
    operands = [x for f in flows for x in f.ready]
    kept = tuple(f.result if f.ready is None else f.ready for f in hold)
    anchor, operands, kept, _ = lax.optimization_barrier((anchor, tuple(operands), kept, tuple(after)))
    for f, k in zip(hold, kept):
        if f.ready is None:
            f.result = k
        else:
            f.ready = k
    operands = list(operands)
    for f in flows:
        count = len(f.ready)
        f.send(operands[:count])
        operands = operands[count:]
    return anchor


class Held:
    def __init__(self, value):
        self.ready, self.result = None, value


def then_complete(flows):
    return Flow(completing([finish(f) for f in flows]))


def finish(flow):
    while flow.ready is not None:
        flow.send(flow.ready)
    return flow.result


def total_small(value):
    for axis in ("fsdp", "grp"):
        size = lax.axis_size(axis)
        others = [swap(value, axis, k) for k in range(1, size)]
        for other in others:
            value = value + other
    return value


def body(
    layer_input,
    segment_ids,
    bucket_table,
    gain_attn,
    weight_query,
    weight_key,
    weight_value,
    weight_out,
    gain_ffn,
    weight_in,
    weight_back,
    gain_final,
    weight_embed,
    bias_table,
    cotangent,
):
    micro, length, width = layer_input.shape
    heads = bias_table.shape[1]
    size = lax.axis_size("fsdp")
    index = lax.axis_index("fsdp")
    me = index.astype(jnp.int32).reshape(1)
    buckets = bias_table.shape[0] * size
    rows = micro * length
    groups = GROUPS

    part = width // size
    span = width // groups
    own_rows = slice(0, part)
    near = Flow(
        gathering(
            pack(
                [weight_query, weight_key, weight_value],
                [(w, own_rows, slice(g * span, (g + 1) * span)) for g in range(groups) for w in range(3)],
            )
        )
    )
    link = depart(me, [near])
    full = lambda w: (own_rows, slice(0, w.shape[1]))
    far = Flow(
        gathering(
            pack(
                [weight_out, weight_in, weight_embed, weight_back],
                [(0, *full(weight_out)), (1, *full(weight_in)), (2, *full(weight_embed))]
                + [
                    (3, slice(q * part, (q + 1) * part), slice(0, width))
                    for q in range(weight_back.shape[0] // part)
                ],
            )
        )
    )
    small = jnp.concatenate([gain_attn, gain_ffn, gain_final, bias_table.reshape(-1)]).reshape(1, -1)
    small = finish(Flow(gathering(small)))
    small = jnp.concatenate(reorder(small, index), axis=0)
    g_one, g_two, g_three = (
        small[:, k * part : (k + 1) * part].reshape(1, width).astype(F32) for k in range(3)
    )
    table = small[:, 3 * part :].reshape(buckets, heads)

    link = depart(link, [near])

    onehot = (bucket_table[:, None] == lax.iota(jnp.int32, buckets)[None, :]).astype(BF)
    bias_rows = lax.dot_general(table, onehot, (((0,), (1,)), ((), ())), preferred_element_type=F32)
    low, wide = key_ranges(segment_ids)
    seg_col = segment_ids.reshape(rows, 1)
    seg_row = segment_ids.reshape(rows // BQ, 1, BQ)
    gains = jnp.concatenate([g_two, g_three], axis=0)
    bias_rows, low, wide, seg_col, seg_row, gains, g_one = lax.optimization_barrier(
        (bias_rows, low, wide, seg_col, seg_row, gains, g_one)
    )
    strips = bias_strips(bias_rows)

    x = layer_input.reshape(rows, width)
    upstream = cotangent.reshape(rows, -1)
    turn = depart(link, [near, far], [strips])
    near = finish(near)
    query, key, value, key_t, value_t, h1_t = project(turn, x, g_one, near, groups)
    start = depart(low, [far], [query])
    attn, attn_t, probs, inverse = attend(
        start, wide, query, key, value_t, strips, seg_col, seg_row, length, groups
    )
    turn = depart(me, [far], [inverse])
    far = finish(far)
    states, dx2, dattn_t, da, h2_t, h3_t, db_t, hidden, dpre = feed_forward(
        turn, x, [attn], upstream, gains, far
    )

    back_send = grad_cols(me, db_t, hidden, size, 1)
    back_keep = []
    back = Flow(summing(back_keep, back_send, True))
    turn = depart(me, [back])
    back_keep.append(grad_cols(turn, db_t, hidden, size, 0))
    turn = depart(me, [back], back_keep)
    turn = depart(turn, [back])
    inner = Flow(summing(*grad_rows(turn, [h2_t], [dpre], size)))

    def back_of(turn, g):
        return attend_back(
            turn, wide, query, key, key_t, value, attn_t, dattn_t, probs, inverse, length, g
        )

    def project_grad(turn, parts, extra=None):
        return Flow(summing(*grad_set(turn, [([h1_t], list(parts[:3]))], size, extra)))

    turn = depart(turn, [inner, back])
    out = grad_set(turn, [([attn_t], [da]), ([h3_t], [upstream])], size)
    turn = depart(low, [inner, back], [out[0]])
    grads = [back_of(turn, 0)]
    out = Flow(summing(*out))
    turn = depart(me, [out], [grads[0][3]] + inner.ready)
    first = project_grad(turn, grads[0])
    turn = depart(low, [inner, out, first], [finish(back)])
    grads.append(back_of(turn, 1))
    turn = depart(me, [out, first], [grads[1][3]])
    second = project_grad(turn, grads[1])
    fold = back.result.shape[0] // finish(inner).shape[0]
    turned = jnp.concatenate(jnp.split(back.result, fold, axis=0), axis=1)
    wide_flow = Flow(completing([inner.result, turned], True))
    finish(out)
    turn = depart(low, [wide_flow, first, second], hold=[out])
    grads.append(back_of(turn, 2))
    finish(first)
    turn = depart(me, [wide_flow, second], [grads[2][3]], [first])
    third = project_grad(turn, grads[2], (jnp.concatenate([g[3] for g in grads], axis=0), onehot.T))

    pieces = near * groups
    spans = [slice(3 * span * g, 3 * span * (g + 1)) for g in range(groups)]
    dparts = [p for g in grads for p in g[:3]]
    blocks = rows // 256
    cuts = (blocks - 2 * (blocks // 3), blocks // 3, blocks // 3)
    turn = depart(me, [second, third])
    d_input = input_back(turn, x, dx2, g_one, dparts, pieces, spans, 0, cuts[0], None)
    joint = then_complete([out, first, second])
    d_input = Held(d_input)
    turn = depart(me, [wide_flow], hold=[d_input])
    turn = depart(turn, [wide_flow, third, joint])
    d_input = Held(
        input_back(turn, x, dx2, g_one, dparts, pieces, spans, cuts[0], cuts[1], d_input.result)
    )
    turn = depart(me, [wide_flow, third, joint], hold=[d_input])
    d_input = Held(
        input_back(turn, x, dx2, g_one, dparts, pieces, spans, cuts[0] + cuts[1], cuts[2], d_input.result)
    )
    last = then_complete([third])
    finish(wide_flow)
    depart(me, [joint, last], hold=[d_input, wide_flow])
    g_in, g_back = wide_flow.result
    cut = g_back.shape[1] // fold // 2
    g_back = jnp.concatenate(
        [
            jnp.concatenate([g_back[:, (h * fold + q) * cut : (h * fold + q + 1) * cut] for h in range(2)], axis=1)
            for q in range(fold)
        ],
        axis=0,
    )
    g_oe, *proj = finish(joint) + finish(last)
    g_out, g_embed = g_oe[:, :width], g_oe[:, width:]
    grad_q, grad_k, grad_v = (
        jnp.concatenate([p[:, k * span : (k + 1) * span] for p in proj], axis=1) for k in range(3)
    )
    g_table = proj[-1][: buckets // size, width : width + heads]

    def gain_grad(gain, *pairs):
        return sum(jnp.sum(w.astype(F32) * g, axis=1) for w, g in pairs) / gain.astype(F32)

    gain_grads = (
        gain_grad(
            gain_attn,
            *((near[0][:, 3 * span * g : 3 * span * (g + 1)], p[:, : 3 * span]) for g, p in enumerate(proj)),
        ),
        gain_grad(gain_ffn, (weight_in, g_in)),
        gain_grad(gain_final, (weight_embed, g_embed)),
    )
    return (
        states.reshape(micro, length, -1),
        d_input.result.reshape(micro, length, width),
        gain_grads[0],
        grad_q,
        grad_k,
        grad_v,
        g_out,
        gain_grads[1],
        g_in,
        g_back,
        gain_grads[2],
        g_embed,
        g_table,
    )


GROUPS = 3


def solution(mesh):
    placed = (
        P(None, ("grp", "fsdp"), None),
        P(None, ("grp", "fsdp")),
        P(),
        P("fsdp"),
        P("fsdp", None),
        P("fsdp", None),
        P("fsdp", None),
        P("fsdp", None),
        P("fsdp"),
        P("fsdp", None),
        P("fsdp", None),
        P("fsdp"),
        P("fsdp", None),
        P("fsdp", None),
        P(None, ("grp", "fsdp"), None),
    )
    return jax.shard_map(
        body,
        mesh=mesh,
        in_specs=placed,
        out_specs=(
            P(None, ("grp", "fsdp"), None),
            P(None, ("grp", "fsdp"), None),
            P("fsdp"),
            P("fsdp", None),
            P("fsdp", None),
            P("fsdp", None),
            P("fsdp", None),
            P("fsdp"),
            P("fsdp", None),
            P("fsdp", None),
            P("fsdp"),
            P("fsdp", None),
            P("fsdp", None),
        ),
        check_vma=False,
    )
```
